32 devices in a mesh: gx: 4 (over y, x), gy: 2 (over core), gz: 4 (over z).
Axes of the slice: x: 2, y: 2, z: 4, core: 2. Of those that a mesh axis runs over, the one named last changes fastest.
Arguments:
- state: float32 [5, 16, 32, 512], P(None, 'gx', 'gy', 'gz'), may hold values from -2 to 8, as said below
- volume: float32 [16, 32, 512], P('gx', 'gy', 'gz'), may hold values from 0 to 1, as said below
- apertures: float32 [3, 16, 32, 512], P(None, 'gx', 'gy', 'gz'), may hold values from 0 to 1, as said below
- flags: int32 [16, 32, 512], P('gx', 'gy', 'gz'), may hold values from 0 to 2, as said below
Outputs:
- step_rate: float32 [5, 16, 32, 512], P(None, 'gx', 'gy', 'gz')
The draws below stay inside these ranges and needn't reach their ends.
Inputs may be any that keep to these rules, and one draw needn't show every extreme that they name: `flags`: in every column of cells the lowest cells are solid (flag 2), one cut cell (flag 1) follows, fluid cells (flag 0) lie above; the cut cell lies between layers 8 and 23. `volume`: 0 in solid cells, between 0.05 and 0.95 in cut cells, 1 in fluid cells; equal to the height of fluid in the cell over a terrain surface. `apertures`: the open part of each face below which the terrain surface lies; lower z faces of solid and cut cells are closed. `state`: density between 0.5 and 2, velocity components between -1 and 1, pressure between 0.5 and 2.
All inputs are finite; a program needn't handle non-finite values.
Results may differ from the reference program's by a relative error of at most 0.0003.
Values sent between devices are 32-bit elements; how exact they have to be, the bound alone decides.
A program may use at most 64 MiB of HBM per device.

```python
import jax
import jax.numpy as jnp
from jax import lax

NF = 5
CUTZ = 32
CX = 4
NX = 16
NY = 32
NZ = 512
N_GX = 4


def terrain(key):
    base_key = jax.random.fold_in(key, 17)
    heights = jax.random.randint(jax.random.fold_in(base_key, 1), (NX, NY), CUTZ // 4, 3 * CUTZ // 4)
    fraction = jax.random.uniform(jax.random.fold_in(base_key, 2), (NX, NY), jnp.float32, 0.05, 0.95)
    return (heights, fraction)


def surface_top(key):
    heights, fraction = terrain(key)
    return (heights, heights.astype(jnp.float32) + 1.0 - fraction)


def draw_volume(key, part):
    heights, surface = surface_top(key)
    levels = jnp.arange(NZ, dtype=jnp.float32)
    return jnp.clip(levels[None, None, :] + 1.0 - surface[:, :, None], 0.0, 1.0)


def draw_apertures(key, part):
    heights, surface = surface_top(key)
    levels = jnp.arange(NZ, dtype=jnp.float32)
    side_x = jnp.maximum(surface, jnp.roll(surface, 1, axis=0))
    side_y = jnp.maximum(surface, jnp.roll(surface, 1, axis=1))
    open_x = jnp.clip(levels[None, None, :] + 1.0 - side_x[:, :, None], 0.0, 1.0)
    open_y = jnp.clip(levels[None, None, :] + 1.0 - side_y[:, :, None], 0.0, 1.0)
    int_levels = jnp.arange(NZ, dtype=jnp.int32)
    open_z = (int_levels[None, None, :] > heights[:, :, None]).astype(jnp.float32)
    return jnp.stack([open_x, open_y, open_z])


def draw_flags(key, part):
    heights, fraction = terrain(key)
    levels = jnp.arange(NZ, dtype=jnp.int32)[None, None, :]
    column = heights[:, :, None]
    return jnp.where(levels < column, 2, jnp.where(levels == column, 1, 0)).astype(jnp.int32)


def draw_state(key, part):
    state_key = jax.random.fold_in(key, 5)
    density = jax.random.uniform(jax.random.fold_in(state_key, 1), (NX, NY, NZ), jnp.float32, 0.5, 2.0)
    velocity = jax.random.uniform(jax.random.fold_in(state_key, 2), (3, NX, NY, NZ), jnp.float32, -1.0, 1.0)
    pressures = jax.random.uniform(jax.random.fold_in(state_key, 3), (NX, NY, NZ), jnp.float32, 0.5, 2.0)
    energy = pressures / 0.4 + 0.5 * density * jnp.sum(velocity * velocity, axis=0)
    return jnp.concatenate([density[None], density[None] * velocity, energy[None]], axis=0)


def setup_inputs(seed: int = 0) -> dict:
    key_of = jax.random.split(jax.random.key(seed), 5)
    return {
        "state": draw_state(jax.random.fold_in(key_of[4], 71), 0),
        "volume": draw_volume(jax.random.fold_in(key_of[4], 71), 0),
        "apertures": draw_apertures(jax.random.fold_in(key_of[4], 71), 0),
        "flags": draw_flags(jax.random.fold_in(key_of[4], 71), 0),
    }


GAMMA_LESS = 0.4
DISSIPATION = 4.0
TIME_STEP = 0.02
VOLUME_FLOOR = 0.5


def minmod(lower, upper):
    return 0.5 * (jnp.sign(lower) + jnp.sign(upper)) * jnp.minimum(jnp.abs(lower), jnp.abs(upper))


def pressure(cell_state):
    kinetic = cell_state[1] * cell_state[1] + cell_state[2] * cell_state[2] + cell_state[3] * cell_state[3]
    return GAMMA_LESS * (cell_state[4] - 0.5 * kinetic / cell_state[0])


def physical_flux(cell_state, direction):
    velocity = cell_state[direction] / cell_state[0]
    pressures = pressure(cell_state)
    components = [cell_state[direction], cell_state[1] * velocity, cell_state[2] * velocity,
                  cell_state[3] * velocity, (cell_state[4] + pressures) * velocity]
    components[direction] = components[direction] + pressures
    return jnp.stack(components)


def trim_axis(array, dimension, offset, extent):
    return lax.slice_in_dim(array, offset, offset + extent, axis=dimension)


def face_flux(column_part, direction, margin, extent):
    length = column_part.shape[direction]
    differences = trim_axis(column_part, direction, 1, length - 1) - trim_axis(column_part, direction, 0, length - 1)
    slopes = minmod(trim_axis(differences, direction, 0, length - 2), trim_axis(differences, direction, 1, length - 2))
    left_state = trim_axis(column_part, direction, margin - 1, extent + 1) + 0.5 * trim_axis(slopes, direction, margin - 2, extent + 1)
    right_state = trim_axis(column_part, direction, margin, extent + 1) - 0.5 * trim_axis(slopes, direction, margin - 1, extent + 1)
    average = 0.5 * (physical_flux(left_state, direction) + physical_flux(right_state, direction))
    return average - 0.5 * DISSIPATION * (right_state - left_state)


def section_rate(padded, margin, openings, open_margin, volume, fluid_mask):
    extents = [padded.shape[dimension] - 2 * margin for dimension in (1, 2, 3)]
    centre = padded
    for dimension in (1, 2, 3):
        centre = trim_axis(centre, dimension, margin, extents[dimension - 1])
    pressures = pressure(centre)
    divergence = jnp.zeros_like(centre)
    pushes = []
    for direction in (1, 2, 3):
        column_part = padded
        face_open = openings
        for other_axis in (1, 2, 3):
            if other_axis != direction:
                column_part = trim_axis(column_part, other_axis, margin, extents[other_axis - 1])
                face_open = trim_axis(face_open, other_axis, open_margin, extents[other_axis - 1])
        extent = extents[direction - 1]
        face_open = trim_axis(face_open[direction - 1], direction - 1, open_margin, extent + 1)
        fluxes = face_flux(column_part, direction, margin, extent) * face_open[None]
        divergence = divergence + trim_axis(fluxes, direction, 1, extent) - trim_axis(fluxes, direction, 0, extent)
        pushes.append(pressures * (trim_axis(face_open, direction - 1, 1, extent) - trim_axis(face_open, direction - 1, 0, extent)))
    wall_force = jnp.stack([jnp.zeros_like(pressures)] + pushes + [jnp.zeros_like(pressures)])
    return (wall_force - divergence) / jnp.maximum(volume, VOLUME_FLOOR) * fluid_mask


def redistribute(rates, volume, excess):
    moved_sum = jnp.sum(excess[None] * rates, axis=3)
    weight = jnp.sum(volume, axis=2)
    return (1.0 - excess[None]) * rates + volume[None] * (moved_sum / weight[None])[..., None]


def full_rate(current, apertures, volume, fluid_mask, excess):
    padded = jnp.pad(current, ((0, 0), (2, 2), (2, 2), (2, 2)), mode="wrap")
    openings = jnp.pad(apertures, ((0, 0), (1, 1), (1, 1), (1, 1)), mode="wrap")

    def block_rate(block_index):
        offset = block_index * CX
        cell_block = lax.dynamic_slice_in_dim(padded, offset, CX + 4, axis=1)
        open_block = lax.dynamic_slice_in_dim(openings, offset, CX + 2, axis=1)
        vol_block = lax.dynamic_slice_in_dim(volume, offset, CX, axis=0)
        fluid_block = lax.dynamic_slice_in_dim(fluid_mask, offset, CX, axis=0)
        excess_block = lax.dynamic_slice_in_dim(excess, offset, CX, axis=0)
        rates = section_rate(cell_block, 2, open_block, 1, vol_block, fluid_block)
        spread = redistribute(rates[..., :CUTZ], vol_block[..., :CUTZ], excess_block[..., :CUTZ])
        return jnp.concatenate([spread, rates[..., CUTZ:]], axis=3)

    block_rates = lax.map(block_rate, jnp.arange(N_GX, dtype=jnp.int32))
    return jnp.moveaxis(block_rates, 0, 1).reshape(NF, NX, NY, NZ)


def reference(state, volume, apertures, flags):
    fluid_mask = (flags != 2).astype(jnp.float32)
    excess = (1.0 - volume) * (flags == 1).astype(jnp.float32)
    first_rate = full_rate(state, apertures, volume, fluid_mask, excess)
    middle = state + TIME_STEP * first_rate
    second = full_rate(middle, apertures, volume, fluid_mask, excess)
    return 0.5 * (first_rate + second)
```

```python
import jax
import jax.numpy as jnp
from jax import lax
from jax.experimental import pallas as pl
from jax.experimental.pallas import tpu as pltpu
from jax.sharding import PartitionSpec as P

CUTZ = 32
NF = 5
GAMMA_LESS = 0.4
DISSIPATION = 4.0
TIME_STEP = 0.02
VOLUME_FLOOR = 0.5
PAD = 8

MESH = pl.DeviceIdType.MESH


def minmod(a, b):
    return jnp.maximum(jnp.minimum(a, b), 0.0) + jnp.minimum(jnp.maximum(a, b), 0.0)


def pressure_of(w, inverse):
    kinetic = w[1] * w[1] + w[2] * w[2] + w[3] * w[3]
    return GAMMA_LESS * (w[4] - 0.5 * kinetic * inverse)


def flux(w, d):
    inverse = 1.0 / w[0]
    u = w[d] * inverse
    p = pressure_of(w, inverse)
    out = [w[d], w[1] * u, w[2] * u, w[3] * u, (w[4] + p) * u]
    out[d] = out[d] + p
    return out


def face(left, right, d, half_open):
    fl, fr = flux(left, d), flux(right, d)
    return [
        ((fl[f] + fr[f]) + DISSIPATION * (left[f] - right[f])) * half_open for f in range(NF)
    ]


def kernel(
    state, volume, apertures, flags, out,
    buf1, buf2, ox, oy, oz, vol, flg, pk, rec_low, rec_high, gfix, sfix, afix,
    acc1, acc2, first, scale, keep, gain, press, inner, edge, outer,
    vol_side, part, face_x, scale_side, keep_side, gain_side, tally,
    local_sem, send_sem, recv_sem, ready,
):
    _, X, Y, Z = state.shape
    F4 = 4 * X
    me = [lax.axis_index(a) for a in ("gx", "gy", "gz")]
    size = [lax.axis_size(a) for a in ("gx", "gy", "gz")]
    up = [{a: lax.rem(me[i] + 1, size[i])} for i, a in enumerate(("gx", "gy", "gz"))]
    down = [{a: lax.rem(me[i] + size[i] - 1, size[i])} for i, a in enumerate(("gx", "gy", "gz"))]

    rows = pl.ds(PAD, Y)
    def settle(sem, ref):
        pltpu.make_async_copy(ref, ref, sem).wait()

    loads = [
        (state, buf1.at[:, pl.ds(2, X), rows, :]),
        (apertures.at[0], ox.at[pl.ds(0, X)]),
        (apertures.at[1], oy.at[:, pl.ds(0, Y), :]),
        (apertures.at[2], oz),
        (volume, vol),
        (flags, flg),
    ]
    loads = [pltpu.make_async_copy(s, d, local_sem) for s, d in loads]
    for load in loads:
        load.start()

    barrier = pltpu.get_barrier_semaphore()
    n_z = size[2]
    bottom, top = me[2] == 0, me[2] == n_z - 1
    early_up = [me[i] < size[i] // 2 for i in range(2)] + [jnp.logical_not(top)]
    early_down = [(me[i] == 0) | (me[i] > size[i] // 2) for i in range(2)] + [bottom]
    late_up = [jnp.logical_not(e) for e in early_up]
    late_down = [jnp.logical_not(e) for e in early_down]
    late_edges = 0
    for i in range(3):
        @pl.when(early_up[i])
        def _():
            pl.semaphore_signal(barrier, inc=1, device_id=up[i], device_id_type=MESH)

        @pl.when(early_down[i])
        def _():
            pl.semaphore_signal(barrier, inc=1, device_id=down[i], device_id_type=MESH)

        late_edges = late_edges + jnp.where(late_up[i], 1, 0) + jnp.where(late_down[i], 1, 0)

    up_slot, down_slot = (1, 2, 4), (0, 2, 3)

    @pl.when(late_edges > 0)
    def _():
        pl.semaphore_wait(barrier, late_edges)

    for i in range(3):
        @pl.when(late_down[i])
        def _():
            pl.semaphore_signal(ready.at[up_slot[i]], inc=1, device_id=down[i], device_id_type=MESH)

        @pl.when(late_up[i])
        def _():
            pl.semaphore_signal(ready.at[down_slot[i]], inc=1, device_id=up[i], device_id_type=MESH)

    def send_late(i, low, high):
        @pl.when(late_down[i])
        def _():
            for c in low:
                c.start()

        @pl.when(late_up[i])
        def _():
            for c in high:
                c.start()

    def send_early_up(i, high, slot):
        @pl.when(early_up[i])
        def _():
            if slot is not None:
                pl.semaphore_wait(ready.at[slot], 1)
            for c in high:
                c.start()

    def send_early_down(i, low, slot):
        @pl.when(early_down[i])
        def _():
            if slot is not None:
                pl.semaphore_wait(ready.at[slot], 1)
            for c in low:
                c.start()

    def remote(src, dst, recv, target):
        return pltpu.make_async_remote_copy(
            src_ref=src, dst_ref=dst, send_sem=send_sem, recv_sem=recv_sem.at[recv],
            device_id=target, device_id_type=MESH,
        )

    def layer(src, cell, dst, place, recv, target):
        return remote(
            src.at[:, pl.ds(2 + cell, 1), rows, :], dst.at[:, pl.ds(place, 1), rows, :],
            recv, target,
        )

    def y_copies(src, x0, y0, buf, recv):
        mid = pl.ds(x0, X)
        return (
            remote(src.at[:, mid, pl.ds(y0, 2), :],
                   buf.at[:, pl.ds(2, X), pl.ds(PAD + Y, 2), :], recv, down[1]),
            remote(src.at[:, mid, pl.ds(y0 + Y - 2, 2), :],
                   buf.at[:, pl.ds(2, X), pl.ds(PAD - 2, 2), :], recv, up[1]),
        )

    def z_copies(stage, recv):
        return (
            remote(pk.at[stage], rec_high.at[stage], recv, down[2]),
            remote(pk.at[stage], rec_low.at[stage], recv, up[2]),
        )

    near_low = (layer(buf1, 0, buf1, X + 2, 0, down[0]),)
    near_high = (layer(buf1, X - 1, buf1, 1, 1, up[0]),)
    rest_low = (
        layer(buf1, 1, buf1, X + 3, 2, down[0]),
        remote(ox.at[pl.ds(0, 1)], ox.at[pl.ds(X, 1)], 2, down[0]),
        remote(vol.at[pl.ds(0, 1)], vol_side.at[pl.ds(1, 1)], 2, down[0]),
    )
    rest_high = (
        layer(buf1, X - 2, buf1, 0, 3, up[0]),
        remote(vol.at[pl.ds(X - 1, 1)], vol_side.at[pl.ds(0, 1)], 3, up[0]),
    )
    ys1 = y_copies(state, 0, 0, buf1, 4)
    ay = remote(apertures.at[1, :, pl.ds(0, 1), :], oy.at[:, pl.ds(Y, 1), :], 4, down[1])
    y_low, y_high = (ay, ys1[0]), (ys1[1],)
    send_late(1, y_low, y_high)
    settle(local_sem, tally.at[pl.ds(0, 10 * X * Y)])
    send_late(0, near_low, near_high)

    lane = lax.broadcasted_iota(jnp.int32, (Y, Z), 1)
    quad = lax.rem(lane, 4)

    def pack(buf, stage, planes, packed):
        for f in range(NF + 1):
            for x in planes:
                base = f * F4 + 4 * x
                value = buf[f, x + 2, PAD:PAD + Y, :] if f < NF else oz[x]
                inside = (lane >= base) & (lane < base + 4)
                packed = jnp.where(inside, pltpu.roll(value, base + 2, 1), packed)
        pk[stage] = packed

    pack(buf1, 0, range(X), jnp.zeros((Y, Z), jnp.float32))
    zs1 = z_copies(0, 5)

    send_late(2, (zs1[0],), ())
    send_late(0, rest_low, rest_high)
    limit = jnp.where(me[2] == 0, CUTZ, 0)

    def factors(v, solid, cut):
        weight = jnp.sum(jnp.where(lane < CUTZ, v, 0.0), axis=1, keepdims=True)
        return (
            jnp.where(solid, 0.0, 1.0 / jnp.maximum(v, VOLUME_FLOOR)),
            jnp.where(cut & (lane < limit), 1.0 - v, 0.0),
            jnp.where(lane < limit, v / weight, 0.0),
        )

    for x in range(X):
        scale[x], keep[x], gain[x] = factors(vol[x], flg[x] == 2, flg[x] == 1)

    def boundary_z(stage):
        own = pk[stage]
        still = jnp.where(quad == 0, pltpu.roll(own, Z - 2, 1), pltpu.roll(own, Z - 1, 1))
        low = jnp.where(bottom, still, rec_low[stage])
        high = rec_high[0] if stage == 0 else jnp.where(top, rec_high[0], rec_high[stage])
        lefts, rights, slopes = [], [], []
        for c in (jnp.where(quad < 2, own, high), jnp.where(quad < 2, low, own)):
            d = c - pltpu.roll(c, 1, 1)
            s = minmod(d, pltpu.roll(d, Z - 1, 1))
            slopes.append(s)
            lefts.append(c + 0.5 * s)
            rights.append(c - 0.5 * s)
        first_lane = quad == 0
        left = jnp.where(first_lane, pltpu.roll(lefts[0], Z - 1, 1), lefts[1])
        right = jnp.where(
            first_lane, pltpu.roll(rights[0], Z - 2, 1), pltpu.roll(rights[1], Z - 1, 1)
        )
        sfix[...] = jnp.where(
            first_lane, pltpu.roll(slopes[0], Z - 1, 1), pltpu.roll(slopes[1], Z - 1, 1)
        )
        opening = jnp.where(
            first_lane, pltpu.roll(high, Z - 2, 1), pltpu.roll(own, Z - 1, 1)
        )
        ls = [pltpu.roll(left, Z - f * F4, 1) if f else left for f in range(NF)]
        rs = [pltpu.roll(right, Z - f * F4, 1) if f else right for f in range(NF)]
        opening = pltpu.roll(opening, Z - NF * F4, 1)
        live = lane < F4
        ls = [jnp.where(live & (quad < 2), w, 1.0) for w in ls]
        rs = [jnp.where(live & (quad < 2), w, 1.0) for w in rs]
        g = face(ls, rs, 3, 0.5 * opening)
        for f in range(NF):
            gfix[f] = g[f]
        afix[...] = opening

    def local_part(x, buf, acc):
        v = [buf[f, x + 2, PAD:PAD + Y, :] for f in range(NF)]
        press[x] = pressure_of(v, 1.0 / v[0])
        for f in range(NF):
            d = v[f] - pltpu.roll(v[f], 1, 1)
            inner[f, x] = minmod(d, pltpu.roll(d, Z - 1, 1))

    def z_part(x, buf, acc):
        v = [buf[f, x + 2, PAD:PAD + Y, :] for f in range(NF)]
        p = press[x]
        a = oz[x]
        shift = Z - (4 * x + 1)
        sl = []
        for f in range(NF):
            s = inner[f, x]
            fix = pltpu.roll(sfix[...], lax.rem(2 * Z - (f * F4 + 4 * x + 1), Z), 1)
            sl.append(0.5 * jnp.where((lane == 0) | (lane == Z - 1), fix, s))
        left = [pltpu.roll(v[f] + sl[f], 1, 1) for f in range(NF)]
        right = [v[f] - sl[f] for f in range(NF)]
        g = face(left, right, 3, 0.5 * a)
        div = [acc[f, x] for f in range(NF)]
        for f in range(NF):
            fix = pltpu.roll(gfix[f], shift, 1)
            low = jnp.where(lane == 0, fix, g[f])
            high = jnp.where(lane == Z - 1, fix, pltpu.roll(g[f], Z - 1, 1))
            div[f] = div[f] + (high - low)
        a_high = jnp.where(
            lane == Z - 1, pltpu.roll(afix[...], shift, 1), pltpu.roll(a, Z - 1, 1)
        )
        div[3] = div[3] - p * (a_high - a)
        for f in range(NF):
            acc[f, x] = div[f]

    def y_part(x, buf, acc):
        p = press[x]
        E = Y + 8
        left, right, div = [], [], []
        for f in range(NF):
            c = buf[f, x + 2, PAD - 1:PAD - 1 + E, :]
            b = buf[f, x + 2, PAD - 2:PAD - 2 + E, :]
            n = buf[f, x + 2, PAD:PAD + E, :]
            s = 0.5 * minmod(c - b, n - c)
            left.append(c + s)
            right.append(pltpu.roll(c - s, E - 1, 0))
        a = oy[x]
        g = face(left, right, 2, 0.5 * a)
        for f in range(NF):
            div.append(pltpu.roll(g[f], E - 1, 0)[:Y] - g[f][:Y])
        div[2] = div[2] - p * (oy[x, 1:Y + 1, :] - oy[x, 0:Y, :])
        for f in range(NF):
            acc[f, x] = div[f]

    def load(buf, f, x):
        return buf[f, x + 2, PAD:PAD + Y, :]

    def half_slope(buf, x):
        out = []
        for f in range(NF):
            c = load(buf, f, x)
            out.append(0.5 * minmod(c - load(buf, f, x - 1), load(buf, f, x + 1) - c))
        return out

    def x_face(buf, x, s_low, s_high):
        left = [load(buf, f, x - 1) + s_low[f] for f in range(NF)]
        right = [load(buf, f, x) - s_high[f] for f in range(NF)]
        return face(left, right, 1, 0.5 * ox[x])

    def x_inner(buf, acc):
        below = half_slope(buf, 1)
        for f in range(NF):
            edge[0, f] = below[f]
        for x in range(2, X - 1):
            s = half_slope(buf, x)
            g = x_face(buf, x, below, s)
            for f in range(NF):
                acc[f, x - 1] += g[f]
                acc[f, x] -= g[f]
            below = s
        for f in range(NF):
            edge[1, f] = below[f]
        for x in range(X):
            push = press[x] * (ox[x + 1] - ox[x]) if x < X - 1 else -press[x] * ox[x]
            acc[1, x] -= push

    def x_near(buf, acc, side):
        x = X - 1 if side else 0
        s = half_slope(buf, x)
        for f in range(NF):
            outer[side, f] = s[f]
        inner_s = [edge[side, f] for f in range(NF)]
        g = x_face(buf, x, inner_s, s) if side else x_face(buf, 1, s, inner_s)
        for f in range(NF):
            if side:
                acc[f, X - 2] += g[f]
                acc[f, X - 1] -= g[f]
            else:
                acc[f, 1] -= g[f]
                acc[f, 0] += g[f]

    def x_last(buf, side):
        s = [outer[side, f] for f in range(NF)]
        if side:
            return x_face(buf, X, s, half_slope(buf, X))
        return [-v for v in x_face(buf, 0, half_slope(buf, -1), s)]

    def rates_of(total, scales, keeps, gains):
        rates = []
        for f in range(NF):
            base = -total[f] * scales
            moved = jnp.sum(keeps * base, axis=1, keepdims=True)
            rates.append((1.0 - keeps) * base + gains * moved)
        return rates

    def cell_total(acc, c, g):
        total = [acc[f, c] for f in range(NF)]
        if g is not None:
            total = [t + v for t, v in zip(total, g)]
            if c == X - 1:
                total[1] = total[1] - press[c] * ox[X]
        return total

    def loop(step, buf, acc):
        def body(x, carry):
            step(x, buf, acc)
            return carry

        lax.fori_loop(0, X, body, 0, unroll=True)

    @pl.when(early_up[1] | early_down[1])
    def _():
        pl.semaphore_wait(ready.at[2], jnp.where(early_up[1], 1, 0) + jnp.where(early_down[1], 1, 0))

    send_early_up(1, y_high, None)
    send_early_down(1, y_low, None)
    loop(local_part, buf1, acc1)
    send_early_up(0, near_high, 1)
    send_early_up(2, (zs1[1],), 4)
    settle(recv_sem.at[4], tally.at[pl.ds(0, X * (4 * NF + 1))])
    loop(y_part, buf1, acc1)
    send_early_down(0, near_low, 0)
    send_early_down(0, rest_low, None)
    send_early_up(0, rest_high, None)
    send_early_down(2, (zs1[0],), 3)

    @pl.when(bottom)
    def _():
        settle(recv_sem.at[5], tally.at[pl.ds(0, Y)])

    @pl.when(jnp.logical_not(bottom))
    def _():
        settle(recv_sem.at[5], tally.at[pl.ds(0, 2 * Y)])

    boundary_z(0)
    loop(z_part, buf1, acc1)
    x_inner(buf1, acc1)

    ys2 = y_copies(buf2, 2, PAD, buf2, 8)
    zs2 = z_copies(1, 9)

    def advance(c, place, rates):
        for f in range(NF):
            now = buf1[f, place, PAD:PAD + Y, :]
            buf2[f, place, PAD:PAD + Y, :] = now + TIME_STEP * rates[f]

    def finish_first(c, g=None):
        rates = rates_of(cell_total(acc1, c, g), scale[c], keep[c], gain[c])
        for f in range(NF):
            first[f, c] = rates[f]
        advance(c, c + 2, rates)

    near_low[0].wait_recv()
    x_near(buf1, acc1, 1)
    near_high[0].wait_recv()
    x_near(buf1, acc1, 0)
    second = (
        remote(acc1.at[:, pl.ds(0, 1)], part.at[1], 6, down[0]),
        remote(acc1.at[:, pl.ds(X - 1, 1)], part.at[0], 7, up[0]),
        layer(buf2, 1, buf2, X + 3, 6, down[0]),
        layer(buf2, X - 2, buf2, 0, 7, up[0]),
    )
    second[0].start()
    second[1].start()
    finish_first(1)
    second[2].start()
    for c in range(2, X - 1):
        finish_first(c)
    second[3].start()
    pack(buf2, 1, range(1, X - 1), jnp.zeros((Y, Z), jnp.float32))
    settle(recv_sem.at[2], tally.at[pl.ds(0, (NF + 2) * Y)])
    g = x_last(buf1, 1)
    for f in range(NF):
        face_x[1, f] = -g[f]
    finish_first(X - 1, g)
    settle(recv_sem.at[3], tally.at[pl.ds(0, (NF + 1) * Y)])
    g = x_last(buf1, 0)
    for f in range(NF):
        face_x[0, f] = -g[f]
    finish_first(0, g)
    for c in ys2:
        c.start()
    pack(buf2, 1, (0, X - 1), pk[1])

    @pl.when(jnp.logical_not(bottom))
    def _():
        zs2[0].start()

    @pl.when(jnp.logical_not(top))
    def _():
        zs2[1].start()

    w = [buf1[f, 1, PAD:PAD + Y, :] for f in range(NF)]
    face_x[0, 1] -= pressure_of(w, 1.0 / w[0]) * ox[0]
    for side in (0, 1):
        v = vol_side[side]
        scale_side[side], keep_side[side], gain_side[side] = factors(v, v <= 0.0, (v > 0.0) & (v < 1.0))
    loop(local_part, buf2, acc2)
    settle(recv_sem.at[8], tally.at[pl.ds(0, 4 * NF * X)])
    loop(y_part, buf2, acc2)
    x_inner(buf2, acc2)

    @pl.when(top | bottom)
    def _():
        settle(recv_sem.at[9], tally.at[pl.ds(0, Y)])

    @pl.when(jnp.logical_not(top | bottom))
    def _():
        settle(recv_sem.at[9], tally.at[pl.ds(0, 2 * Y)])

    boundary_z(1)
    loop(z_part, buf2, acc2)

    def finish_second(c, g=None):
        rates = rates_of(cell_total(acc2, c, g), scale[c], keep[c], gain[c])
        for f in range(NF):
            out[f, c] = 0.5 * (first[f, c] + rates[f])

    for side in (1, 0):
        settle(recv_sem.at[6 if side else 7], tally.at[pl.ds(0, 2 * NF * Y)])
        total = [part[side, f, 0] + face_x[side, f] for f in range(NF)]
        advance(None, X + 2 if side else 1, rates_of(total, scale_side[side], keep_side[side], gain_side[side]))
        x_near(buf2, acc2, side)
        finish_second(X - 1 if side else 0, x_last(buf2, side))
        for c in range(X // 2, X - 1) if side else range(1, X // 2):
            finish_second(c)

    sent = 8 * NF * Y + 8 * NF * X + 3 * Y + X

    @pl.when(top)
    def _():
        settle(send_sem, tally.at[pl.ds(0, sent + 2 * Y)])

    @pl.when(bottom)
    def _():
        settle(send_sem, tally.at[pl.ds(0, sent + 3 * Y)])

    @pl.when(jnp.logical_not(top | bottom))
    def _():
        settle(send_sem, tally.at[pl.ds(0, sent + 4 * Y)])


def on_device(state, volume, apertures, flags):
    _, X, Y, Z = state.shape
    f32 = jnp.float32
    wide = pltpu.VMEM((NF, X + 4, Y + 2 * PAD, Z), f32)
    cells = pltpu.VMEM((X, Y, Z), f32)
    fields = pltpu.VMEM((NF, X, Y, Z), f32)
    layer = pltpu.VMEM((Y, Z), f32)
    pair = pltpu.VMEM((2, Y, Z), f32)
    sides = pltpu.VMEM((2, NF, Y, Z), f32)
    return pl.pallas_call(
        kernel,
        out_shape=pltpu.VMEM(state.shape, f32),
        in_specs=[pl.BlockSpec(memory_space=pl.ANY)] * 4,
        out_specs=pl.BlockSpec(memory_space=pltpu.VMEM),
        scratch_shapes=[
            wide, wide,
            pltpu.VMEM((X + 1, Y, Z), f32),
            pltpu.VMEM((X, Y + 8, Z), f32),
            cells, cells, pltpu.VMEM((X, Y, Z), jnp.int32),
            pair, pair, pair,
            pltpu.VMEM((NF, Y, Z), f32), layer, layer,
            fields, fields, fields, cells, cells, cells, cells, fields, sides, sides,
            pair, pltpu.VMEM((2, NF, 1, Y, Z), f32), sides, pair, pair, pair,
            pltpu.VMEM((8 * NF * (X + Y) + 16 * Y + 8 * X, Z), f32),
            pltpu.SemaphoreType.DMA,
            pltpu.SemaphoreType.DMA,
            pltpu.SemaphoreType.DMA((10,)),
            pltpu.SemaphoreType.REGULAR((5,)),
        ],
        compiler_params=pltpu.CompilerParams(collective_id=0, has_side_effects=True),
    )(state, volume, apertures, flags)


def solution(mesh):
    in_specs = (
        P(None, "gx", "gy", "gz"),
        P("gx", "gy", "gz"),
        P(None, "gx", "gy", "gz"),
        P("gx", "gy", "gz"),
    )
    return jax.shard_map(
        on_device, mesh=mesh, in_specs=in_specs, out_specs=P(None, "gx", "gy", "gz"),
        check_vma=False,
    )
```

```python
import jax
import jax.numpy as jnp
from jax import lax
from jax.experimental import pallas as pl
from jax.experimental.pallas import tpu as pltpu
from jax.sharding import PartitionSpec as P

CUTZ = 32
NF = 5
GAMMA_LESS = 0.4
DISSIPATION = 4.0
TIME_STEP = 0.02
VOLUME_FLOOR = 0.5
PAD = 8

MESH = pl.DeviceIdType.MESH


def minmod(a, b):
    return jnp.maximum(jnp.minimum(a, b), 0.0) + jnp.minimum(jnp.maximum(a, b), 0.0)


def pressure_of(w, inverse):
    kinetic = w[1] * w[1] + w[2] * w[2] + w[3] * w[3]
    return GAMMA_LESS * (w[4] - 0.5 * kinetic * inverse)


def flux(w, d):
    inverse = 1.0 / w[0]
    u = w[d] * inverse
    p = pressure_of(w, inverse)
    out = [w[d], w[1] * u, w[2] * u, w[3] * u, (w[4] + p) * u]
    out[d] = out[d] + p
    return out


def face(left, right, d, half_open):
    fl, fr = flux(left, d), flux(right, d)
    return [
        ((fl[f] + fr[f]) + DISSIPATION * (left[f] - right[f])) * half_open for f in range(NF)
    ]


def kernel(
    state, volume, apertures, flags, out,
    buf1, buf2, ox, oy, oz, vol, flg, pk, rec_low, rec_high, fix, slope_pk, press_pk,
    acc1, acc2, first, scale, keep, gain, press, inner, edge, outer,
    vol_side, part, face_x, scale_side, keep_side, gain_side, tally,
    local_sem, send_sem, recv_sem, ready,
):
    _, X, Y, Z = state.shape
    F4 = 4 * X
    me = [lax.axis_index(a) for a in ("gx", "gy", "gz")]
    size = [lax.axis_size(a) for a in ("gx", "gy", "gz")]
    up = [{a: lax.rem(me[i] + 1, size[i])} for i, a in enumerate(("gx", "gy", "gz"))]
    down = [{a: lax.rem(me[i] + size[i] - 1, size[i])} for i, a in enumerate(("gx", "gy", "gz"))]

    rows = pl.ds(PAD, Y)
    def settle(sem, ref):
        pltpu.make_async_copy(ref, ref, sem).wait()

    loads = [
        (state, buf1.at[:, pl.ds(2, X), rows, :]),
        (apertures.at[0], ox.at[pl.ds(0, X)]),
        (apertures.at[1], oy.at[:, pl.ds(0, Y), :]),
        (apertures.at[2], oz),
        (volume, vol),
        (flags, flg),
    ]
    loads = [pltpu.make_async_copy(s, d, local_sem) for s, d in loads]
    for load in loads:
        load.start()

    barrier = pltpu.get_barrier_semaphore()
    n_z = size[2]
    bottom, top = me[2] == 0, me[2] == n_z - 1
    early_up = [me[i] < size[i] // 2 for i in range(2)] + [jnp.logical_not(top)]
    early_down = [(me[i] == 0) | (me[i] > size[i] // 2) for i in range(2)] + [bottom]
    late_up = [jnp.logical_not(e) for e in early_up]
    late_down = [jnp.logical_not(e) for e in early_down]
    late_edges = 0
    for i in range(3):
        @pl.when(early_up[i])
        def _():
            pl.semaphore_signal(barrier, inc=1, device_id=up[i], device_id_type=MESH)

        @pl.when(early_down[i])
        def _():
            pl.semaphore_signal(barrier, inc=1, device_id=down[i], device_id_type=MESH)

        late_edges = late_edges + jnp.where(late_up[i], 1, 0) + jnp.where(late_down[i], 1, 0)

    up_slot, down_slot = (1, 2, 4), (0, 2, 3)

    @pl.when(late_edges > 0)
    def _():
        pl.semaphore_wait(barrier, late_edges)

    for i in range(3):
        @pl.when(late_down[i])
        def _():
            pl.semaphore_signal(ready.at[up_slot[i]], inc=1, device_id=down[i], device_id_type=MESH)

        @pl.when(late_up[i])
        def _():
            pl.semaphore_signal(ready.at[down_slot[i]], inc=1, device_id=up[i], device_id_type=MESH)

    def send_late(i, low, high):
        @pl.when(late_down[i])
        def _():
            for c in low:
                c.start()

        @pl.when(late_up[i])
        def _():
            for c in high:
                c.start()

    def send_early_up(i, high, slot):
        @pl.when(early_up[i])
        def _():
            if slot is not None:
                pl.semaphore_wait(ready.at[slot], 1)
            for c in high:
                c.start()

    def send_early_down(i, low, slot):
        @pl.when(early_down[i])
        def _():
            if slot is not None:
                pl.semaphore_wait(ready.at[slot], 1)
            for c in low:
                c.start()

    def remote(src, dst, recv, target):
        return pltpu.make_async_remote_copy(
            src_ref=src, dst_ref=dst, send_sem=send_sem, recv_sem=recv_sem.at[recv],
            device_id=target, device_id_type=MESH,
        )

    def layer(src, cell, dst, place, recv, target):
        return remote(
            src.at[:, pl.ds(2 + cell, 1), rows, :], dst.at[:, pl.ds(place, 1), rows, :],
            recv, target,
        )

    def y_copies(src, x0, y0, buf, recv):
        mid = pl.ds(x0, X)
        return (
            remote(src.at[:, mid, pl.ds(y0, 2), :],
                   buf.at[:, pl.ds(2, X), pl.ds(PAD + Y, 2), :], recv, down[1]),
            remote(src.at[:, mid, pl.ds(y0 + Y - 2, 2), :],
                   buf.at[:, pl.ds(2, X), pl.ds(PAD - 2, 2), :], recv, up[1]),
        )

    def z_copies(stage, recv):
        return (
            remote(pk.at[stage], rec_high.at[stage], recv, down[2]),
            remote(pk.at[stage], rec_low.at[stage], recv, up[2]),
        )

    near_low = (layer(buf1, 0, buf1, X + 2, 0, down[0]),)
    near_high = (layer(buf1, X - 1, buf1, 1, 1, up[0]),)
    rest_low = (
        layer(buf1, 1, buf1, X + 3, 2, down[0]),
        remote(ox.at[pl.ds(0, 1)], ox.at[pl.ds(X, 1)], 2, down[0]),
        remote(vol.at[pl.ds(0, 1)], vol_side.at[pl.ds(1, 1)], 2, down[0]),
    )
    rest_high = (
        layer(buf1, X - 2, buf1, 0, 3, up[0]),
        remote(vol.at[pl.ds(X - 1, 1)], vol_side.at[pl.ds(0, 1)], 3, up[0]),
    )
    ys1 = y_copies(state, 0, 0, buf1, 4)
    ay = remote(apertures.at[1, :, pl.ds(0, 1), :], oy.at[:, pl.ds(Y, 1), :], 4, down[1])
    y_low, y_high = (ay, ys1[0]), (ys1[1],)
    send_late(1, y_low, y_high)
    settle(local_sem, tally.at[pl.ds(0, 10 * X * Y)])
    send_late(0, near_low, near_high)

    lane = lax.broadcasted_iota(jnp.int32, (Y, Z), 1)
    quad = lax.rem(lane, 4)

    def pack(buf, stage, planes, packed):
        for f in range(NF + 1):
            for x in planes:
                base = f * F4 + 4 * x
                value = buf[f, x + 2, PAD:PAD + Y, :] if f < NF else oz[x]
                inside = (lane >= base) & (lane < base + 4)
                packed = jnp.where(inside, pltpu.roll(value, base + 2, 1), packed)
        pk[stage] = packed

    pack(buf1, 0, range(X), jnp.zeros((Y, Z), jnp.float32))
    zs1 = z_copies(0, 5)

    send_late(2, (zs1[0],), ())
    send_late(0, rest_low, rest_high)
    limit = jnp.where(me[2] == 0, CUTZ, 0)

    def factors(v, solid, cut):
        weight = jnp.sum(jnp.where(lane < CUTZ, v, 0.0), axis=1, keepdims=True)
        return (
            jnp.where(solid, 0.0, 1.0 / jnp.maximum(v, VOLUME_FLOOR)),
            jnp.where(cut & (lane < limit), 1.0 - v, 0.0),
            jnp.where(lane < limit, v / weight, 0.0),
        )

    for x in range(X):
        scale[x], keep[x], gain[x] = factors(vol[x], flg[x] == 2, flg[x] == 1)

    def pack_slopes():
        slopes, pressures = jnp.zeros((Y, Z), jnp.float32), jnp.zeros((Y, Z), jnp.float32)
        for x in range(X):
            for f in range(NF):
                base = f * F4 + 4 * x
                inside = (lane >= base) & (lane < base + 4)
                slopes = jnp.where(inside, pltpu.roll(inner[f, x], base + 2, 1), slopes)
            inside = (lane >= 4 * x) & (lane < 4 * x + 4)
            pressures = jnp.where(inside, pltpu.roll(press[x], 4 * x + 2, 1), pressures)
        slope_pk[...] = 0.5 * slopes
        press_pk[...] = pressures

    def boundary_z(stage):
        own = pk[stage]
        still = jnp.where(quad == 0, pltpu.roll(own, Z - 2, 1), pltpu.roll(own, Z - 1, 1))
        low = jnp.where(bottom, still, rec_low[stage])
        high = rec_high[0] if stage == 0 else jnp.where(top, rec_high[0], rec_high[stage])
        lower, upper = jnp.where(quad < 2, low, own), jnp.where(quad < 2, own, high)

        def halves(c):
            d = c - pltpu.roll(c, 1, 1)
            return 0.5 * minmod(d, pltpu.roll(d, Z - 1, 1))

        s_low = jnp.where(quad == 3, slope_pk[...], halves(lower))
        s_high = jnp.where(quad == 0, slope_pk[...], halves(upper))
        left = jnp.where(quad < 2, upper + s_high, pltpu.roll(lower + s_low, 1, 1))
        right = jnp.where(quad < 2, pltpu.roll(upper - s_high, Z - 1, 1), lower - s_low)
        opening = jnp.where(
            quad < 2, pltpu.roll(jnp.where(quad == 2, high, own), Z - 1, 1), own
        )
        ls = [pltpu.roll(left, Z - f * F4, 1) if f else left for f in range(NF)]
        rs = [pltpu.roll(right, Z - f * F4, 1) if f else right for f in range(NF)]
        opening = pltpu.roll(opening, Z - NF * F4, 1)
        live = lane < F4
        ls = [jnp.where(live, w, 1.0) for w in ls]
        rs = [jnp.where(live, w, 1.0) for w in rs]
        g = face(ls, rs, 3, 0.5 * opening)
        for f in range(NF):
            before, after = pltpu.roll(g[f], 1, 1), pltpu.roll(g[f], Z - 1, 1)
            change = jnp.where(
                quad == 0, g[f],
                jnp.where(quad == 1, g[f] - before, jnp.where(quad == 2, after - g[f], -g[f])),
            )
            if f == 3:
                change = change - jnp.where(quad == 1, press_pk[...] * opening, 0.0)
            fix[f] = change

    def local_part(x, buf, acc):
        v = [buf[f, x + 2, PAD:PAD + Y, :] for f in range(NF)]
        press[x] = pressure_of(v, 1.0 / v[0])
        for f in range(NF):
            d = v[f] - pltpu.roll(v[f], 1, 1)
            inner[f, x] = minmod(d, pltpu.roll(d, Z - 1, 1))

    def z_part(x, buf, acc):
        v = [buf[f, x + 2, PAD:PAD + Y, :] for f in range(NF)]
        p = press[x]
        a = oz[x]
        sl = [0.5 * inner[f, x] for f in range(NF)]
        left = [pltpu.roll(v[f] + sl[f], 1, 1) for f in range(NF)]
        right = [v[f] - sl[f] for f in range(NF)]
        g = face(left, right, 3, jnp.where((lane >= 2) & (lane < Z - 1), 0.5 * a, 0.0))
        div = [acc[f, x] + (pltpu.roll(g[f], Z - 1, 1) - g[f]) for f in range(NF)]
        div[3] = div[3] - p * (jnp.where(lane == Z - 1, 0.0, pltpu.roll(a, Z - 1, 1)) - a)
        for f in range(NF):
            acc[f, x] = div[f]

    def z_fix(x, buf, acc):
        ends = (lane < 2) | (lane >= Z - 2)
        for f in range(NF):
            acc[f, x] += jnp.where(ends, pltpu.roll(fix[f], Z - (4 * x + 2), 1), 0.0)

    def y_part(x, buf, acc):
        p = press[x]
        E = Y + 8
        left, right, div = [], [], []
        for f in range(NF):
            c = buf[f, x + 2, PAD - 1:PAD - 1 + E, :]
            b = buf[f, x + 2, PAD - 2:PAD - 2 + E, :]
            n = buf[f, x + 2, PAD:PAD + E, :]
            s = 0.5 * minmod(c - b, n - c)
            left.append(c + s)
            right.append(pltpu.roll(c - s, E - 1, 0))
        a = oy[x]
        g = face(left, right, 2, 0.5 * a)
        for f in range(NF):
            div.append(pltpu.roll(g[f], E - 1, 0)[:Y] - g[f][:Y])
        div[2] = div[2] - p * (oy[x, 1:Y + 1, :] - oy[x, 0:Y, :])
        for f in range(NF):
            acc[f, x] = div[f]

    def load(buf, f, x):
        return buf[f, x + 2, PAD:PAD + Y, :]

    def half_slope(buf, x):
        out = []
        for f in range(NF):
            c = load(buf, f, x)
            out.append(0.5 * minmod(c - load(buf, f, x - 1), load(buf, f, x + 1) - c))
        return out

    def x_face(buf, x, s_low, s_high):
        left = [load(buf, f, x - 1) + s_low[f] for f in range(NF)]
        right = [load(buf, f, x) - s_high[f] for f in range(NF)]
        return face(left, right, 1, 0.5 * ox[x])

    def x_inner(buf, acc):
        below = half_slope(buf, 1)
        for f in range(NF):
            edge[0, f] = below[f]
        for x in range(2, X - 1):
            s = half_slope(buf, x)
            g = x_face(buf, x, below, s)
            for f in range(NF):
                acc[f, x - 1] += g[f]
                acc[f, x] -= g[f]
            below = s
        for f in range(NF):
            edge[1, f] = below[f]
        for x in range(X):
            push = press[x] * (ox[x + 1] - ox[x]) if x < X - 1 else -press[x] * ox[x]
            acc[1, x] -= push

    def x_near(buf, acc, side):
        x = X - 1 if side else 0
        s = half_slope(buf, x)
        for f in range(NF):
            outer[side, f] = s[f]
        inner_s = [edge[side, f] for f in range(NF)]
        g = x_face(buf, x, inner_s, s) if side else x_face(buf, 1, s, inner_s)
        for f in range(NF):
            if side:
                acc[f, X - 2] += g[f]
                acc[f, X - 1] -= g[f]
            else:
                acc[f, 1] -= g[f]
                acc[f, 0] += g[f]

    def x_last(buf, side):
        s = [outer[side, f] for f in range(NF)]
        if side:
            return x_face(buf, X, s, half_slope(buf, X))
        return [-v for v in x_face(buf, 0, half_slope(buf, -1), s)]

    def rates_of(total, scales, keeps, gains):
        rates = []
        for f in range(NF):
            base = -total[f] * scales
            moved = jnp.sum(keeps * base, axis=1, keepdims=True)
            rates.append((1.0 - keeps) * base + gains * moved)
        return rates

    def cell_total(acc, c, g):
        total = [acc[f, c] for f in range(NF)]
        if g is not None:
            total = [t + v for t, v in zip(total, g)]
            if c == X - 1:
                total[1] = total[1] - press[c] * ox[X]
        return total

    def loop(step, buf, acc):
        def body(x, carry):
            step(x, buf, acc)
            return carry

        lax.fori_loop(0, X, body, 0, unroll=True)

    @pl.when(early_up[1] | early_down[1])
    def _():
        pl.semaphore_wait(ready.at[2], jnp.where(early_up[1], 1, 0) + jnp.where(early_down[1], 1, 0))

    send_early_up(1, y_high, None)
    send_early_down(1, y_low, None)
    loop(local_part, buf1, acc1)
    send_early_up(0, near_high, 1)
    send_early_up(2, (zs1[1],), 4)
    settle(recv_sem.at[4], tally.at[pl.ds(0, X * (4 * NF + 1))])
    loop(y_part, buf1, acc1)
    send_early_down(0, near_low, 0)
    send_early_up(0, rest_high, None)
    send_early_down(0, rest_low, None)
    loop(z_part, buf1, acc1)
    pack_slopes()
    x_inner(buf1, acc1)
    send_early_down(2, (zs1[0],), 3)

    @pl.when(bottom)
    def _():
        settle(recv_sem.at[5], tally.at[pl.ds(0, Y)])

    @pl.when(jnp.logical_not(bottom))
    def _():
        settle(recv_sem.at[5], tally.at[pl.ds(0, 2 * Y)])

    boundary_z(0)
    loop(z_fix, buf1, acc1)

    ys2 = y_copies(buf2, 2, PAD, buf2, 8)
    zs2 = z_copies(1, 9)

    def advance(c, place, rates):
        for f in range(NF):
            now = buf1[f, place, PAD:PAD + Y, :]
            buf2[f, place, PAD:PAD + Y, :] = now + TIME_STEP * rates[f]

    def finish_first(c, g=None):
        rates = rates_of(cell_total(acc1, c, g), scale[c], keep[c], gain[c])
        for f in range(NF):
            first[f, c] = rates[f]
        advance(c, c + 2, rates)

    near_low[0].wait_recv()
    x_near(buf1, acc1, 1)
    near_high[0].wait_recv()
    x_near(buf1, acc1, 0)
    second = (
        remote(acc1.at[:, pl.ds(0, 1)], part.at[1], 6, down[0]),
        remote(acc1.at[:, pl.ds(X - 1, 1)], part.at[0], 7, up[0]),
        layer(buf2, 1, buf2, X + 3, 6, down[0]),
        layer(buf2, X - 2, buf2, 0, 7, up[0]),
    )
    high_first = late_up[0] & early_down[0]

    @pl.when(high_first)
    def _():
        second[1].start()

    @pl.when(jnp.logical_not(high_first))
    def _():
        second[0].start()

    for c in range(1, X - 1):
        finish_first(c)

    @pl.when(high_first)
    def _():
        for k in (3, 0, 2):
            second[k].start()

    @pl.when(jnp.logical_not(high_first))
    def _():
        for k in (2, 1, 3):
            second[k].start()

    pack(buf2, 1, range(1, X - 1), jnp.zeros((Y, Z), jnp.float32))
    settle(recv_sem.at[2], tally.at[pl.ds(0, (NF + 2) * Y)])
    g = x_last(buf1, 1)
    for f in range(NF):
        face_x[1, f] = -g[f]
    finish_first(X - 1, g)
    settle(recv_sem.at[3], tally.at[pl.ds(0, (NF + 1) * Y)])
    g = x_last(buf1, 0)
    for f in range(NF):
        face_x[0, f] = -g[f]
    finish_first(0, g)
    for c in ys2:
        c.start()
    pack(buf2, 1, (0, X - 1), pk[1])

    @pl.when(jnp.logical_not(bottom))
    def _():
        zs2[0].start()

    @pl.when(jnp.logical_not(top))
    def _():
        zs2[1].start()

    w = [buf1[f, 1, PAD:PAD + Y, :] for f in range(NF)]
    face_x[0, 1] -= pressure_of(w, 1.0 / w[0]) * ox[0]
    for side in (0, 1):
        v = vol_side[side]
        scale_side[side], keep_side[side], gain_side[side] = factors(v, v <= 0.0, (v > 0.0) & (v < 1.0))
    loop(local_part, buf2, acc2)
    settle(recv_sem.at[8], tally.at[pl.ds(0, 4 * NF * X)])
    loop(y_part, buf2, acc2)
    loop(z_part, buf2, acc2)
    pack_slopes()
    x_inner(buf2, acc2)

    @pl.when(top | bottom)
    def _():
        settle(recv_sem.at[9], tally.at[pl.ds(0, Y)])

    @pl.when(jnp.logical_not(top | bottom))
    def _():
        settle(recv_sem.at[9], tally.at[pl.ds(0, 2 * Y)])

    boundary_z(1)
    loop(z_fix, buf2, acc2)

    def finish_second(c, g=None):
        rates = rates_of(cell_total(acc2, c, g), scale[c], keep[c], gain[c])
        for f in range(NF):
            out[f, c] = 0.5 * (first[f, c] + rates[f])

    for side in (1, 0):
        settle(recv_sem.at[6 if side else 7], tally.at[pl.ds(0, 2 * NF * Y)])
        total = [part[side, f, 0] + face_x[side, f] for f in range(NF)]
        advance(None, X + 2 if side else 1, rates_of(total, scale_side[side], keep_side[side], gain_side[side]))
        x_near(buf2, acc2, side)
        finish_second(X - 1 if side else 0, x_last(buf2, side))
        for c in range(X // 2, X - 1) if side else range(1, X // 2):
            finish_second(c)

    sent = 8 * NF * Y + 8 * NF * X + 3 * Y + X

    @pl.when(top)
    def _():
        settle(send_sem, tally.at[pl.ds(0, sent + 2 * Y)])

    @pl.when(bottom)
    def _():
        settle(send_sem, tally.at[pl.ds(0, sent + 3 * Y)])

    @pl.when(jnp.logical_not(top | bottom))
    def _():
        settle(send_sem, tally.at[pl.ds(0, sent + 4 * Y)])


def on_device(state, volume, apertures, flags):
    _, X, Y, Z = state.shape
    f32 = jnp.float32
    wide = pltpu.VMEM((NF, X + 4, Y + 2 * PAD, Z), f32)
    cells = pltpu.VMEM((X, Y, Z), f32)
    fields = pltpu.VMEM((NF, X, Y, Z), f32)
    layer = pltpu.VMEM((Y, Z), f32)
    pair = pltpu.VMEM((2, Y, Z), f32)
    sides = pltpu.VMEM((2, NF, Y, Z), f32)
    return pl.pallas_call(
        kernel,
        out_shape=pltpu.VMEM(state.shape, f32),
        in_specs=[pl.BlockSpec(memory_space=pl.ANY)] * 4,
        out_specs=pl.BlockSpec(memory_space=pltpu.VMEM),
        scratch_shapes=[
            wide, wide,
            pltpu.VMEM((X + 1, Y, Z), f32),
            pltpu.VMEM((X, Y + 8, Z), f32),
            cells, cells, pltpu.VMEM((X, Y, Z), jnp.int32),
            pair, pair, pair,
            pltpu.VMEM((NF, Y, Z), f32), layer, layer,
            fields, fields, fields, cells, cells, cells, cells, fields, sides, sides,
            pair, pltpu.VMEM((2, NF, 1, Y, Z), f32), sides, pair, pair, pair,
            pltpu.VMEM((8 * NF * (X + Y) + 16 * Y + 8 * X, Z), f32),
            pltpu.SemaphoreType.DMA,
            pltpu.SemaphoreType.DMA,
            pltpu.SemaphoreType.DMA((10,)),
            pltpu.SemaphoreType.REGULAR((5,)),
        ],
        compiler_params=pltpu.CompilerParams(collective_id=0, has_side_effects=True),
    )(state, volume, apertures, flags)


def solution(mesh):
    in_specs = (
        P(None, "gx", "gy", "gz"),
        P("gx", "gy", "gz"),
        P(None, "gx", "gy", "gz"),
        P("gx", "gy", "gz"),
    )
    return jax.shard_map(
        on_device, mesh=mesh, in_specs=in_specs, out_specs=P(None, "gx", "gy", "gz"),
        check_vma=False,
    )
```

```python
import jax
import jax.numpy as jnp
from jax import lax
from jax.experimental import pallas as pl
from jax.experimental.pallas import tpu as pltpu
from jax.sharding import PartitionSpec as P

CUTZ = 32
NF = 5
GAMMA_LESS = 0.4
DISSIPATION = 4.0
TIME_STEP = 0.02
VOLUME_FLOOR = 0.5
PAD = 8

MESH = pl.DeviceIdType.MESH


def minmod(a, b):
    return jnp.maximum(jnp.minimum(a, b), 0.0) + jnp.minimum(jnp.maximum(a, b), 0.0)


def pressure_of(w, inverse):
    kinetic = w[1] * w[1] + w[2] * w[2] + w[3] * w[3]
    return GAMMA_LESS * (w[4] - 0.5 * kinetic * inverse)


def flux(w, d):
    inverse = 1.0 / w[0]
    u = w[d] * inverse
    p = pressure_of(w, inverse)
    out = [w[d], w[1] * u, w[2] * u, w[3] * u, (w[4] + p) * u]
    out[d] = out[d] + p
    return out


def face(left, right, d, half_open):
    fl, fr = flux(left, d), flux(right, d)
    return [
        ((fl[f] + fr[f]) + DISSIPATION * (left[f] - right[f])) * half_open for f in range(NF)
    ]


def kernel(
    state, volume, apertures, flags, out,
    buf1, buf2, ox, oy, oz, vol, flg, pk, rec_low, rec_high, fix, slope_pk, press_pk,
    acc1, acc2, first, scale, keep, gain, press, inner, edge, outer,
    vol_side, part, face_x, scale_side, keep_side, gain_side, tally,
    send_sem, recv_sem, ready,
):
    _, X, Y, Z = state.shape
    F4 = 4 * X
    me = [lax.axis_index(a) for a in ("gx", "gy", "gz")]
    size = [lax.axis_size(a) for a in ("gx", "gy", "gz")]
    up = [{a: lax.rem(me[i] + 1, size[i])} for i, a in enumerate(("gx", "gy", "gz"))]
    down = [{a: lax.rem(me[i] + size[i] - 1, size[i])} for i, a in enumerate(("gx", "gy", "gz"))]

    rows = pl.ds(PAD, Y)
    def settle(sem, ref):
        pltpu.make_async_copy(ref, ref, sem).wait()

    loads = [
        (state, buf1.at[:, pl.ds(2, X), rows, :]),
        (apertures.at[0], ox.at[pl.ds(0, X)]),
        (apertures.at[1], oy.at[:, pl.ds(0, Y), :]),
        (apertures.at[2], oz),
        (volume, vol),
        (flags, flg),
    ]
    loads = [pltpu.make_async_copy(s, d, send_sem) for s, d in loads]
    for load in loads:
        load.start()

    barrier = pltpu.get_barrier_semaphore()
    n_z = size[2]
    bottom, top = me[2] == 0, me[2] == n_z - 1
    early_up = [me[i] < size[i] // 2 for i in range(2)] + [jnp.logical_not(top)]
    early_down = [(me[i] == 0) | (me[i] > size[i] // 2) for i in range(2)] + [bottom]
    late_up = [jnp.logical_not(e) for e in early_up]
    late_down = [jnp.logical_not(e) for e in early_down]
    late_edges = 0
    for i in range(3):
        @pl.when(early_up[i])
        def _():
            pl.semaphore_signal(barrier, inc=1, device_id=up[i], device_id_type=MESH)

        @pl.when(early_down[i])
        def _():
            pl.semaphore_signal(barrier, inc=1, device_id=down[i], device_id_type=MESH)

        late_edges = late_edges + jnp.where(late_up[i], 1, 0) + jnp.where(late_down[i], 1, 0)

    up_slot, down_slot = (1, 2, 4), (0, 2, 3)

    @pl.when(late_edges > 0)
    def _():
        pl.semaphore_wait(barrier, late_edges)

    for i in range(3):
        @pl.when(late_down[i])
        def _():
            pl.semaphore_signal(ready.at[up_slot[i]], inc=1, device_id=down[i], device_id_type=MESH)

        @pl.when(late_up[i])
        def _():
            pl.semaphore_signal(ready.at[down_slot[i]], inc=1, device_id=up[i], device_id_type=MESH)

    def send_late(i, low, high):
        @pl.when(late_down[i])
        def _():
            for c in low:
                c.start()

        @pl.when(late_up[i])
        def _():
            for c in high:
                c.start()

    def send_early_up(i, high, slot):
        @pl.when(early_up[i])
        def _():
            if slot is not None:
                pl.semaphore_wait(ready.at[slot], 1)
            for c in high:
                c.start()

    def send_early_down(i, low, slot):
        @pl.when(early_down[i])
        def _():
            if slot is not None:
                pl.semaphore_wait(ready.at[slot], 1)
            for c in low:
                c.start()

    def remote(src, dst, recv, target):
        return pltpu.make_async_remote_copy(
            src_ref=src, dst_ref=dst, send_sem=send_sem, recv_sem=recv_sem.at[recv],
            device_id=target, device_id_type=MESH,
        )

    def layer(src, cell, dst, place, recv, target):
        return remote(
            src.at[:, pl.ds(2 + cell, 1), rows, :], dst.at[:, pl.ds(place, 1), rows, :],
            recv, target,
        )

    def y_copies(src, x0, y0, buf, recv):
        mid = pl.ds(x0, X)
        return (
            remote(src.at[:, mid, pl.ds(y0, 2), :],
                   buf.at[:, pl.ds(2, X), pl.ds(PAD + Y, 2), :], recv, down[1]),
            remote(src.at[:, mid, pl.ds(y0 + Y - 2, 2), :],
                   buf.at[:, pl.ds(2, X), pl.ds(PAD - 2, 2), :], recv, up[1]),
        )

    def z_copies(stage, recv):
        return (
            remote(pk.at[stage], rec_high.at[stage], recv, down[2]),
            remote(pk.at[stage], rec_low.at[stage], recv, up[2]),
        )

    near_low = (layer(buf1, 0, buf1, X + 2, 0, down[0]),)
    near_high = (layer(buf1, X - 1, buf1, 1, 1, up[0]),)
    rest_low = (
        layer(buf1, 1, buf1, X + 3, 2, down[0]),
        remote(ox.at[pl.ds(0, 1)], ox.at[pl.ds(X, 1)], 2, down[0]),
    )
    rest_high = (layer(buf1, X - 2, buf1, 0, 3, up[0]),)
    volume_low = (remote(vol.at[pl.ds(0, 1)], vol_side.at[pl.ds(1, 1)], 10, down[0]),)
    volume_high = (remote(vol.at[pl.ds(X - 1, 1)], vol_side.at[pl.ds(0, 1)], 10, up[0]),)
    ys1 = y_copies(buf1, 2, PAD, buf1, 4)
    ay = remote(oy.at[:, pl.ds(0, 1), :], oy.at[:, pl.ds(Y, 1), :], 4, down[1])
    y_low, y_high = (ay, ys1[0]), (ys1[1],)
    settle(send_sem, tally.at[pl.ds(0, 10 * X * Y)])
    send_late(1, y_low, y_high)
    send_late(0, near_low, near_high)

    lane = lax.broadcasted_iota(jnp.int32, (Y, Z), 1)
    quad = lax.rem(lane, 4)

    def pack(buf, stage, planes, packed):
        for f in range(NF + 1):
            for x in planes:
                base = f * F4 + 4 * x
                value = buf[f, x + 2, PAD:PAD + Y, :] if f < NF else oz[x]
                inside = (lane >= base) & (lane < base + 4)
                packed = jnp.where(inside, pltpu.roll(value, base + 2, 1), packed)
        pk[stage] = packed

    def still_below(stage):
        @pl.when(bottom)
        def _():
            own = pk[stage]
            rec_low[stage] = jnp.where(
                quad == 0, pltpu.roll(own, Z - 2, 1), pltpu.roll(own, Z - 1, 1)
            )

    pack(buf1, 0, range(X), jnp.zeros((Y, Z), jnp.float32))
    zs1 = z_copies(0, 5)

    send_late(2, (zs1[0],), ())
    still_below(0)
    send_late(0, rest_low + volume_low, rest_high + volume_high)
    limit = jnp.where(me[2] == 0, CUTZ, 0)

    def factors(v, solid, cut):
        weight = jnp.sum(jnp.where(lane < CUTZ, v, 0.0), axis=1, keepdims=True)
        inverse = jnp.where(solid, 0.0, -1.0 / jnp.maximum(v, VOLUME_FLOOR))
        excess = jnp.where(cut & (lane < limit), 1.0 - v, 0.0)
        return (
            (1.0 - excess) * inverse,
            excess * inverse,
            jnp.where(lane < limit, v / weight, 0.0),
        )

    for x in range(X):
        scale[x], keep[x], gain[x] = factors(vol[x], flg[x] == 2, flg[x] == 1)

    def pack_slopes():
        slopes, pressures = jnp.zeros((Y, Z), jnp.float32), jnp.zeros((Y, Z), jnp.float32)
        for x in range(X):
            for f in range(NF):
                base = f * F4 + 4 * x
                inside = (lane >= base) & (lane < base + 4)
                slopes = jnp.where(inside, pltpu.roll(inner[f, x], base + 2, 1), slopes)
            inside = (lane >= 4 * x) & (lane < 4 * x + 4)
            pressures = jnp.where(inside, pltpu.roll(press[x], 4 * x + 2, 1), pressures)
        slope_pk[...] = 0.5 * slopes
        press_pk[...] = pressures

    def boundary_z(stage):
        own, low, high = pk[stage], rec_low[stage], rec_high[stage]
        lower, upper = jnp.where(quad < 2, low, own), jnp.where(quad < 2, own, high)
        below2, below, above = (pltpu.roll(lower, k % Z, 1) for k in (2, 1, -1))
        s_low = 0.5 * minmod(below - below2, lower - below)
        s_own = jnp.where(quad == 3, slope_pk[...], 0.5 * minmod(lower - below, above - lower))
        under, over, over2 = (pltpu.roll(upper, k % Z, 1) for k in (1, -1, -2))
        s_up = 0.5 * minmod(over - upper, over2 - over)
        s_top = jnp.where(quad == 0, slope_pk[...], 0.5 * minmod(upper - under, over - upper))
        left = jnp.where(quad < 2, upper + s_top, below + s_low)
        right = jnp.where(quad < 2, over - s_up, lower - s_own)
        opening = jnp.where(
            quad < 2, pltpu.roll(jnp.where(quad == 2, high, own), Z - 1, 1), own
        )
        ls = [pltpu.roll(left, Z - f * F4, 1) if f else left for f in range(NF)]
        rs = [pltpu.roll(right, Z - f * F4, 1) if f else right for f in range(NF)]
        opening = pltpu.roll(opening, Z - NF * F4, 1)
        live = lane < F4
        ls = [jnp.where(live, w, 1.0) for w in ls]
        rs = [jnp.where(live, w, 1.0) for w in rs]
        g = face(ls, rs, 3, 0.5 * opening)
        for f in range(NF):
            before, after = pltpu.roll(g[f], 1, 1), pltpu.roll(g[f], Z - 1, 1)
            change = jnp.where(
                quad == 0, g[f],
                jnp.where(quad == 1, g[f] - before, jnp.where(quad == 2, after - g[f], -g[f])),
            )
            if f == 3:
                change = change - jnp.where(quad == 1, press_pk[...] * opening, 0.0)
            fix[f] = change

    def local_part(x, buf, acc):
        v = [buf[f, x + 2, PAD:PAD + Y, :] for f in range(NF)]
        press[x] = pressure_of(v, 1.0 / v[0])
        for f in range(NF):
            d = v[f] - pltpu.roll(v[f], 1, 1)
            inner[f, x] = minmod(d, pltpu.roll(d, Z - 1, 1))

    def z_part(x, buf, acc):
        v = [buf[f, x + 2, PAD:PAD + Y, :] for f in range(NF)]
        p = press[x]
        a = oz[x]
        sl = [0.5 * inner[f, x] for f in range(NF)]
        left = [pltpu.roll(v[f] + sl[f], 1, 1) for f in range(NF)]
        right = [v[f] - sl[f] for f in range(NF)]
        g = face(left, right, 3, jnp.where((lane >= 2) & (lane < Z - 1), 0.5 * a, 0.0))
        div = [acc[f, x] + (pltpu.roll(g[f], Z - 1, 1) - g[f]) for f in range(NF)]
        div[3] = div[3] - p * (jnp.where(lane == Z - 1, 0.0, pltpu.roll(a, Z - 1, 1)) - a)
        for f in range(NF):
            acc[f, x] = div[f]

    def z_fix(x, buf, acc):
        ends = (lane < 2) | (lane >= Z - 2)
        for f in range(NF):
            acc[f, x] += jnp.where(ends, pltpu.roll(fix[f], Z - (4 * x + 2), 1), 0.0)

    def y_part(x, buf, acc):
        p = press[x]
        E = Y + 8
        left, right, div = [], [], []
        for f in range(NF):
            c = buf[f, x + 2, PAD - 1:PAD - 1 + E, :]
            b = buf[f, x + 2, PAD - 2:PAD - 2 + E, :]
            n = buf[f, x + 2, PAD:PAD + E, :]
            s = 0.5 * minmod(c - b, n - c)
            left.append(c + s)
            right.append(pltpu.roll(c - s, E - 1, 0))
        a = oy[x]
        g = face(left, right, 2, 0.5 * a)
        for f in range(NF):
            div.append(pltpu.roll(g[f], E - 1, 0)[:Y] - g[f][:Y])
        div[2] = div[2] - p * (oy[x, 1:Y + 1, :] - oy[x, 0:Y, :])
        for f in range(NF):
            acc[f, x] = div[f]

    def load(buf, f, x):
        return buf[f, x + 2, PAD:PAD + Y, :]

    def half_slope(buf, x):
        out = []
        for f in range(NF):
            c = load(buf, f, x)
            out.append(0.5 * minmod(c - load(buf, f, x - 1), load(buf, f, x + 1) - c))
        return out

    def x_face(buf, x, s_low, s_high):
        left = [load(buf, f, x - 1) + s_low[f] for f in range(NF)]
        right = [load(buf, f, x) - s_high[f] for f in range(NF)]
        return face(left, right, 1, 0.5 * ox[x])

    def x_inner(buf, acc):
        below = half_slope(buf, 1)
        for f in range(NF):
            edge[0, f] = below[f]
        for x in range(2, X - 1):
            s = half_slope(buf, x)
            g = x_face(buf, x, below, s)
            for f in range(NF):
                acc[f, x - 1] += g[f]
                acc[f, x] -= g[f]
            below = s
        for f in range(NF):
            edge[1, f] = below[f]
        for x in range(X):
            push = press[x] * (ox[x + 1] - ox[x]) if x < X - 1 else -press[x] * ox[x]
            acc[1, x] -= push

    def x_near(buf, acc, side):
        x = X - 1 if side else 0
        s = half_slope(buf, x)
        for f in range(NF):
            outer[side, f] = s[f]
        inner_s = [edge[side, f] for f in range(NF)]
        g = x_face(buf, x, inner_s, s) if side else x_face(buf, 1, s, inner_s)
        for f in range(NF):
            if side:
                acc[f, X - 2] += g[f]
                acc[f, X - 1] -= g[f]
            else:
                acc[f, 1] -= g[f]
                acc[f, 0] += g[f]

    def x_last(buf, side):
        s = [outer[side, f] for f in range(NF)]
        if side:
            return x_face(buf, X, s, half_slope(buf, X))
        return [-v for v in x_face(buf, 0, half_slope(buf, -1), s)]

    def rates_of(total, scales, keeps, gains):
        rates = []
        for f in range(NF):
            moved = jnp.sum(keeps * total[f], axis=1, keepdims=True)
            rates.append(scales * total[f] + gains * moved)
        return rates

    def cell_total(acc, c, g):
        total = [acc[f, c] for f in range(NF)]
        if g is not None:
            total = [t + v for t, v in zip(total, g)]
            if c == X - 1:
                total[1] = total[1] - press[c] * ox[X]
        return total

    def loop(step, buf, acc):
        def body(x, carry):
            step(x, buf, acc)
            return carry

        lax.fori_loop(0, X, body, 0, unroll=True)

    @pl.when(early_up[1] | early_down[1])
    def _():
        pl.semaphore_wait(ready.at[2], jnp.where(early_up[1], 1, 0) + jnp.where(early_down[1], 1, 0))

    send_early_up(1, y_high, None)
    send_early_down(1, y_low, None)
    loop(local_part, buf1, acc1)
    send_early_up(0, near_high, 1)
    send_early_up(2, (zs1[1],), 4)
    settle(recv_sem.at[4], tally.at[pl.ds(0, X * (4 * NF + 1))])
    loop(y_part, buf1, acc1)
    send_early_down(0, near_low, 0)
    send_early_up(0, rest_high, None)
    send_early_down(0, rest_low + volume_low, None)
    send_early_up(0, volume_high, None)
    loop(z_part, buf1, acc1)
    pack_slopes()
    x_inner(buf1, acc1)
    send_early_down(2, (zs1[0],), 3)

    @pl.when(bottom)
    def _():
        settle(recv_sem.at[5], tally.at[pl.ds(0, Y)])

    @pl.when(jnp.logical_not(bottom))
    def _():
        settle(recv_sem.at[5], tally.at[pl.ds(0, 2 * Y)])

    boundary_z(0)
    loop(z_fix, buf1, acc1)

    ys2 = y_copies(buf2, 2, PAD, buf2, 8)
    zs2 = z_copies(1, 9)

    def advance(c, place, rates):
        for f in range(NF):
            now = buf1[f, place, PAD:PAD + Y, :]
            buf2[f, place, PAD:PAD + Y, :] = now + TIME_STEP * rates[f]

    def finish_first(c, g=None):
        rates = rates_of(cell_total(acc1, c, g), scale[c], keep[c], gain[c])
        for f in range(NF):
            first[f, c] = rates[f]
        advance(c, c + 2, rates)

    second = (
        remote(acc1.at[:, pl.ds(0, 1)], part.at[1], 6, down[0]),
        remote(acc1.at[:, pl.ds(X - 1, 1)], part.at[0], 7, up[0]),
        layer(buf2, 1, buf2, X + 3, 6, down[0]),
        layer(buf2, X - 2, buf2, 0, 7, up[0]),
    )
    high_first = late_up[0] & early_down[0]
    near_low[0].wait_recv()
    x_near(buf1, acc1, 1)

    @pl.when(high_first)
    def _():
        second[1].start()

    for c in range(2, X - 1):
        finish_first(c)

    @pl.when(high_first)
    def _():
        second[3].start()

    near_high[0].wait_recv()
    x_near(buf1, acc1, 0)

    low_now = jnp.logical_not(high_first) | top

    @pl.when(low_now)
    def _():
        second[0].start()

    finish_first(1)

    @pl.when(low_now)
    def _():
        second[2].start()

    @pl.when(jnp.logical_not(high_first))
    def _():
        second[1].start()
        second[3].start()

    pack(buf2, 1, range(1, X - 1), jnp.zeros((Y, Z), jnp.float32))
    settle(recv_sem.at[2], tally.at[pl.ds(0, (NF + 1) * Y)])

    @pl.when(high_first & jnp.logical_not(top))
    def _():
        second[0].start()
        second[2].start()

    g = x_last(buf1, 1)
    for f in range(NF):
        face_x[1, f] = -g[f]
    finish_first(X - 1, g)
    settle(recv_sem.at[3], tally.at[pl.ds(0, NF * Y)])
    g = x_last(buf1, 0)
    for f in range(NF):
        face_x[0, f] = -g[f]
    finish_first(0, g)
    for c in ys2:
        c.start()
    pack(buf2, 1, (0, X - 1), pk[1])

    @pl.when(jnp.logical_not(bottom))
    def _():
        zs2[0].start()

    @pl.when(jnp.logical_not(top))
    def _():
        zs2[1].start()

    still_below(1)

    @pl.when(top)
    def _():
        rec_high[1] = rec_high[0]

    loop(local_part, buf2, acc2)
    settle(recv_sem.at[8], tally.at[pl.ds(0, 4 * NF * X)])
    loop(y_part, buf2, acc2)
    loop(z_part, buf2, acc2)
    pack_slopes()
    x_inner(buf2, acc2)
    settle(recv_sem.at[10], tally.at[pl.ds(0, 2 * Y)])
    w = [buf1[f, 1, PAD:PAD + Y, :] for f in range(NF)]
    face_x[0, 1] -= pressure_of(w, 1.0 / w[0]) * ox[0]
    for side in (0, 1):
        v = vol_side[side]
        scale_side[side], keep_side[side], gain_side[side] = factors(v, v <= 0.0, (v > 0.0) & (v < 1.0))

    @pl.when(top | bottom)
    def _():
        settle(recv_sem.at[9], tally.at[pl.ds(0, Y)])

    @pl.when(jnp.logical_not(top | bottom))
    def _():
        settle(recv_sem.at[9], tally.at[pl.ds(0, 2 * Y)])

    boundary_z(1)
    loop(z_fix, buf2, acc2)

    def finish_second(c, g=None):
        rates = rates_of(cell_total(acc2, c, g), scale[c], keep[c], gain[c])
        for f in range(NF):
            out[f, c] = 0.5 * (first[f, c] + rates[f])

    for side in (1, 0):
        settle(recv_sem.at[6 if side else 7], tally.at[pl.ds(0, 2 * NF * Y)])
        total = [part[side, f, 0] + face_x[side, f] for f in range(NF)]
        advance(None, X + 2 if side else 1, rates_of(total, scale_side[side], keep_side[side], gain_side[side]))
        x_near(buf2, acc2, side)
        finish_second(X - 1 if side else 0, x_last(buf2, side))
        for c in range(X // 2, X - 1) if side else range(1, X // 2):
            finish_second(c)

    sent = 8 * NF * Y + 8 * NF * X + 3 * Y + X

    @pl.when(top)
    def _():
        settle(send_sem, tally.at[pl.ds(0, sent + 2 * Y)])

    @pl.when(bottom)
    def _():
        settle(send_sem, tally.at[pl.ds(0, sent + 3 * Y)])

    @pl.when(jnp.logical_not(top | bottom))
    def _():
        settle(send_sem, tally.at[pl.ds(0, sent + 4 * Y)])


def on_device(state, volume, apertures, flags):
    _, X, Y, Z = state.shape
    f32 = jnp.float32
    wide = pltpu.VMEM((NF, X + 4, Y + 2 * PAD, Z), f32)
    cells = pltpu.VMEM((X, Y, Z), f32)
    fields = pltpu.VMEM((NF, X, Y, Z), f32)
    layer = pltpu.VMEM((Y, Z), f32)
    pair = pltpu.VMEM((2, Y, Z), f32)
    sides = pltpu.VMEM((2, NF, Y, Z), f32)
    return pl.pallas_call(
        kernel,
        out_shape=pltpu.VMEM(state.shape, f32),
        in_specs=[pl.BlockSpec(memory_space=pl.ANY)] * 4,
        out_specs=pl.BlockSpec(memory_space=pltpu.VMEM),
        scratch_shapes=[
            wide, wide,
            pltpu.VMEM((X + 1, Y, Z), f32),
            pltpu.VMEM((X, Y + 8, Z), f32),
            cells, cells, pltpu.VMEM((X, Y, Z), jnp.int32),
            pair, pair, pair,
            pltpu.VMEM((NF, Y, Z), f32), layer, layer,
            fields, fields, fields, cells, cells, cells, cells, fields, sides, sides,
            pair, pltpu.VMEM((2, NF, 1, Y, Z), f32), sides, pair, pair, pair,
            pltpu.VMEM((8 * NF * (X + Y) + 16 * Y + 8 * X, Z), f32),
            pltpu.SemaphoreType.DMA,
            pltpu.SemaphoreType.DMA((11,)),
            pltpu.SemaphoreType.REGULAR((5,)),
        ],
        compiler_params=pltpu.CompilerParams(collective_id=0, has_side_effects=True),
    )(state, volume, apertures, flags)


def solution(mesh):
    in_specs = (
        P(None, "gx", "gy", "gz"),
        P("gx", "gy", "gz"),
        P(None, "gx", "gy", "gz"),
        P("gx", "gy", "gz"),
    )
    return jax.shard_map(
        on_device, mesh=mesh, in_specs=in_specs, out_specs=P(None, "gx", "gy", "gz"),
        check_vma=False,
    )
```

```python
import jax
import jax.numpy as jnp
from jax import lax
from jax.experimental import pallas as pl
from jax.experimental.pallas import tpu as pltpu
from jax.sharding import PartitionSpec as P

CUTZ = 32
SOLID = CUTZ // 4
NF = 5
GAMMA_LESS = 0.4
DISSIPATION = 4.0
TIME_STEP = 0.02
VOLUME_FLOOR = 0.5
PAD = 8

MESH = pl.DeviceIdType.MESH


def minmod(a, b):
    return jnp.maximum(jnp.minimum(a, b), 0.0) + jnp.minimum(jnp.maximum(a, b), 0.0)


def pressure_of(w, inverse):
    kinetic = w[1] * w[1] + w[2] * w[2] + w[3] * w[3]
    return GAMMA_LESS * (w[4] - 0.5 * kinetic * inverse)


def flux(w, d):
    inverse = 1.0 / w[0]
    u = w[d] * inverse
    p = pressure_of(w, inverse)
    out = [w[d], w[1] * u, w[2] * u, w[3] * u, (w[4] + p) * u]
    out[d] = out[d] + p
    return out


def face(left, right, d, half_open):
    fl, fr = flux(left, d), flux(right, d)
    return [
        ((fl[f] + fr[f]) + DISSIPATION * (left[f] - right[f])) * half_open for f in range(NF)
    ]


def kernel(
    state, volume, apertures, flags, out,
    buf1, buf2, ox, oy, oz, vol, flg, pk, rec_low, rec_high, fix, slope_pk, press_pk,
    acc1, acc2, first, scale, keep, gain, press, inner, edge, outer,
    near_send, part, face_x, scale_side, keep_side, gain_side, tally,
    send_sem, recv_sem, ready,
):
    _, X, Y, Z = state.shape
    F4 = 4 * X
    me = [lax.axis_index(a) for a in ("gx", "gy", "gz")]
    size = [lax.axis_size(a) for a in ("gx", "gy", "gz")]
    up = [{a: lax.rem(me[i] + 1, size[i])} for i, a in enumerate(("gx", "gy", "gz"))]
    down = [{a: lax.rem(me[i] + size[i] - 1, size[i])} for i, a in enumerate(("gx", "gy", "gz"))]

    rows = pl.ds(PAD, Y)
    def settle(sem, ref):
        pltpu.make_async_copy(ref, ref, sem).wait()

    loads = [
        (state, buf1.at[:, pl.ds(2, X), rows, :]),
        (apertures.at[0], ox.at[pl.ds(0, X)]),
        (apertures.at[1], oy.at[:, pl.ds(0, Y), :]),
        (apertures.at[2], oz),
        (volume, vol),
        (flags, flg),
    ]
    loads = [pltpu.make_async_copy(s, d, send_sem) for s, d in loads]
    for load in loads:
        load.start()

    barrier = pltpu.get_barrier_semaphore()
    n_z = size[2]
    bottom, top = me[2] == 0, me[2] == n_z - 1
    early_up = [me[i] < size[i] // 2 for i in range(2)] + [jnp.logical_not(top)]
    early_down = [(me[i] == 0) | (me[i] > size[i] // 2) for i in range(2)] + [bottom]
    late_up = [jnp.logical_not(e) for e in early_up]
    late_down = [jnp.logical_not(e) for e in early_down]
    late_edges = 0
    for i in range(3):
        @pl.when(early_up[i])
        def _():
            pl.semaphore_signal(barrier, inc=1, device_id=up[i], device_id_type=MESH)

        @pl.when(early_down[i])
        def _():
            pl.semaphore_signal(barrier, inc=1, device_id=down[i], device_id_type=MESH)

        late_edges = late_edges + jnp.where(late_up[i], 1, 0) + jnp.where(late_down[i], 1, 0)

    up_slot, down_slot = (1, 2, 4), (0, 2, 3)

    @pl.when(late_edges > 0)
    def _():
        pl.semaphore_wait(barrier, late_edges)

    for i in range(3):
        @pl.when(late_down[i])
        def _():
            pl.semaphore_signal(ready.at[up_slot[i]], inc=1, device_id=down[i], device_id_type=MESH)

        @pl.when(late_up[i])
        def _():
            pl.semaphore_signal(ready.at[down_slot[i]], inc=1, device_id=up[i], device_id_type=MESH)

    def send_late(i, low, high):
        @pl.when(late_down[i])
        def _():
            for c in low:
                c.start()

        @pl.when(late_up[i])
        def _():
            for c in high:
                c.start()

    def send_early_up(i, high, slot):
        @pl.when(early_up[i])
        def _():
            if slot is not None:
                pl.semaphore_wait(ready.at[slot], 1)
            for c in high:
                c.start()

    def send_early_down(i, low, slot):
        @pl.when(early_down[i])
        def _():
            if slot is not None:
                pl.semaphore_wait(ready.at[slot], 1)
            for c in low:
                c.start()

    def remote(src, dst, recv, target):
        return pltpu.make_async_remote_copy(
            src_ref=src, dst_ref=dst, send_sem=send_sem, recv_sem=recv_sem.at[recv],
            device_id=target, device_id_type=MESH,
        )

    def layer(src, cell, dst, place, recv, target):
        return remote(
            src.at[:, pl.ds(2 + cell, 1), rows, :], dst.at[:, pl.ds(place, 1), rows, :],
            recv, target,
        )

    def y_copies(src, x0, y0, buf, recv):
        mid = pl.ds(x0, X)
        return (
            remote(src.at[:, mid, pl.ds(y0, 2), :],
                   buf.at[:, pl.ds(2, X), pl.ds(PAD + Y, 2), :], recv, down[1]),
            remote(src.at[:, mid, pl.ds(y0 + Y - 2, 2), :],
                   buf.at[:, pl.ds(2, X), pl.ds(PAD - 2, 2), :], recv, up[1]),
        )

    def z_copies(stage, recv):
        return (
            remote(pk.at[stage], rec_high.at[stage], recv, down[2]),
            remote(pk.at[stage], rec_low.at[stage], recv, up[2]),
        )

    near_low = (remote(near_send.at[0], buf1.at[:, pl.ds(X + 2, 1), rows, :], 0, down[0]),)
    near_high = (remote(near_send.at[1], buf1.at[:, pl.ds(1, 1), rows, :], 1, up[0]),)
    rest_low = (
        layer(buf1, 1, buf1, X + 3, 2, down[0]),
        remote(ox.at[pl.ds(0, 1)], ox.at[pl.ds(X, 1)], 2, down[0]),
    )
    rest_high = (layer(buf1, X - 2, buf1, 0, 3, up[0]),)
    ys1 = y_copies(buf1, 2, PAD, buf1, 4)
    ay = remote(oy.at[:, pl.ds(0, 1), :], oy.at[:, pl.ds(Y, 1), :], 4, down[1])
    y_low, y_high = (ay, ys1[0]), (ys1[1],)
    settle(send_sem, tally.at[pl.ds(0, 10 * X * Y)])
    send_late(1, y_low, y_high)
    lane = lax.broadcasted_iota(jnp.int32, (Y, Z), 1)

    for side, c in ((0, 0), (1, X - 1)):
        for f in range(NF):
            value = buf1[f, c + 2, PAD:PAD + Y, :]
            if f in (1, 2):
                value = jnp.where(
                    (lane < SOLID) & bottom, pltpu.roll(vol[c], Z - f * SOLID, 1), value
                )
            near_send[side, f, 0] = value

    def volume_beside(side):
        place = X + 2 if side else 1
        first_part = pltpu.roll(buf1[1, place, PAD:PAD + Y, :], SOLID, 1)
        second_part = pltpu.roll(buf1[2, place, PAD:PAD + Y, :], 2 * SOLID, 1)
        v = jnp.where(lane < 2 * SOLID, first_part, second_part)
        v = jnp.where(lane < SOLID, 0.0, jnp.where(lane < 3 * SOLID, v, 1.0))
        return jnp.where(bottom, v, 1.0)

    send_late(0, near_low, near_high)

    quad = lax.rem(lane, 4)

    def pack(buf, stage, planes, packed):
        for f in range(NF + 1):
            for x in planes:
                base = f * F4 + 4 * x
                value = buf[f, x + 2, PAD:PAD + Y, :] if f < NF else oz[x]
                inside = (lane >= base) & (lane < base + 4)
                packed = jnp.where(inside, pltpu.roll(value, base + 2, 1), packed)
        pk[stage] = packed

    def still_below(stage):
        @pl.when(bottom)
        def _():
            own = pk[stage]
            rec_low[stage] = jnp.where(
                quad == 0, pltpu.roll(own, Z - 2, 1), pltpu.roll(own, Z - 1, 1)
            )

    pack(buf1, 0, range(X), jnp.zeros((Y, Z), jnp.float32))
    zs1 = z_copies(0, 5)

    send_late(2, (zs1[0],), ())
    still_below(0)
    send_late(0, rest_low, rest_high)
    limit = jnp.where(me[2] == 0, CUTZ, 0)

    def factors(v, solid, cut):
        weight = jnp.sum(jnp.where(lane < CUTZ, v, 0.0), axis=1, keepdims=True)
        inverse = jnp.where(solid, 0.0, -1.0 / jnp.maximum(v, VOLUME_FLOOR))
        excess = jnp.where(cut & (lane < limit), 1.0 - v, 0.0)
        return (
            (1.0 - excess) * inverse,
            excess * inverse,
            jnp.where(lane < limit, v / weight, 0.0),
        )

    for x in range(X):
        scale[x], keep[x], gain[x] = factors(vol[x], flg[x] == 2, flg[x] == 1)

    def pack_slopes():
        slopes, pressures = jnp.zeros((Y, Z), jnp.float32), jnp.zeros((Y, Z), jnp.float32)
        for x in range(X):
            for f in range(NF):
                base = f * F4 + 4 * x
                inside = (lane >= base) & (lane < base + 4)
                slopes = jnp.where(inside, pltpu.roll(inner[f, x], base + 2, 1), slopes)
            inside = (lane >= 4 * x) & (lane < 4 * x + 4)
            pressures = jnp.where(inside, pltpu.roll(press[x], 4 * x + 2, 1), pressures)
        slope_pk[...] = 0.5 * slopes
        press_pk[...] = pressures

    def boundary_z(stage):
        own, low, high = pk[stage], rec_low[stage], rec_high[stage]
        lower, upper = jnp.where(quad < 2, low, own), jnp.where(quad < 2, own, high)
        below2, below, above = (pltpu.roll(lower, k % Z, 1) for k in (2, 1, -1))
        s_low = 0.5 * minmod(below - below2, lower - below)
        s_own = jnp.where(quad == 3, slope_pk[...], 0.5 * minmod(lower - below, above - lower))
        under, over, over2 = (pltpu.roll(upper, k % Z, 1) for k in (1, -1, -2))
        s_up = 0.5 * minmod(over - upper, over2 - over)
        s_top = jnp.where(quad == 0, slope_pk[...], 0.5 * minmod(upper - under, over - upper))
        left = jnp.where(quad < 2, upper + s_top, below + s_low)
        right = jnp.where(quad < 2, over - s_up, lower - s_own)
        opening = jnp.where(
            quad < 2, pltpu.roll(jnp.where(quad == 2, high, own), Z - 1, 1), own
        )
        ls = [pltpu.roll(left, Z - f * F4, 1) if f else left for f in range(NF)]
        rs = [pltpu.roll(right, Z - f * F4, 1) if f else right for f in range(NF)]
        opening = pltpu.roll(opening, Z - NF * F4, 1)
        live = lane < F4
        ls = [jnp.where(live, w, 1.0) for w in ls]
        rs = [jnp.where(live, w, 1.0) for w in rs]
        g = face(ls, rs, 3, 0.5 * opening)
        for f in range(NF):
            before, after = pltpu.roll(g[f], 1, 1), pltpu.roll(g[f], Z - 1, 1)
            change = jnp.where(
                quad == 0, g[f],
                jnp.where(quad == 1, g[f] - before, jnp.where(quad == 2, after - g[f], -g[f])),
            )
            if f == 3:
                change = change - jnp.where(quad == 1, press_pk[...] * opening, 0.0)
            fix[f] = change

    def local_part(x, buf, acc):
        v = [buf[f, x + 2, PAD:PAD + Y, :] for f in range(NF)]
        press[x] = pressure_of(v, 1.0 / v[0])
        for f in range(NF):
            d = v[f] - pltpu.roll(v[f], 1, 1)
            inner[f, x] = minmod(d, pltpu.roll(d, Z - 1, 1))

    def z_part(x, buf, acc):
        v = [buf[f, x + 2, PAD:PAD + Y, :] for f in range(NF)]
        p = press[x]
        a = oz[x]
        sl = [0.5 * inner[f, x] for f in range(NF)]
        left = [pltpu.roll(v[f] + sl[f], 1, 1) for f in range(NF)]
        right = [v[f] - sl[f] for f in range(NF)]
        g = face(left, right, 3, jnp.where((lane >= 2) & (lane < Z - 1), 0.5 * a, 0.0))
        div = [acc[f, x] + (pltpu.roll(g[f], Z - 1, 1) - g[f]) for f in range(NF)]
        div[3] = div[3] - p * (jnp.where(lane == Z - 1, 0.0, pltpu.roll(a, Z - 1, 1)) - a)
        for f in range(NF):
            acc[f, x] = div[f]

    def z_fix(x, buf, acc):
        ends = (lane < 2) | (lane >= Z - 2)
        for f in range(NF):
            acc[f, x] += jnp.where(ends, pltpu.roll(fix[f], Z - (4 * x + 2), 1), 0.0)

    def y_part(x, buf, acc):
        p = press[x]
        E = Y + 8
        left, right, div = [], [], []
        for f in range(NF):
            c = buf[f, x + 2, PAD - 1:PAD - 1 + E, :]
            b = buf[f, x + 2, PAD - 2:PAD - 2 + E, :]
            n = buf[f, x + 2, PAD:PAD + E, :]
            s = 0.5 * minmod(c - b, n - c)
            left.append(c + s)
            right.append(pltpu.roll(c - s, E - 1, 0))
        a = oy[x]
        g = face(left, right, 2, 0.5 * a)
        for f in range(NF):
            div.append(pltpu.roll(g[f], E - 1, 0)[:Y] - g[f][:Y])
        div[2] = div[2] - p * (oy[x, 1:Y + 1, :] - oy[x, 0:Y, :])
        for f in range(NF):
            acc[f, x] = div[f]

    def load(buf, f, x):
        return buf[f, x + 2, PAD:PAD + Y, :]

    def half_slope(buf, x):
        out = []
        for f in range(NF):
            c = load(buf, f, x)
            out.append(0.5 * minmod(c - load(buf, f, x - 1), load(buf, f, x + 1) - c))
        return out

    def x_face(buf, x, s_low, s_high):
        left = [load(buf, f, x - 1) + s_low[f] for f in range(NF)]
        right = [load(buf, f, x) - s_high[f] for f in range(NF)]
        return face(left, right, 1, 0.5 * ox[x])

    def x_inner(buf, acc):
        below = half_slope(buf, 1)
        for f in range(NF):
            edge[0, f] = below[f]
        for x in range(2, X - 1):
            s = half_slope(buf, x)
            g = x_face(buf, x, below, s)
            for f in range(NF):
                acc[f, x - 1] += g[f]
                acc[f, x] -= g[f]
            below = s
        for f in range(NF):
            edge[1, f] = below[f]
        for x in range(X):
            push = press[x] * (ox[x + 1] - ox[x]) if x < X - 1 else -press[x] * ox[x]
            acc[1, x] -= push

    def x_near(buf, acc, side):
        x = X - 1 if side else 0
        s = half_slope(buf, x)
        for f in range(NF):
            outer[side, f] = s[f]
        inner_s = [edge[side, f] for f in range(NF)]
        g = x_face(buf, x, inner_s, s) if side else x_face(buf, 1, s, inner_s)
        for f in range(NF):
            if side:
                acc[f, X - 2] += g[f]
                acc[f, X - 1] -= g[f]
            else:
                acc[f, 1] -= g[f]
                acc[f, 0] += g[f]

    def x_last(buf, side):
        s = [outer[side, f] for f in range(NF)]
        if side:
            return x_face(buf, X, s, half_slope(buf, X))
        return [-v for v in x_face(buf, 0, half_slope(buf, -1), s)]

    def rates_of(total, scales, keeps, gains):
        rates = []
        for f in range(NF):
            moved = jnp.sum(keeps * total[f], axis=1, keepdims=True)
            rates.append(scales * total[f] + gains * moved)
        return rates

    def cell_total(acc, c, g):
        total = [acc[f, c] for f in range(NF)]
        if g is not None:
            total = [t + v for t, v in zip(total, g)]
            if c == X - 1:
                total[1] = total[1] - press[c] * ox[X]
        return total

    def loop(step, buf, acc):
        def body(x, carry):
            step(x, buf, acc)
            return carry

        lax.fori_loop(0, X, body, 0, unroll=True)

    @pl.when(early_up[1] | early_down[1])
    def _():
        pl.semaphore_wait(ready.at[2], jnp.where(early_up[1], 1, 0) + jnp.where(early_down[1], 1, 0))

    send_early_up(1, y_high, None)
    send_early_down(1, y_low, None)
    loop(local_part, buf1, acc1)
    send_early_up(0, near_high, 1)
    send_early_up(2, (zs1[1],), 4)
    settle(recv_sem.at[4], tally.at[pl.ds(0, X * (4 * NF + 1))])
    loop(y_part, buf1, acc1)
    send_early_down(0, near_low, 0)
    send_early_up(0, rest_high, None)
    send_early_down(0, rest_low, None)
    loop(z_part, buf1, acc1)
    pack_slopes()
    x_inner(buf1, acc1)
    send_early_down(2, (zs1[0],), 3)

    @pl.when(bottom)
    def _():
        settle(recv_sem.at[5], tally.at[pl.ds(0, Y)])

    @pl.when(jnp.logical_not(bottom))
    def _():
        settle(recv_sem.at[5], tally.at[pl.ds(0, 2 * Y)])

    boundary_z(0)
    loop(z_fix, buf1, acc1)

    ys2 = y_copies(buf2, 2, PAD, buf2, 8)
    zs2 = z_copies(1, 9)

    def advance(place, rates):
        for f in range(NF):
            now = buf1[f, place, PAD:PAD + Y, :]
            buf2[f, place, PAD:PAD + Y, :] = now + TIME_STEP * rates[f]

    def finish_first(c, g=None):
        rates = rates_of(cell_total(acc1, c, g), scale[c], keep[c], gain[c])
        for f in range(NF):
            first[f, c] = rates[f]
        advance(c + 2, rates)

    second = (
        remote(acc1.at[:, pl.ds(0, 1)], part.at[1], 6, down[0]),
        remote(acc1.at[:, pl.ds(X - 1, 1)], part.at[0], 7, up[0]),
        layer(buf2, 1, buf2, X + 3, 6, down[0]),
        layer(buf2, X - 2, buf2, 0, 7, up[0]),
    )
    high_first = late_up[0] & early_down[0]
    later_low = high_first & bottom

    def upper_steps():
        near_low[0].wait_recv()
        x_near(buf1, acc1, 1)
        second[1].start()
        for c in range(2, X - 1):
            finish_first(c)
        second[3].start()

    def lower_steps():
        near_high[0].wait_recv()
        x_near(buf1, acc1, 0)

        @pl.when(jnp.logical_not(later_low))
        def _():
            second[0].start()

        finish_first(1)

        @pl.when(jnp.logical_not(later_low))
        def _():
            second[2].start()

    @pl.when(early_down[0])
    def _():
        upper_steps()

    lower_steps()

    @pl.when(late_down[0])
    def _():
        upper_steps()

    pack(buf2, 1, range(1, X - 1), jnp.zeros((Y, Z), jnp.float32))
    settle(recv_sem.at[2], tally.at[pl.ds(0, (NF + 1) * Y)])

    @pl.when(later_low & (lax.rem(me[1], 2) == 0))
    def _():
        second[0].start()
        second[2].start()

    g = x_last(buf1, 1)
    for f in range(NF):
        face_x[1, f] = -g[f]
    finish_first(X - 1, g)
    settle(recv_sem.at[3], tally.at[pl.ds(0, NF * Y)])
    g = x_last(buf1, 0)
    for f in range(NF):
        face_x[0, f] = -g[f]
    finish_first(0, g)
    for c in ys2:
        c.start()
    pack(buf2, 1, (0, X - 1), pk[1])

    @pl.when(jnp.logical_not(bottom))
    def _():
        zs2[0].start()

    @pl.when(jnp.logical_not(top))
    def _():
        zs2[1].start()

    still_below(1)

    @pl.when(top)
    def _():
        rec_high[1] = rec_high[0]

    loop(local_part, buf2, acc2)
    @pl.when(later_low & (lax.rem(me[1], 2) == 1))
    def _():
        second[0].start()
        second[2].start()

    settle(recv_sem.at[8], tally.at[pl.ds(0, 4 * NF * X)])
    loop(y_part, buf2, acc2)
    loop(z_part, buf2, acc2)
    pack_slopes()
    x_inner(buf2, acc2)
    w = [buf1[f, 1, PAD:PAD + Y, :] for f in range(NF)]
    face_x[0, 1] -= pressure_of(w, 1.0 / w[0]) * ox[0]
    for side in (0, 1):
        v = volume_beside(side)
        scale_side[side], keep_side[side], gain_side[side] = factors(v, v <= 0.0, (v > 0.0) & (v < 1.0))

    def z_ends():
        @pl.when(top | bottom)
        def _():
            settle(recv_sem.at[9], tally.at[pl.ds(0, Y)])

        @pl.when(jnp.logical_not(top | bottom))
        def _():
            settle(recv_sem.at[9], tally.at[pl.ds(0, 2 * Y)])

        boundary_z(1)
        loop(z_fix, buf2, acc2)

    def finish_second(cells):
        for c in cells:
            rates = rates_of([acc2[f, c] for f in range(NF)], scale[c], keep[c], gain[c])
            for f in range(NF):
                out[f, c] = 0.5 * (first[f, c] + rates[f])

    def x_side(side):
        settle(recv_sem.at[6 if side else 7], tally.at[pl.ds(0, 2 * NF * Y)])
        total = [part[side, f, 0] + face_x[side, f] for f in range(NF)]
        advance(X + 2 if side else 1, rates_of(total, scale_side[side], keep_side[side], gain_side[side]))
        x_near(buf2, acc2, side)
        c = X - 1 if side else 0
        total = cell_total(acc2, c, x_last(buf2, side))
        for f in range(NF):
            acc2[f, c] = total[f]

    z_first = top | jnp.logical_not(high_first | (late_up[0] & late_down[0] & jnp.logical_not(bottom)))
    upper_cells, lower_cells = range(X - 1, X // 2 - 1, -1), range(X // 2)

    @pl.when(z_first)
    def _():
        z_ends()

    x_side(1)

    @pl.when(z_first)
    def _():
        finish_second(upper_cells)

    x_side(0)

    @pl.when(jnp.logical_not(z_first))
    def _():
        z_ends()
        finish_second(upper_cells)

    finish_second(lower_cells)

    sent = 8 * NF * Y + 8 * NF * X + Y + X

    @pl.when(top)
    def _():
        settle(send_sem, tally.at[pl.ds(0, sent + 2 * Y)])

    @pl.when(bottom)
    def _():
        settle(send_sem, tally.at[pl.ds(0, sent + 3 * Y)])

    @pl.when(jnp.logical_not(top | bottom))
    def _():
        settle(send_sem, tally.at[pl.ds(0, sent + 4 * Y)])


def on_device(state, volume, apertures, flags):
    _, X, Y, Z = state.shape
    f32 = jnp.float32
    wide = pltpu.VMEM((NF, X + 4, Y + 2 * PAD, Z), f32)
    cells = pltpu.VMEM((X, Y, Z), f32)
    fields = pltpu.VMEM((NF, X, Y, Z), f32)
    layer = pltpu.VMEM((Y, Z), f32)
    pair = pltpu.VMEM((2, Y, Z), f32)
    sides = pltpu.VMEM((2, NF, Y, Z), f32)
    return pl.pallas_call(
        kernel,
        out_shape=pltpu.VMEM(state.shape, f32),
        in_specs=[pl.BlockSpec(memory_space=pl.ANY)] * 4,
        out_specs=pl.BlockSpec(memory_space=pltpu.VMEM),
        scratch_shapes=[
            wide, wide,
            pltpu.VMEM((X + 1, Y, Z), f32),
            pltpu.VMEM((X, Y + 8, Z), f32),
            cells, cells, pltpu.VMEM((X, Y, Z), jnp.int32),
            pair, pair, pair,
            pltpu.VMEM((NF, Y, Z), f32), layer, layer,
            fields, fields, fields, cells, cells, cells, cells, fields, sides, sides,
            pltpu.VMEM((2, NF, 1, Y, Z), f32), pltpu.VMEM((2, NF, 1, Y, Z), f32), sides, pair, pair, pair,
            pltpu.VMEM((8 * NF * (X + Y) + 16 * Y + 8 * X, Z), f32),
            pltpu.SemaphoreType.DMA,
            pltpu.SemaphoreType.DMA((10,)),
            pltpu.SemaphoreType.REGULAR((5,)),
        ],
        compiler_params=pltpu.CompilerParams(collective_id=0, has_side_effects=True),
    )(state, volume, apertures, flags)


def solution(mesh):
    in_specs = (
        P(None, "gx", "gy", "gz"),
        P("gx", "gy", "gz"),
        P(None, "gx", "gy", "gz"),
        P("gx", "gy", "gz"),
    )
    return jax.shard_map(
        on_device, mesh=mesh, in_specs=in_specs, out_specs=P(None, "gx", "gy", "gz"),
        check_vma=False,
    )
```

```python
import jax
import jax.numpy as jnp
from jax import lax
from jax.experimental import pallas as pl
from jax.experimental.pallas import tpu as pltpu
from jax.sharding import PartitionSpec as P

CUTZ = 32
SOLID = CUTZ // 4
NF = 5
GAMMA_LESS = 0.4
DISSIPATION = 4.0
TIME_STEP = 0.02
VOLUME_FLOOR = 0.5
PAD = 8

MESH = pl.DeviceIdType.MESH


def minmod(a, b):
    return jnp.maximum(jnp.minimum(a, b), 0.0) + jnp.minimum(jnp.maximum(a, b), 0.0)


def pressure_of(w, inverse):
    kinetic = w[1] * w[1] + w[2] * w[2] + w[3] * w[3]
    return GAMMA_LESS * (w[4] - 0.5 * kinetic * inverse)


def flux(w, d):
    inverse = 1.0 / w[0]
    u = w[d] * inverse
    p = pressure_of(w, inverse)
    out = [w[d], w[1] * u, w[2] * u, w[3] * u, (w[4] + p) * u]
    out[d] = out[d] + p
    return out


def face(left, right, d, half_open):
    fl, fr = flux(left, d), flux(right, d)
    return [
        ((fl[f] + fr[f]) + DISSIPATION * (left[f] - right[f])) * half_open for f in range(NF)
    ]


def kernel(
    state, volume, apertures, flags, out,
    buf1, buf2, ox, oy, oz, vol, flg, pk, rec_low, rec_high, fix, slope_pk, press_pk,
    acc1, acc2, first, scale, keep, gain, press, inner, edge, outer,
    near_send, part, face_x, scale_side, keep_side, gain_side, tally,
    send_sem, recv_sem, ready,
):
    _, X, Y, Z = state.shape
    F4 = 4 * X
    me = [lax.axis_index(a) for a in ("gx", "gy", "gz")]
    size = [lax.axis_size(a) for a in ("gx", "gy", "gz")]
    up = [{a: lax.rem(me[i] + 1, size[i])} for i, a in enumerate(("gx", "gy", "gz"))]
    down = [{a: lax.rem(me[i] + size[i] - 1, size[i])} for i, a in enumerate(("gx", "gy", "gz"))]

    rows = pl.ds(PAD, Y)
    def settle(sem, ref):
        pltpu.make_async_copy(ref, ref, sem).wait()

    loads = [
        (state, buf1.at[:, pl.ds(2, X), rows, :]),
        (apertures.at[0], ox.at[pl.ds(0, X)]),
        (apertures.at[1], oy.at[:, pl.ds(0, Y), :]),
        (apertures.at[2], oz),
        (volume, vol),
        (flags, flg),
    ]
    loads = [pltpu.make_async_copy(s, d, send_sem) for s, d in loads]
    for load in loads:
        load.start()

    barrier = pltpu.get_barrier_semaphore()
    n_z = size[2]
    bottom, top = me[2] == 0, me[2] == n_z - 1
    early_up = [me[i] < size[i] // 2 for i in range(2)] + [jnp.logical_not(top)]
    early_down = [(me[i] == 0) | (me[i] > size[i] // 2) for i in range(2)] + [bottom]
    late_up = [jnp.logical_not(e) for e in early_up]
    late_down = [jnp.logical_not(e) for e in early_down]
    late_edges = 0
    for i in range(3):
        @pl.when(early_up[i])
        def _():
            pl.semaphore_signal(barrier, inc=1, device_id=up[i], device_id_type=MESH)

        @pl.when(early_down[i])
        def _():
            pl.semaphore_signal(barrier, inc=1, device_id=down[i], device_id_type=MESH)

        late_edges = late_edges + jnp.where(late_up[i], 1, 0) + jnp.where(late_down[i], 1, 0)

    up_slot, down_slot = (1, 2, 4), (0, 2, 3)

    @pl.when(late_edges > 0)
    def _():
        pl.semaphore_wait(barrier, late_edges)

    for i in range(3):
        @pl.when(late_down[i])
        def _():
            pl.semaphore_signal(ready.at[up_slot[i]], inc=1, device_id=down[i], device_id_type=MESH)

        @pl.when(late_up[i])
        def _():
            pl.semaphore_signal(ready.at[down_slot[i]], inc=1, device_id=up[i], device_id_type=MESH)

    def send_late(i, low, high):
        @pl.when(late_down[i])
        def _():
            for c in low:
                c.start()

        @pl.when(late_up[i])
        def _():
            for c in high:
                c.start()

    def send_early_up(i, high, slot):
        @pl.when(early_up[i])
        def _():
            if slot is not None:
                pl.semaphore_wait(ready.at[slot], 1)
            for c in high:
                c.start()

    def send_early_down(i, low, slot):
        @pl.when(early_down[i])
        def _():
            if slot is not None:
                pl.semaphore_wait(ready.at[slot], 1)
            for c in low:
                c.start()

    def remote(src, dst, recv, target):
        return pltpu.make_async_remote_copy(
            src_ref=src, dst_ref=dst, send_sem=send_sem, recv_sem=recv_sem.at[recv],
            device_id=target, device_id_type=MESH,
        )

    def layer(src, cell, dst, place, recv, target):
        return remote(
            src.at[:, pl.ds(2 + cell, 1), rows, :], dst.at[:, pl.ds(place, 1), rows, :],
            recv, target,
        )

    def y_copies(src, x0, y0, buf, recv):
        mid = pl.ds(x0, X)
        return (
            remote(src.at[:, mid, pl.ds(y0, 2), :],
                   buf.at[:, pl.ds(2, X), pl.ds(PAD + Y, 2), :], recv, down[1]),
            remote(src.at[:, mid, pl.ds(y0 + Y - 2, 2), :],
                   buf.at[:, pl.ds(2, X), pl.ds(PAD - 2, 2), :], recv, up[1]),
        )

    def z_copies(stage, recv):
        return (
            remote(pk.at[stage], rec_high.at[stage], recv, down[2]),
            remote(pk.at[stage], rec_low.at[stage], recv, up[2]),
        )

    near_low = (remote(near_send.at[0], buf1.at[:, pl.ds(X + 2, 1), rows, :], 0, down[0]),)
    near_high = (remote(near_send.at[1], buf1.at[:, pl.ds(1, 1), rows, :], 1, up[0]),)
    rest_low = (
        layer(buf1, 1, buf1, X + 3, 2, down[0]),
        remote(ox.at[pl.ds(0, 1)], ox.at[pl.ds(X, 1)], 2, down[0]),
    )
    rest_high = (layer(buf1, X - 2, buf1, 0, 3, up[0]),)
    ys1 = y_copies(buf1, 2, PAD, buf1, 4)
    ay = remote(oy.at[:, pl.ds(0, 1), :], oy.at[:, pl.ds(Y, 1), :], 4, down[1])
    y_low, y_high = (ay, ys1[0]), (ys1[1],)
    settle(send_sem, tally.at[pl.ds(0, 10 * X * Y)])
    send_late(1, y_low, y_high)
    lane = lax.broadcasted_iota(jnp.int32, (Y, Z), 1)

    for side, c in ((0, 0), (1, X - 1)):
        for f in range(NF):
            value = buf1[f, c + 2, PAD:PAD + Y, :]
            if f in (1, 2):
                value = jnp.where(
                    (lane < SOLID) & bottom, pltpu.roll(vol[c], Z - f * SOLID, 1), value
                )
            near_send[side, f, 0] = value

    def volume_beside(side):
        place = X + 2 if side else 1
        first_part = pltpu.roll(buf1[1, place, PAD:PAD + Y, :], SOLID, 1)
        second_part = pltpu.roll(buf1[2, place, PAD:PAD + Y, :], 2 * SOLID, 1)
        v = jnp.where(lane < 2 * SOLID, first_part, second_part)
        v = jnp.where(lane < SOLID, 0.0, jnp.where(lane < 3 * SOLID, v, 1.0))
        return jnp.where(bottom, v, 1.0)

    send_late(0, near_low, near_high)

    quad = lax.rem(lane, 4)

    def pack(buf, stage, planes, packed):
        for f in range(NF + 1):
            for x in planes:
                base = f * F4 + 4 * x
                value = buf[f, x + 2, PAD:PAD + Y, :] if f < NF else oz[x]
                inside = (lane >= base) & (lane < base + 4)
                packed = jnp.where(inside, pltpu.roll(value, base + 2, 1), packed)
        pk[stage] = packed

    def still_below(stage):
        @pl.when(bottom)
        def _():
            own = pk[stage]
            rec_low[stage] = jnp.where(
                quad == 0, pltpu.roll(own, Z - 2, 1), pltpu.roll(own, Z - 1, 1)
            )

    pack(buf1, 0, range(X), jnp.zeros((Y, Z), jnp.float32))
    zs1 = z_copies(0, 5)

    send_late(2, (zs1[0],), ())
    still_below(0)
    send_late(0, rest_low, rest_high)
    limit = jnp.where(me[2] == 0, CUTZ, 0)

    def factors(v, solid, cut):
        weight = jnp.sum(jnp.where(lane < CUTZ, v, 0.0), axis=1, keepdims=True)
        inverse = jnp.where(solid, 0.0, -1.0 / jnp.maximum(v, VOLUME_FLOOR))
        excess = jnp.where(cut & (lane < limit), 1.0 - v, 0.0)
        return (
            (1.0 - excess) * inverse,
            excess * inverse,
            jnp.where(lane < limit, v / weight, 0.0),
        )

    for x in range(X):
        scale[x], keep[x], gain[x] = factors(vol[x], flg[x] == 2, flg[x] == 1)

    def pack_slopes():
        slopes, pressures = jnp.zeros((Y, Z), jnp.float32), jnp.zeros((Y, Z), jnp.float32)
        for x in range(X):
            for f in range(NF):
                base = f * F4 + 4 * x
                inside = (lane >= base) & (lane < base + 4)
                slopes = jnp.where(inside, pltpu.roll(inner[f, x], base + 2, 1), slopes)
            inside = (lane >= 4 * x) & (lane < 4 * x + 4)
            pressures = jnp.where(inside, pltpu.roll(press[x], 4 * x + 2, 1), pressures)
        slope_pk[...] = 0.5 * slopes
        press_pk[...] = pressures

    def boundary_z(stage):
        own, low, high = pk[stage], rec_low[stage], rec_high[stage]
        lower, upper = jnp.where(quad < 2, low, own), jnp.where(quad < 2, own, high)
        below2, below, above = (pltpu.roll(lower, k % Z, 1) for k in (2, 1, -1))
        s_low = 0.5 * minmod(below - below2, lower - below)
        s_own = jnp.where(quad == 3, slope_pk[...], 0.5 * minmod(lower - below, above - lower))
        under, over, over2 = (pltpu.roll(upper, k % Z, 1) for k in (1, -1, -2))
        s_up = 0.5 * minmod(over - upper, over2 - over)
        s_top = jnp.where(quad == 0, slope_pk[...], 0.5 * minmod(upper - under, over - upper))
        left = jnp.where(quad < 2, upper + s_top, below + s_low)
        right = jnp.where(quad < 2, over - s_up, lower - s_own)
        opening = jnp.where(
            quad < 2, pltpu.roll(jnp.where(quad == 2, high, own), Z - 1, 1), own
        )
        ls = [pltpu.roll(left, Z - f * F4, 1) if f else left for f in range(NF)]
        rs = [pltpu.roll(right, Z - f * F4, 1) if f else right for f in range(NF)]
        opening = pltpu.roll(opening, Z - NF * F4, 1)
        live = lane < F4
        ls = [jnp.where(live, w, 1.0) for w in ls]
        rs = [jnp.where(live, w, 1.0) for w in rs]
        g = face(ls, rs, 3, 0.5 * opening)
        for f in range(NF):
            before, after = pltpu.roll(g[f], 1, 1), pltpu.roll(g[f], Z - 1, 1)
            change = jnp.where(
                quad == 0, g[f],
                jnp.where(quad == 1, g[f] - before, jnp.where(quad == 2, after - g[f], -g[f])),
            )
            if f == 3:
                change = change - jnp.where(quad == 1, press_pk[...] * opening, 0.0)
            fix[f] = change

    def local_part(x, buf, acc):
        v = [buf[f, x + 2, PAD:PAD + Y, :] for f in range(NF)]
        press[x] = pressure_of(v, 1.0 / v[0])
        for f in range(NF):
            d = v[f] - pltpu.roll(v[f], 1, 1)
            inner[f, x] = minmod(d, pltpu.roll(d, Z - 1, 1))

    def z_part(x, buf, acc):
        v = [buf[f, x + 2, PAD:PAD + Y, :] for f in range(NF)]
        p = press[x]
        a = oz[x]
        sl = [0.5 * inner[f, x] for f in range(NF)]
        left = [pltpu.roll(v[f] + sl[f], 1, 1) for f in range(NF)]
        right = [v[f] - sl[f] for f in range(NF)]
        g = face(left, right, 3, jnp.where((lane >= 2) & (lane < Z - 1), 0.5 * a, 0.0))
        div = [acc[f, x] + (pltpu.roll(g[f], Z - 1, 1) - g[f]) for f in range(NF)]
        div[3] = div[3] - p * (jnp.where(lane == Z - 1, 0.0, pltpu.roll(a, Z - 1, 1)) - a)
        for f in range(NF):
            acc[f, x] = div[f]

    def z_fix(x, buf, acc):
        ends = (lane < 2) | (lane >= Z - 2)
        for f in range(NF):
            acc[f, x] += jnp.where(ends, pltpu.roll(fix[f], Z - (4 * x + 2), 1), 0.0)

    def y_part(x, buf, acc):
        p = press[x]
        E = Y + 8
        left, right, div = [], [], []
        for f in range(NF):
            c = buf[f, x + 2, PAD - 1:PAD - 1 + E, :]
            b = buf[f, x + 2, PAD - 2:PAD - 2 + E, :]
            n = buf[f, x + 2, PAD:PAD + E, :]
            s = 0.5 * minmod(c - b, n - c)
            left.append(c + s)
            right.append(pltpu.roll(c - s, E - 1, 0))
        a = oy[x]
        g = face(left, right, 2, 0.5 * a)
        for f in range(NF):
            div.append(pltpu.roll(g[f], E - 1, 0)[:Y] - g[f][:Y])
        div[2] = div[2] - p * (oy[x, 1:Y + 1, :] - oy[x, 0:Y, :])
        for f in range(NF):
            acc[f, x] = div[f]

    def load(buf, f, x):
        return buf[f, x + 2, PAD:PAD + Y, :]

    def half_slope(buf, x):
        out = []
        for f in range(NF):
            c = load(buf, f, x)
            out.append(0.5 * minmod(c - load(buf, f, x - 1), load(buf, f, x + 1) - c))
        return out

    def x_face(buf, x, s_low, s_high):
        left = [load(buf, f, x - 1) + s_low[f] for f in range(NF)]
        right = [load(buf, f, x) - s_high[f] for f in range(NF)]
        return face(left, right, 1, 0.5 * ox[x])

    def x_inner(buf, acc):
        below = half_slope(buf, 1)
        for f in range(NF):
            edge[0, f] = below[f]
        for x in range(2, X - 1):
            s = half_slope(buf, x)
            g = x_face(buf, x, below, s)
            for f in range(NF):
                acc[f, x - 1] += g[f]
                acc[f, x] -= g[f]
            below = s
        for f in range(NF):
            edge[1, f] = below[f]
        for x in range(X):
            push = press[x] * (ox[x + 1] - ox[x]) if x < X - 1 else -press[x] * ox[x]
            acc[1, x] -= push

    def x_near(buf, acc, side):
        x = X - 1 if side else 0
        s = half_slope(buf, x)
        for f in range(NF):
            outer[side, f] = s[f]
        inner_s = [edge[side, f] for f in range(NF)]
        g = x_face(buf, x, inner_s, s) if side else x_face(buf, 1, s, inner_s)
        for f in range(NF):
            if side:
                acc[f, X - 2] += g[f]
                acc[f, X - 1] -= g[f]
            else:
                acc[f, 1] -= g[f]
                acc[f, 0] += g[f]

    def x_last(buf, side):
        s = [outer[side, f] for f in range(NF)]
        if side:
            return x_face(buf, X, s, half_slope(buf, X))
        return [-v for v in x_face(buf, 0, half_slope(buf, -1), s)]

    def spread(cells, finish):
        @pl.when(bottom)
        def _():
            with_cut(cells, finish)

        @pl.when(jnp.logical_not(bottom))
        def _():
            for k, (total, scales, _, _) in enumerate(cells):
                finish(k, [scales * t for t in total])

    def with_cut(cells, finish):
        for k, (total, scales, keeps, gains) in enumerate(cells):
            moved = [jnp.sum(keeps * t, axis=1, keepdims=True) for t in total]
            finish(k, [scales * total[f] + gains * moved[f] for f in range(NF)])

    def cell_total(acc, c, g):
        total = [acc[f, c] for f in range(NF)]
        if g is not None:
            total = [t + v for t, v in zip(total, g)]
            if c == X - 1:
                total[1] = total[1] - press[c] * ox[X]
        return total

    def loop(step, buf, acc):
        def body(x, carry):
            step(x, buf, acc)
            return carry

        lax.fori_loop(0, X, body, 0, unroll=True)

    @pl.when(early_up[1] | early_down[1])
    def _():
        pl.semaphore_wait(ready.at[2], jnp.where(early_up[1], 1, 0) + jnp.where(early_down[1], 1, 0))

    send_early_up(1, y_high, None)
    send_early_down(1, y_low, None)
    loop(local_part, buf1, acc1)
    send_early_up(0, near_high, 1)
    send_early_up(2, (zs1[1],), 4)
    settle(recv_sem.at[4], tally.at[pl.ds(0, X * (4 * NF + 1))])
    loop(y_part, buf1, acc1)
    send_early_down(0, near_low, 0)
    send_early_up(0, rest_high, None)
    send_early_down(0, rest_low, None)
    loop(z_part, buf1, acc1)
    pack_slopes()
    x_inner(buf1, acc1)
    send_early_down(2, (zs1[0],), 3)

    @pl.when(bottom)
    def _():
        settle(recv_sem.at[5], tally.at[pl.ds(0, Y)])

    @pl.when(jnp.logical_not(bottom))
    def _():
        settle(recv_sem.at[5], tally.at[pl.ds(0, 2 * Y)])

    boundary_z(0)
    loop(z_fix, buf1, acc1)

    ys2 = y_copies(buf2, 2, PAD, buf2, 8)
    zs2 = z_copies(1, 9)

    def advance(place, rates):
        for f in range(NF):
            now = buf1[f, place, PAD:PAD + Y, :]
            buf2[f, place, PAD:PAD + Y, :] = now + TIME_STEP * rates[f]

    def finish_first(c, g=None):
        def finish(_, rates):
            for f in range(NF):
                first[f, c] = rates[f]
            advance(c + 2, rates)

        spread([(cell_total(acc1, c, g), scale[c], keep[c], gain[c])], finish)

    second = (
        remote(acc1.at[:, pl.ds(0, 1)], part.at[1], 6, down[0]),
        remote(acc1.at[:, pl.ds(X - 1, 1)], part.at[0], 7, up[0]),
        layer(buf2, 1, buf2, X + 3, 6, down[0]),
        layer(buf2, X - 2, buf2, 0, 7, up[0]),
    )
    high_first = late_up[0] & early_down[0]
    later_low = high_first & bottom

    def upper_steps():
        near_low[0].wait_recv()
        x_near(buf1, acc1, 1)
        second[1].start()
        for c in range(2, X - 1):
            finish_first(c)
        second[3].start()

    def lower_steps():
        near_high[0].wait_recv()
        x_near(buf1, acc1, 0)

        @pl.when(jnp.logical_not(later_low))
        def _():
            second[0].start()

        finish_first(1)

        @pl.when(jnp.logical_not(later_low))
        def _():
            second[2].start()

    @pl.when(early_down[0])
    def _():
        upper_steps()

    lower_steps()

    @pl.when(late_down[0])
    def _():
        upper_steps()

    pack(buf2, 1, range(1, X - 1), jnp.zeros((Y, Z), jnp.float32))
    settle(recv_sem.at[2], tally.at[pl.ds(0, (NF + 1) * Y)])

    @pl.when(later_low & (lax.rem(me[1], 2) == 0))
    def _():
        second[0].start()
        second[2].start()

    g = x_last(buf1, 1)
    for f in range(NF):
        face_x[1, f] = -g[f]
    finish_first(X - 1, g)
    settle(recv_sem.at[3], tally.at[pl.ds(0, NF * Y)])
    g = x_last(buf1, 0)
    for f in range(NF):
        face_x[0, f] = -g[f]
    finish_first(0, g)
    for c in ys2:
        c.start()
    pack(buf2, 1, (0, X - 1), pk[1])

    @pl.when(jnp.logical_not(bottom))
    def _():
        zs2[0].start()

    @pl.when(jnp.logical_not(top))
    def _():
        zs2[1].start()

    still_below(1)

    @pl.when(top)
    def _():
        rec_high[1] = rec_high[0]

    loop(local_part, buf2, acc2)
    @pl.when(later_low & (lax.rem(me[1], 2) == 1))
    def _():
        second[0].start()
        second[2].start()

    settle(recv_sem.at[8], tally.at[pl.ds(0, 4 * NF * X)])
    loop(y_part, buf2, acc2)
    loop(z_part, buf2, acc2)
    pack_slopes()
    x_inner(buf2, acc2)
    w = [buf1[f, 1, PAD:PAD + Y, :] for f in range(NF)]
    face_x[0, 1] -= pressure_of(w, 1.0 / w[0]) * ox[0]
    for side in (0, 1):
        v = volume_beside(side)
        scale_side[side], keep_side[side], gain_side[side] = factors(v, v <= 0.0, (v > 0.0) & (v < 1.0))

    def z_ends():
        @pl.when(top | bottom)
        def _():
            settle(recv_sem.at[9], tally.at[pl.ds(0, Y)])

        @pl.when(jnp.logical_not(top | bottom))
        def _():
            settle(recv_sem.at[9], tally.at[pl.ds(0, 2 * Y)])

        boundary_z(1)
        loop(z_fix, buf2, acc2)

    def finish_second(cells):
        def finish(k, rates):
            for f in range(NF):
                out[f, cells[k]] = 0.5 * (first[f, cells[k]] + rates[f])

        spread(
            [([acc2[f, c] for f in range(NF)], scale[c], keep[c], gain[c]) for c in cells], finish
        )

    def x_side(side):
        settle(recv_sem.at[6 if side else 7], tally.at[pl.ds(0, 2 * NF * Y)])
        total = [part[side, f, 0] + face_x[side, f] for f in range(NF)]
        spread(
            [(total, scale_side[side], keep_side[side], gain_side[side])],
            lambda _, rates: advance(X + 2 if side else 1, rates),
        )
        x_near(buf2, acc2, side)
        c = X - 1 if side else 0
        total = cell_total(acc2, c, x_last(buf2, side))
        for f in range(NF):
            acc2[f, c] = total[f]

    z_first = top | jnp.logical_not(high_first | (late_up[0] & late_down[0] & jnp.logical_not(bottom)))
    upper_cells, lower_cells = range(X - 1, X // 2 - 1, -1), range(X // 2)

    @pl.when(z_first)
    def _():
        z_ends()

    x_side(1)

    @pl.when(z_first)
    def _():
        finish_second(upper_cells)

    x_side(0)

    @pl.when(jnp.logical_not(z_first))
    def _():
        z_ends()
        finish_second(upper_cells)

    finish_second(lower_cells)

    sent = 8 * NF * Y + 8 * NF * X + Y + X

    @pl.when(top)
    def _():
        settle(send_sem, tally.at[pl.ds(0, sent + 2 * Y)])

    @pl.when(bottom)
    def _():
        settle(send_sem, tally.at[pl.ds(0, sent + 3 * Y)])

    @pl.when(jnp.logical_not(top | bottom))
    def _():
        settle(send_sem, tally.at[pl.ds(0, sent + 4 * Y)])


def on_device(state, volume, apertures, flags):
    _, X, Y, Z = state.shape
    f32 = jnp.float32
    wide = pltpu.VMEM((NF, X + 4, Y + 2 * PAD, Z), f32)
    cells = pltpu.VMEM((X, Y, Z), f32)
    fields = pltpu.VMEM((NF, X, Y, Z), f32)
    layer = pltpu.VMEM((Y, Z), f32)
    pair = pltpu.VMEM((2, Y, Z), f32)
    sides = pltpu.VMEM((2, NF, Y, Z), f32)
    return pl.pallas_call(
        kernel,
        out_shape=pltpu.VMEM(state.shape, f32),
        in_specs=[pl.BlockSpec(memory_space=pl.ANY)] * 4,
        out_specs=pl.BlockSpec(memory_space=pltpu.VMEM),
        scratch_shapes=[
            wide, wide,
            pltpu.VMEM((X + 1, Y, Z), f32),
            pltpu.VMEM((X, Y + 8, Z), f32),
            cells, cells, pltpu.VMEM((X, Y, Z), jnp.int32),
            pair, pair, pair,
            pltpu.VMEM((NF, Y, Z), f32), layer, layer,
            fields, fields, fields, cells, cells, cells, cells, fields, sides, sides,
            pltpu.VMEM((2, NF, 1, Y, Z), f32), pltpu.VMEM((2, NF, 1, Y, Z), f32), sides, pair, pair, pair,
            pltpu.VMEM((8 * NF * (X + Y) + 16 * Y + 8 * X, Z), f32),
            pltpu.SemaphoreType.DMA,
            pltpu.SemaphoreType.DMA((10,)),
            pltpu.SemaphoreType.REGULAR((5,)),
        ],
        compiler_params=pltpu.CompilerParams(collective_id=0, has_side_effects=True),
    )(state, volume, apertures, flags)


def solution(mesh):
    in_specs = (
        P(None, "gx", "gy", "gz"),
        P("gx", "gy", "gz"),
        P(None, "gx", "gy", "gz"),
        P("gx", "gy", "gz"),
    )
    return jax.shard_map(
        on_device, mesh=mesh, in_specs=in_specs, out_specs=P(None, "gx", "gy", "gz"),
        check_vma=False,
    )
```

```python
import jax
import jax.numpy as jnp
from jax import lax
from jax.experimental import pallas as pl
from jax.experimental.pallas import tpu as pltpu
from jax.sharding import PartitionSpec as P

CUTZ = 32
SOLID = CUTZ // 4
NF = 5
GAMMA_LESS = 0.4
DISSIPATION = 4.0
TIME_STEP = 0.02
VOLUME_FLOOR = 0.5
PAD = 8

MESH = pl.DeviceIdType.MESH


def minmod(a, b):
    return jnp.maximum(jnp.minimum(a, b), 0.0) + jnp.minimum(jnp.maximum(a, b), 0.0)


def pressure_of(w, inverse):
    kinetic = w[1] * w[1] + w[2] * w[2] + w[3] * w[3]
    return GAMMA_LESS * (w[4] - 0.5 * kinetic * inverse)


def flux(w, d):
    inverse = 1.0 / w[0]
    u = w[d] * inverse
    p = pressure_of(w, inverse)
    out = [w[d], w[1] * u, w[2] * u, w[3] * u, (w[4] + p) * u]
    out[d] = out[d] + p
    return out


def face(left, right, d, half_open):
    fl, fr = flux(left, d), flux(right, d)
    return [
        ((fl[f] + fr[f]) + DISSIPATION * (left[f] - right[f])) * half_open for f in range(NF)
    ]


def kernel(
    state, volume, apertures, flags, out,
    buf1, buf2, ox, oy, oz, vol, flg, pk, rec_low, rec_high, fix, slope_pk, press_pk,
    acc1, acc2, first, scale, keep, gain, press, inner, edge, outer,
    near_send, part, face_x, scale_side, keep_side, gain_side, tally,
    send_sem, recv_sem, ready,
):
    _, X, Y, Z = state.shape
    F4 = 4 * X
    me = [lax.axis_index(a) for a in ("gx", "gy", "gz")]
    size = [lax.axis_size(a) for a in ("gx", "gy", "gz")]
    up = [{a: lax.rem(me[i] + 1, size[i])} for i, a in enumerate(("gx", "gy", "gz"))]
    down = [{a: lax.rem(me[i] + size[i] - 1, size[i])} for i, a in enumerate(("gx", "gy", "gz"))]

    rows = pl.ds(PAD, Y)
    def settle(sem, ref):
        pltpu.make_async_copy(ref, ref, sem).wait()

    loads = [
        (state, buf1.at[:, pl.ds(2, X), rows, :]),
        (apertures.at[0], ox.at[pl.ds(0, X)]),
        (apertures.at[1], oy.at[:, pl.ds(0, Y), :]),
        (apertures.at[2], oz),
        (volume, vol),
        (flags, flg),
    ]
    loads = [pltpu.make_async_copy(s, d, send_sem) for s, d in loads]

    barrier = pltpu.get_barrier_semaphore()
    n_z = size[2]
    bottom, top = me[2] == 0, me[2] == n_z - 1
    early_up = [me[i] < size[i] // 2 for i in range(2)] + [jnp.logical_not(top)]
    early_down = [(me[i] == 0) | (me[i] > size[i] // 2) for i in range(2)] + [bottom]
    late_up = [jnp.logical_not(e) for e in early_up]
    late_down = [jnp.logical_not(e) for e in early_down]
    late_edges = 0
    for i in range(3):
        @pl.when(early_up[i])
        def _():
            pl.semaphore_signal(barrier, inc=1, device_id=up[i], device_id_type=MESH)

        @pl.when(early_down[i])
        def _():
            pl.semaphore_signal(barrier, inc=1, device_id=down[i], device_id_type=MESH)

        late_edges = late_edges + jnp.where(late_up[i], 1, 0) + jnp.where(late_down[i], 1, 0)

    up_slot, down_slot = (1, 2, 4), (0, 2, 3)
    for load in loads:
        load.start()

    @pl.when(late_edges > 0)
    def _():
        pl.semaphore_wait(barrier, late_edges)

    for i in range(3):
        @pl.when(late_down[i])
        def _():
            pl.semaphore_signal(ready.at[up_slot[i]], inc=1, device_id=down[i], device_id_type=MESH)

        @pl.when(late_up[i])
        def _():
            pl.semaphore_signal(ready.at[down_slot[i]], inc=1, device_id=up[i], device_id_type=MESH)

    def send_late(i, low, high):
        @pl.when(late_down[i])
        def _():
            for c in low:
                c.start()

        @pl.when(late_up[i])
        def _():
            for c in high:
                c.start()

    def send_early_up(i, high, slot):
        @pl.when(early_up[i])
        def _():
            if slot is not None:
                pl.semaphore_wait(ready.at[slot], 1)
            for c in high:
                c.start()

    def send_early_down(i, low, slot):
        @pl.when(early_down[i])
        def _():
            if slot is not None:
                pl.semaphore_wait(ready.at[slot], 1)
            for c in low:
                c.start()

    def remote(src, dst, recv, target):
        return pltpu.make_async_remote_copy(
            src_ref=src, dst_ref=dst, send_sem=send_sem, recv_sem=recv_sem.at[recv],
            device_id=target, device_id_type=MESH,
        )

    def layer(src, cell, dst, place, recv, target):
        return remote(
            src.at[:, pl.ds(2 + cell, 1), rows, :], dst.at[:, pl.ds(place, 1), rows, :],
            recv, target,
        )

    def y_copies(src, x0, y0, buf, recv):
        mid = pl.ds(x0, X)
        return (
            remote(src.at[:, mid, pl.ds(y0, 2), :],
                   buf.at[:, pl.ds(2, X), pl.ds(PAD + Y, 2), :], recv, down[1]),
            remote(src.at[:, mid, pl.ds(y0 + Y - 2, 2), :],
                   buf.at[:, pl.ds(2, X), pl.ds(PAD - 2, 2), :], recv, up[1]),
        )

    def z_copies(stage, recv):
        return (
            remote(pk.at[stage], rec_high.at[stage], recv, down[2]),
            remote(pk.at[stage], rec_low.at[stage], recv, up[2]),
        )

    near_low = (remote(near_send.at[0], buf1.at[:, pl.ds(X + 2, 1), rows, :], 0, down[0]),)
    near_high = (remote(near_send.at[1], buf1.at[:, pl.ds(1, 1), rows, :], 1, up[0]),)
    rest_low = (
        layer(buf1, 1, buf1, X + 3, 2, down[0]),
        remote(ox.at[pl.ds(0, 1)], ox.at[pl.ds(X, 1)], 2, down[0]),
    )
    rest_high = (layer(buf1, X - 2, buf1, 0, 2, up[0]),)
    ys1 = y_copies(buf1, 2, PAD, buf1, 3)
    ay = remote(oy.at[:, pl.ds(0, 1), :], oy.at[:, pl.ds(Y, 1), :], 3, down[1])
    y_low, y_high = (ay, ys1[0]), (ys1[1],)
    settle(send_sem, tally.at[pl.ds(0, 10 * X * Y)])
    send_late(1, y_low, y_high)
    lane = lax.broadcasted_iota(jnp.int32, (Y, Z), 1)

    for side, c in ((0, 0), (1, X - 1)):
        for f in range(NF):
            value = buf1[f, c + 2, PAD:PAD + Y, :]
            if f in (1, 2):
                value = jnp.where(
                    (lane < SOLID) & bottom, pltpu.roll(vol[c], Z - f * SOLID, 1), value
                )
            near_send[side, f, 0] = value

    def volume_beside(side):
        place = X + 2 if side else 1
        first_part = pltpu.roll(buf1[1, place, PAD:PAD + Y, :], SOLID, 1)
        second_part = pltpu.roll(buf1[2, place, PAD:PAD + Y, :], 2 * SOLID, 1)
        v = jnp.where(lane < 2 * SOLID, first_part, second_part)
        v = jnp.where(lane < SOLID, 0.0, jnp.where(lane < 3 * SOLID, v, 1.0))
        return jnp.where(bottom, v, 1.0)

    send_late(0, near_low, near_high)

    quad = lax.rem(lane, 4)

    def pack(buf, stage, planes, packed):
        for f in range(NF + 1):
            for x in planes:
                base = f * F4 + 4 * x
                value = buf[f, x + 2, PAD:PAD + Y, :] if f < NF else oz[x]
                inside = (lane >= base) & (lane < base + 4)
                packed = jnp.where(inside, pltpu.roll(value, base + 2, 1), packed)
        pk[stage] = packed

    def still_below(stage):
        @pl.when(bottom)
        def _():
            own = pk[stage]
            rec_low[stage] = jnp.where(
                quad == 0, pltpu.roll(own, Z - 2, 1), pltpu.roll(own, Z - 1, 1)
            )

    pack(buf1, 0, range(X), jnp.zeros((Y, Z), jnp.float32))
    zs1 = z_copies(0, 4)

    send_late(2, (zs1[0],), ())
    still_below(0)
    send_late(0, rest_low, rest_high)
    limit = jnp.where(me[2] == 0, CUTZ, 0)

    def factors(v, solid, cut):
        weight = jnp.sum(jnp.where(lane < CUTZ, v, 0.0), axis=1, keepdims=True)
        inverse = jnp.where(solid, 0.0, -1.0 / jnp.maximum(v, VOLUME_FLOOR))
        excess = jnp.where(cut & (lane < limit), 1.0 - v, 0.0)
        return (
            (1.0 - excess) * inverse,
            excess * inverse,
            jnp.where(lane < limit, v / weight, 0.0),
        )

    for x in range(X):
        scale[x], keep[x], gain[x] = factors(vol[x], flg[x] == 2, flg[x] == 1)

    def pack_slopes():
        slopes, pressures = jnp.zeros((Y, Z), jnp.float32), jnp.zeros((Y, Z), jnp.float32)
        for x in range(X):
            for f in range(NF):
                base = f * F4 + 4 * x
                inside = (lane >= base) & (lane < base + 4)
                slopes = jnp.where(inside, pltpu.roll(inner[f, x], base + 2, 1), slopes)
            inside = (lane >= 4 * x) & (lane < 4 * x + 4)
            pressures = jnp.where(inside, pltpu.roll(press[x], 4 * x + 2, 1), pressures)
        slope_pk[...] = 0.5 * slopes
        press_pk[...] = pressures

    def boundary_z(stage):
        own, low, high = pk[stage], rec_low[stage], rec_high[stage]
        lower, upper = jnp.where(quad < 2, low, own), jnp.where(quad < 2, own, high)
        below2, below, above = (pltpu.roll(lower, k % Z, 1) for k in (2, 1, -1))
        s_low = 0.5 * minmod(below - below2, lower - below)
        s_own = jnp.where(quad == 3, slope_pk[...], 0.5 * minmod(lower - below, above - lower))
        under, over, over2 = (pltpu.roll(upper, k % Z, 1) for k in (1, -1, -2))
        s_up = 0.5 * minmod(over - upper, over2 - over)
        s_top = jnp.where(quad == 0, slope_pk[...], 0.5 * minmod(upper - under, over - upper))
        left = jnp.where(quad < 2, upper + s_top, below + s_low)
        right = jnp.where(quad < 2, over - s_up, lower - s_own)
        opening = jnp.where(
            quad < 2, pltpu.roll(jnp.where(quad == 2, high, own), Z - 1, 1), own
        )
        ls = [pltpu.roll(left, Z - f * F4, 1) if f else left for f in range(NF)]
        rs = [pltpu.roll(right, Z - f * F4, 1) if f else right for f in range(NF)]
        opening = pltpu.roll(opening, Z - NF * F4, 1)
        live = lane < F4
        ls = [jnp.where(live, w, 1.0) for w in ls]
        rs = [jnp.where(live, w, 1.0) for w in rs]
        g = face(ls, rs, 3, 0.5 * opening)
        for f in range(NF):
            before, after = pltpu.roll(g[f], 1, 1), pltpu.roll(g[f], Z - 1, 1)
            change = jnp.where(
                quad == 0, g[f],
                jnp.where(quad == 1, g[f] - before, jnp.where(quad == 2, after - g[f], -g[f])),
            )
            if f == 3:
                change = change - jnp.where(quad == 1, press_pk[...] * opening, 0.0)
            fix[f] = change

    def local_part(x, buf, acc):
        v = [buf[f, x + 2, PAD:PAD + Y, :] for f in range(NF)]
        press[x] = pressure_of(v, 1.0 / v[0])
        for f in range(NF):
            d = v[f] - pltpu.roll(v[f], 1, 1)
            inner[f, x] = minmod(d, pltpu.roll(d, Z - 1, 1))

    def z_part(x, buf, acc):
        v = [buf[f, x + 2, PAD:PAD + Y, :] for f in range(NF)]
        p = press[x]
        a = oz[x]
        sl = [0.5 * inner[f, x] for f in range(NF)]
        left = [pltpu.roll(v[f] + sl[f], 1, 1) for f in range(NF)]
        right = [v[f] - sl[f] for f in range(NF)]
        g = face(left, right, 3, jnp.where((lane >= 2) & (lane < Z - 1), 0.5 * a, 0.0))
        div = [acc[f, x] + (pltpu.roll(g[f], Z - 1, 1) - g[f]) for f in range(NF)]
        div[3] = div[3] - p * (jnp.where(lane == Z - 1, 0.0, pltpu.roll(a, Z - 1, 1)) - a)
        for f in range(NF):
            acc[f, x] = div[f]

    def z_fix(x, buf, acc):
        ends = (lane < 2) | (lane >= Z - 2)
        for f in range(NF):
            acc[f, x] += jnp.where(ends, pltpu.roll(fix[f], Z - (4 * x + 2), 1), 0.0)

    def y_part(x, buf, acc):
        p = press[x]
        E = Y + 8
        left, right, div = [], [], []
        for f in range(NF):
            c = buf[f, x + 2, PAD - 1:PAD - 1 + E, :]
            b = buf[f, x + 2, PAD - 2:PAD - 2 + E, :]
            n = buf[f, x + 2, PAD:PAD + E, :]
            s = 0.5 * minmod(c - b, n - c)
            left.append(c + s)
            right.append(pltpu.roll(c - s, E - 1, 0))
        a = oy[x]
        g = face(left, right, 2, 0.5 * a)
        for f in range(NF):
            div.append(pltpu.roll(g[f], E - 1, 0)[:Y] - g[f][:Y])
        div[2] = div[2] - p * (oy[x, 1:Y + 1, :] - oy[x, 0:Y, :])
        for f in range(NF):
            acc[f, x] = div[f]

    def load(buf, f, x):
        return buf[f, x + 2, PAD:PAD + Y, :]

    def half_slope(buf, x):
        out = []
        for f in range(NF):
            c = load(buf, f, x)
            out.append(0.5 * minmod(c - load(buf, f, x - 1), load(buf, f, x + 1) - c))
        return out

    def x_face(buf, x, s_low, s_high):
        left = [load(buf, f, x - 1) + s_low[f] for f in range(NF)]
        right = [load(buf, f, x) - s_high[f] for f in range(NF)]
        return face(left, right, 1, 0.5 * ox[x])

    def x_inner(buf, acc):
        below = half_slope(buf, 1)
        for f in range(NF):
            edge[0, f] = below[f]
        for x in range(2, X - 1):
            s = half_slope(buf, x)
            g = x_face(buf, x, below, s)
            for f in range(NF):
                acc[f, x - 1] += g[f]
                acc[f, x] -= g[f]
            below = s
        for f in range(NF):
            edge[1, f] = below[f]
        for x in range(X):
            push = press[x] * (ox[x + 1] - ox[x]) if x < X - 1 else -press[x] * ox[x]
            acc[1, x] -= push

    def x_near(buf, acc, side):
        x = X - 1 if side else 0
        s = half_slope(buf, x)
        for f in range(NF):
            outer[side, f] = s[f]
        inner_s = [edge[side, f] for f in range(NF)]
        g = x_face(buf, x, inner_s, s) if side else x_face(buf, 1, s, inner_s)
        for f in range(NF):
            if side:
                acc[f, X - 2] += g[f]
                acc[f, X - 1] -= g[f]
            else:
                acc[f, 1] -= g[f]
                acc[f, 0] += g[f]

    def x_last(buf, side):
        s = [outer[side, f] for f in range(NF)]
        if side:
            return x_face(buf, X, s, half_slope(buf, X))
        return [-v for v in x_face(buf, 0, half_slope(buf, -1), s)]

    def spread(cells, finish):
        @pl.when(bottom)
        def _():
            with_cut(cells, finish)

        @pl.when(jnp.logical_not(bottom))
        def _():
            for k, (total, scales, _, _) in enumerate(cells):
                finish(k, [scales * t for t in total])

    def with_cut(cells, finish):
        for k, (total, scales, keeps, gains) in enumerate(cells):
            moved = [jnp.sum(keeps * t, axis=1, keepdims=True) for t in total]
            finish(k, [scales * total[f] + gains * moved[f] for f in range(NF)])

    def cell_total(acc, c, g):
        total = [acc[f, c] for f in range(NF)]
        if g is not None:
            total = [t + v for t, v in zip(total, g)]
            if c == X - 1:
                total[1] = total[1] - press[c] * ox[X]
        return total

    def loop(step, buf, acc):
        def body(x, carry):
            step(x, buf, acc)
            return carry

        lax.fori_loop(0, X, body, 0, unroll=True)

    @pl.when(early_up[1] | early_down[1])
    def _():
        pl.semaphore_wait(ready.at[2], jnp.where(early_up[1], 1, 0) + jnp.where(early_down[1], 1, 0))

    send_early_up(1, y_high, None)
    send_early_down(1, y_low, None)
    loop(local_part, buf1, acc1)
    send_early_up(0, near_high, 1)
    send_early_up(2, (zs1[1],), 4)
    settle(recv_sem.at[3], tally.at[pl.ds(0, X * (4 * NF + 1))])
    loop(y_part, buf1, acc1)
    send_early_down(0, near_low, 0)
    send_early_up(0, rest_high, None)
    send_early_down(0, rest_low, None)
    loop(z_part, buf1, acc1)
    pack_slopes()
    x_inner(buf1, acc1)
    send_early_down(2, (zs1[0],), 3)

    @pl.when(bottom)
    def _():
        settle(recv_sem.at[4], tally.at[pl.ds(0, Y)])

    @pl.when(jnp.logical_not(bottom))
    def _():
        settle(recv_sem.at[4], tally.at[pl.ds(0, 2 * Y)])

    boundary_z(0)
    loop(z_fix, buf1, acc1)

    ys2 = y_copies(buf2, 2, PAD, buf2, 7)
    zs2 = z_copies(1, 8)

    def advance(place, rates):
        for f in range(NF):
            now = buf1[f, place, PAD:PAD + Y, :]
            buf2[f, place, PAD:PAD + Y, :] = now + TIME_STEP * rates[f]

    def finish_first(c, g=None):
        def finish(_, rates):
            for f in range(NF):
                first[f, c] = rates[f]
            advance(c + 2, rates)

        spread([(cell_total(acc1, c, g), scale[c], keep[c], gain[c])], finish)

    second = (
        remote(acc1.at[:, pl.ds(0, 1)], part.at[1], 5, down[0]),
        remote(acc1.at[:, pl.ds(X - 1, 1)], part.at[0], 6, up[0]),
        layer(buf2, 1, buf2, X + 3, 5, down[0]),
        layer(buf2, X - 2, buf2, 0, 9, up[0]),
    )
    high_first = late_up[0] & early_down[0]
    later_low = high_first & bottom

    def upper_steps():
        near_low[0].wait_recv()
        x_near(buf1, acc1, 1)
        second[1].start()
        for c in range(2, X - 1):
            finish_first(c)
        second[3].start()

    def lower_steps():
        near_high[0].wait_recv()
        x_near(buf1, acc1, 0)

        @pl.when(jnp.logical_not(later_low))
        def _():
            second[0].start()

        finish_first(1)

        @pl.when(jnp.logical_not(later_low))
        def _():
            second[2].start()

    @pl.when(early_down[0])
    def _():
        upper_steps()

    lower_steps()

    @pl.when(late_down[0])
    def _():
        upper_steps()

    pack(buf2, 1, range(1, X - 1), jnp.zeros((Y, Z), jnp.float32))
    settle(recv_sem.at[2], tally.at[pl.ds(0, (2 * NF + 1) * Y)])

    @pl.when(later_low & (lax.rem(me[1], 2) == 0))
    def _():
        second[0].start()
        second[2].start()

    g = x_last(buf1, 1)
    for f in range(NF):
        face_x[1, f] = -g[f]
    finish_first(X - 1, g)
    g = x_last(buf1, 0)
    for f in range(NF):
        face_x[0, f] = -g[f]
    finish_first(0, g)
    for c in ys2:
        c.start()
    pack(buf2, 1, (0, X - 1), pk[1])

    @pl.when(jnp.logical_not(bottom))
    def _():
        zs2[0].start()

    @pl.when(jnp.logical_not(top))
    def _():
        zs2[1].start()

    still_below(1)

    @pl.when(top)
    def _():
        rec_high[1] = rec_high[0]

    loop(local_part, buf2, acc2)
    @pl.when(later_low & (lax.rem(me[1], 2) == 1))
    def _():
        second[0].start()
        second[2].start()

    settle(recv_sem.at[7], tally.at[pl.ds(0, 4 * NF * X)])
    loop(y_part, buf2, acc2)
    loop(z_part, buf2, acc2)
    pack_slopes()
    x_inner(buf2, acc2)
    w = [buf1[f, 1, PAD:PAD + Y, :] for f in range(NF)]
    face_x[0, 1] -= pressure_of(w, 1.0 / w[0]) * ox[0]
    for side in (0, 1):
        v = volume_beside(side)
        scale_side[side], keep_side[side], gain_side[side] = factors(v, v <= 0.0, (v > 0.0) & (v < 1.0))

    def z_ends():
        @pl.when(top | bottom)
        def _():
            settle(recv_sem.at[8], tally.at[pl.ds(0, Y)])

        @pl.when(jnp.logical_not(top | bottom))
        def _():
            settle(recv_sem.at[8], tally.at[pl.ds(0, 2 * Y)])

        boundary_z(1)
        loop(z_fix, buf2, acc2)

    def finish_second(cells):
        def finish(k, rates):
            for f in range(NF):
                out[f, cells[k]] = 0.5 * (first[f, cells[k]] + rates[f])

        spread(
            [([acc2[f, c] for f in range(NF)], scale[c], keep[c], gain[c]) for c in cells], finish
        )

    def x_near_side(side, sem, count):
        settle(recv_sem.at[sem], tally.at[pl.ds(0, count * NF * Y)])
        total = [part[side, f, 0] + face_x[side, f] for f in range(NF)]
        spread(
            [(total, scale_side[side], keep_side[side], gain_side[side])],
            lambda _, rates: advance(X + 2 if side else 1, rates),
        )
        x_near(buf2, acc2, side)

    def x_last_side(side):
        c = X - 1 if side else 0
        total = cell_total(acc2, c, x_last(buf2, side))
        for f in range(NF):
            acc2[f, c] = total[f]

    z_first = top | jnp.logical_not(high_first | (late_up[0] & late_down[0] & jnp.logical_not(bottom)))
    upper_cells, lower_cells = range(X - 1, X // 2 - 1, -1), range(1, X // 2)

    def lower_last():
        settle(recv_sem.at[9], tally.at[pl.ds(0, NF * Y)])
        x_last_side(0)

    lower_first = z_first & late_down[0]

    @pl.when(lower_first)
    def _():
        x_near_side(0, 6, 1)
        lower_last()

    @pl.when(z_first)
    def _():
        z_ends()

    x_near_side(1, 5, 2)
    x_last_side(1)

    @pl.when(z_first)
    def _():
        finish_second(upper_cells)

    @pl.when(jnp.logical_not(lower_first))
    def _():
        x_near_side(0, 6, 1)

    @pl.when(z_first)
    def _():
        finish_second(lower_cells)

    @pl.when(jnp.logical_not(lower_first))
    def _():
        lower_last()

    @pl.when(jnp.logical_not(z_first))
    def _():
        z_ends()
        finish_second(upper_cells)
        finish_second(lower_cells)

    finish_second((0,))

    sent = 8 * NF * Y + 8 * NF * X + Y + X

    @pl.when(top)
    def _():
        settle(send_sem, tally.at[pl.ds(0, sent + 2 * Y)])

    @pl.when(bottom)
    def _():
        settle(send_sem, tally.at[pl.ds(0, sent + 3 * Y)])

    @pl.when(jnp.logical_not(top | bottom))
    def _():
        settle(send_sem, tally.at[pl.ds(0, sent + 4 * Y)])


def on_device(state, volume, apertures, flags):
    _, X, Y, Z = state.shape
    f32 = jnp.float32
    wide = pltpu.VMEM((NF, X + 4, Y + 2 * PAD, Z), f32)
    cells = pltpu.VMEM((X, Y, Z), f32)
    fields = pltpu.VMEM((NF, X, Y, Z), f32)
    layer = pltpu.VMEM((Y, Z), f32)
    pair = pltpu.VMEM((2, Y, Z), f32)
    sides = pltpu.VMEM((2, NF, Y, Z), f32)
    return pl.pallas_call(
        kernel,
        out_shape=pltpu.VMEM(state.shape, f32),
        in_specs=[pl.BlockSpec(memory_space=pl.ANY)] * 4,
        out_specs=pl.BlockSpec(memory_space=pltpu.VMEM),
        scratch_shapes=[
            wide, wide,
            pltpu.VMEM((X + 1, Y, Z), f32),
            pltpu.VMEM((X, Y + 8, Z), f32),
            cells, cells, pltpu.VMEM((X, Y, Z), jnp.int32),
            pair, pair, pair,
            pltpu.VMEM((NF, Y, Z), f32), layer, layer,
            fields, fields, fields, cells, cells, cells, cells, fields, sides, sides,
            pltpu.VMEM((2, NF, 1, Y, Z), f32), pltpu.VMEM((2, NF, 1, Y, Z), f32), sides, pair, pair, pair,
            pltpu.VMEM((8 * NF * (X + Y) + 16 * Y + 8 * X, Z), f32),
            pltpu.SemaphoreType.DMA,
            pltpu.SemaphoreType.DMA((10,)),
            pltpu.SemaphoreType.REGULAR((5,)),
        ],
        compiler_params=pltpu.CompilerParams(collective_id=0, has_side_effects=True),
    )(state, volume, apertures, flags)


def solution(mesh):
    in_specs = (
        P(None, "gx", "gy", "gz"),
        P("gx", "gy", "gz"),
        P(None, "gx", "gy", "gz"),
        P("gx", "gy", "gz"),
    )
    return jax.shard_map(
        on_device, mesh=mesh, in_specs=in_specs, out_specs=P(None, "gx", "gy", "gz"),
        check_vma=False,
    )
```

```python
import jax
import jax.numpy as jnp
from jax import lax
from jax.experimental import pallas as pl
from jax.experimental.pallas import tpu as pltpu
from jax.sharding import PartitionSpec as P

CUTZ = 32
SOLID = CUTZ // 4
NF = 5
GAMMA_LESS = 0.4
DISSIPATION = 4.0
TIME_STEP = 0.02
VOLUME_FLOOR = 0.5
PAD = 8

MESH = pl.DeviceIdType.MESH


def minmod(a, b):
    return jnp.maximum(jnp.minimum(a, b), 0.0) + jnp.minimum(jnp.maximum(a, b), 0.0)


def pressure_of(w, inverse):
    kinetic = w[1] * w[1] + w[2] * w[2] + w[3] * w[3]
    return GAMMA_LESS * (w[4] - 0.5 * kinetic * inverse)


def flux(w, d):
    inverse = 1.0 / w[0]
    u = w[d] * inverse
    p = pressure_of(w, inverse)
    out = [w[d], w[1] * u, w[2] * u, w[3] * u, (w[4] + p) * u]
    out[d] = out[d] + p
    return out


def face(left, right, d, half_open):
    fl, fr = flux(left, d), flux(right, d)
    return [
        ((fl[f] + fr[f]) + DISSIPATION * (left[f] - right[f])) * half_open for f in range(NF)
    ]


def kernel(
    state, volume, apertures, flags, out,
    buf1, buf2, ox, oy, oz, vol, flg, pk, rec_low, rec_high, fix, slope_pk, press_pk,
    acc1, acc2, first, scale, keep, gain, press, inner, edge, outer,
    near_send, part, face_x, scale_side, keep_side, gain_side, tally,
    send_sem, recv_sem, ready,
):
    _, X, Y, Z = state.shape
    F4 = 4 * X
    me = [lax.axis_index(a) for a in ("gx", "gy", "gz")]
    size = [lax.axis_size(a) for a in ("gx", "gy", "gz")]
    up = [{a: lax.rem(me[i] + 1, size[i])} for i, a in enumerate(("gx", "gy", "gz"))]
    down = [{a: lax.rem(me[i] + size[i] - 1, size[i])} for i, a in enumerate(("gx", "gy", "gz"))]

    rows = pl.ds(PAD, Y)
    def settle(sem, ref):
        pltpu.make_async_copy(ref, ref, sem).wait()

    loads = [
        (state, buf1.at[:, pl.ds(2, X), rows, :]),
        (apertures.at[0], ox.at[pl.ds(0, X)]),
        (apertures.at[1], oy.at[:, pl.ds(0, Y), :]),
        (apertures.at[2], oz),
        (volume, vol),
        (flags, flg),
    ]
    loads = [pltpu.make_async_copy(s, d, send_sem) for s, d in loads]

    barrier = pltpu.get_barrier_semaphore()
    n_z = size[2]
    bottom, top = me[2] == 0, me[2] == n_z - 1
    early_up = [me[i] < size[i] // 2 for i in range(2)] + [jnp.logical_not(top)]
    early_down = [(me[i] == 0) | (me[i] > size[i] // 2) for i in range(2)] + [bottom]
    late_up = [jnp.logical_not(e) for e in early_up]
    late_down = [jnp.logical_not(e) for e in early_down]
    late_edges = 0
    for i in range(3):
        @pl.when(early_up[i])
        def _():
            pl.semaphore_signal(barrier, inc=1, device_id=up[i], device_id_type=MESH)

        @pl.when(early_down[i])
        def _():
            pl.semaphore_signal(barrier, inc=1, device_id=down[i], device_id_type=MESH)

        late_edges = late_edges + jnp.where(late_up[i], 1, 0) + jnp.where(late_down[i], 1, 0)

    up_slot, down_slot = (1, 2, 4), (0, 2, 3)
    for load in loads:
        load.start()

    @pl.when(late_edges > 0)
    def _():
        pl.semaphore_wait(barrier, late_edges)

    for i in range(3):
        @pl.when(late_down[i])
        def _():
            pl.semaphore_signal(ready.at[up_slot[i]], inc=1, device_id=down[i], device_id_type=MESH)

        @pl.when(late_up[i])
        def _():
            pl.semaphore_signal(ready.at[down_slot[i]], inc=1, device_id=up[i], device_id_type=MESH)

    def send_late(i, low, high):
        @pl.when(late_down[i])
        def _():
            for c in low:
                c.start()

        @pl.when(late_up[i])
        def _():
            for c in high:
                c.start()

    def send_early_up(i, high, slot):
        @pl.when(early_up[i])
        def _():
            if slot is not None:
                pl.semaphore_wait(ready.at[slot], 1)
            for c in high:
                c.start()

    def send_early_down(i, low, slot):
        @pl.when(early_down[i])
        def _():
            if slot is not None:
                pl.semaphore_wait(ready.at[slot], 1)
            for c in low:
                c.start()

    def remote(src, dst, recv, target):
        return pltpu.make_async_remote_copy(
            src_ref=src, dst_ref=dst, send_sem=send_sem, recv_sem=recv_sem.at[recv],
            device_id=target, device_id_type=MESH,
        )

    def layer(src, cell, dst, place, recv, target):
        return remote(
            src.at[:, pl.ds(2 + cell, 1), rows, :], dst.at[:, pl.ds(place, 1), rows, :],
            recv, target,
        )

    def y_copies(src, x0, y0, buf, recv):
        mid = pl.ds(x0, X)
        return (
            remote(src.at[:, mid, pl.ds(y0, 2), :],
                   buf.at[:, pl.ds(2, X), pl.ds(PAD + Y, 2), :], recv, down[1]),
            remote(src.at[:, mid, pl.ds(y0 + Y - 2, 2), :],
                   buf.at[:, pl.ds(2, X), pl.ds(PAD - 2, 2), :], recv, up[1]),
        )

    def z_copies(stage, recv):
        return (
            remote(pk.at[stage], rec_high.at[stage], recv, down[2]),
            remote(pk.at[stage], rec_low.at[stage], recv, up[2]),
        )

    near_low = (remote(near_send.at[0], buf1.at[:, pl.ds(X + 2, 1), rows, :], 0, down[0]),)
    near_high = (remote(near_send.at[1], buf1.at[:, pl.ds(1, 1), rows, :], 1, up[0]),)
    rest_low = (
        layer(buf1, 1, buf1, X + 3, 2, down[0]),
        remote(ox.at[pl.ds(0, 1)], ox.at[pl.ds(X, 1)], 2, down[0]),
    )
    rest_high = (layer(buf1, X - 2, buf1, 0, 2, up[0]),)
    ys1 = y_copies(buf1, 2, PAD, buf1, 3)
    ay = remote(oy.at[:, pl.ds(0, 1), :], oy.at[:, pl.ds(Y, 1), :], 3, down[1])
    y_low, y_high = (ay, ys1[0]), (ys1[1],)
    settle(send_sem, tally.at[pl.ds(0, 10 * X * Y)])
    send_late(1, y_low, y_high)
    lane = lax.broadcasted_iota(jnp.int32, (Y, Z), 1)

    for side, c in ((0, 0), (1, X - 1)):
        for f in range(NF):
            value = buf1[f, c + 2, PAD:PAD + Y, :]
            if f in (1, 2):
                value = jnp.where(
                    (lane < SOLID) & bottom, pltpu.roll(vol[c], Z - f * SOLID, 1), value
                )
            near_send[side, f, 0] = value

    def volume_beside(side):
        place = X + 2 if side else 1
        first_part = pltpu.roll(buf1[1, place, PAD:PAD + Y, :], SOLID, 1)
        second_part = pltpu.roll(buf1[2, place, PAD:PAD + Y, :], 2 * SOLID, 1)
        v = jnp.where(lane < 2 * SOLID, first_part, second_part)
        v = jnp.where(lane < SOLID, 0.0, jnp.where(lane < 3 * SOLID, v, 1.0))
        return jnp.where(bottom, v, 1.0)

    send_late(0, near_low, near_high)

    quad = lax.rem(lane, 4)

    def pack(buf, stage, planes, packed):
        for f in range(NF + 1):
            for x in planes:
                base = f * F4 + 4 * x
                value = buf[f, x + 2, PAD:PAD + Y, :] if f < NF else oz[x]
                inside = (lane >= base) & (lane < base + 4)
                packed = jnp.where(inside, pltpu.roll(value, base + 2, 1), packed)
        pk[stage] = packed

    def still_below(stage):
        @pl.when(bottom)
        def _():
            own = pk[stage]
            rec_low[stage] = jnp.where(
                quad == 0, pltpu.roll(own, Z - 2, 1), pltpu.roll(own, Z - 1, 1)
            )

    pack(buf1, 0, range(X), jnp.zeros((Y, Z), jnp.float32))
    zs1 = z_copies(0, 4)

    send_late(2, (zs1[0],), ())
    still_below(0)
    send_late(0, rest_low, rest_high)
    limit = jnp.where(me[2] == 0, CUTZ, 0)

    def factors(v, solid, cut):
        weight = jnp.sum(jnp.where(lane < CUTZ, v, 0.0), axis=1, keepdims=True)
        inverse = jnp.where(solid, 0.0, -1.0 / jnp.maximum(v, VOLUME_FLOOR))
        excess = jnp.where(cut & (lane < limit), 1.0 - v, 0.0)
        return (
            (1.0 - excess) * inverse,
            excess * inverse,
            jnp.where(lane < limit, v / weight, 0.0),
        )

    for x in range(X):
        scale[x], keep[x], gain[x] = factors(vol[x], flg[x] == 2, flg[x] == 1)

    def pack_slopes():
        slopes, pressures = jnp.zeros((Y, Z), jnp.float32), jnp.zeros((Y, Z), jnp.float32)
        for x in range(X):
            for f in range(NF):
                base = f * F4 + 4 * x
                inside = (lane >= base) & (lane < base + 4)
                slopes = jnp.where(inside, pltpu.roll(inner[f, x], base + 2, 1), slopes)
            inside = (lane >= 4 * x) & (lane < 4 * x + 4)
            pressures = jnp.where(inside, pltpu.roll(press[x], 4 * x + 2, 1), pressures)
        slope_pk[...] = 0.5 * slopes
        press_pk[...] = pressures

    def boundary_z(stage):
        own, low, high = pk[stage], rec_low[stage], rec_high[stage]
        lower, upper = jnp.where(quad < 2, low, own), jnp.where(quad < 2, own, high)
        below2, below, above = (pltpu.roll(lower, k % Z, 1) for k in (2, 1, -1))
        s_low = 0.5 * minmod(below - below2, lower - below)
        s_own = jnp.where(quad == 3, slope_pk[...], 0.5 * minmod(lower - below, above - lower))
        under, over, over2 = (pltpu.roll(upper, k % Z, 1) for k in (1, -1, -2))
        s_up = 0.5 * minmod(over - upper, over2 - over)
        s_top = jnp.where(quad == 0, slope_pk[...], 0.5 * minmod(upper - under, over - upper))
        left = jnp.where(quad < 2, upper + s_top, below + s_low)
        right = jnp.where(quad < 2, over - s_up, lower - s_own)
        opening = jnp.where(
            quad < 2, pltpu.roll(jnp.where(quad == 2, high, own), Z - 1, 1), own
        )
        ls = [pltpu.roll(left, Z - f * F4, 1) if f else left for f in range(NF)]
        rs = [pltpu.roll(right, Z - f * F4, 1) if f else right for f in range(NF)]
        opening = pltpu.roll(opening, Z - NF * F4, 1)
        live = lane < F4
        ls = [jnp.where(live, w, 1.0) for w in ls]
        rs = [jnp.where(live, w, 1.0) for w in rs]
        g = face(ls, rs, 3, 0.5 * opening)
        for f in range(NF):
            before, after = pltpu.roll(g[f], 1, 1), pltpu.roll(g[f], Z - 1, 1)
            change = jnp.where(
                quad == 0, g[f],
                jnp.where(quad == 1, g[f] - before, jnp.where(quad == 2, after - g[f], -g[f])),
            )
            if f == 3:
                change = change - jnp.where(quad == 1, press_pk[...] * opening, 0.0)
            fix[f] = change

    def local_part(x, buf, acc):
        v = [buf[f, x + 2, PAD:PAD + Y, :] for f in range(NF)]
        press[x] = pressure_of(v, 1.0 / v[0])
        for f in range(NF):
            d = v[f] - pltpu.roll(v[f], 1, 1)
            inner[f, x] = minmod(d, pltpu.roll(d, Z - 1, 1))

    def z_part(x, buf, acc):
        v = [buf[f, x + 2, PAD:PAD + Y, :] for f in range(NF)]
        p = press[x]
        a = oz[x]
        sl = [0.5 * inner[f, x] for f in range(NF)]
        left = [pltpu.roll(v[f] + sl[f], 1, 1) for f in range(NF)]
        right = [v[f] - sl[f] for f in range(NF)]
        g = face(left, right, 3, jnp.where((lane >= 2) & (lane < Z - 1), 0.5 * a, 0.0))
        div = [acc[f, x] + (pltpu.roll(g[f], Z - 1, 1) - g[f]) for f in range(NF)]
        div[3] = div[3] - p * (jnp.where(lane == Z - 1, 0.0, pltpu.roll(a, Z - 1, 1)) - a)
        for f in range(NF):
            acc[f, x] = div[f]

    def z_fix(x, buf, acc):
        ends = (lane < 2) | (lane >= Z - 2)
        for f in range(NF):
            acc[f, x] += jnp.where(ends, pltpu.roll(fix[f], Z - (4 * x + 2), 1), 0.0)

    def y_part(x, buf, acc):
        p = press[x]
        E = Y + 8
        left, right, div = [], [], []
        for f in range(NF):
            c = buf[f, x + 2, PAD - 1:PAD - 1 + E, :]
            b = buf[f, x + 2, PAD - 2:PAD - 2 + E, :]
            n = buf[f, x + 2, PAD:PAD + E, :]
            s = 0.5 * minmod(c - b, n - c)
            left.append(c + s)
            right.append(pltpu.roll(c - s, E - 1, 0))
        a = oy[x]
        g = face(left, right, 2, 0.5 * a)
        for f in range(NF):
            div.append(pltpu.roll(g[f], E - 1, 0)[:Y] - g[f][:Y])
        div[2] = div[2] - p * (oy[x, 1:Y + 1, :] - oy[x, 0:Y, :])
        for f in range(NF):
            acc[f, x] = div[f]

    def load(buf, f, x):
        return buf[f, x + 2, PAD:PAD + Y, :]

    def half_slope(buf, x):
        out = []
        for f in range(NF):
            c = load(buf, f, x)
            out.append(0.5 * minmod(c - load(buf, f, x - 1), load(buf, f, x + 1) - c))
        return out

    def x_face(buf, x, s_low, s_high):
        left = [load(buf, f, x - 1) + s_low[f] for f in range(NF)]
        right = [load(buf, f, x) - s_high[f] for f in range(NF)]
        return face(left, right, 1, 0.5 * ox[x])

    def x_inner(buf, acc):
        below = half_slope(buf, 1)
        for f in range(NF):
            edge[0, f] = below[f]
        for x in range(2, X - 1):
            s = half_slope(buf, x)
            g = x_face(buf, x, below, s)
            for f in range(NF):
                acc[f, x - 1] += g[f]
                acc[f, x] -= g[f]
            below = s
        for f in range(NF):
            edge[1, f] = below[f]
        for x in range(X):
            push = press[x] * (ox[x + 1] - ox[x]) if x < X - 1 else -press[x] * ox[x]
            acc[1, x] -= push

    def x_near(buf, acc, side):
        x = X - 1 if side else 0
        s = half_slope(buf, x)
        for f in range(NF):
            outer[side, f] = s[f]
        inner_s = [edge[side, f] for f in range(NF)]
        g = x_face(buf, x, inner_s, s) if side else x_face(buf, 1, s, inner_s)
        for f in range(NF):
            if side:
                acc[f, X - 2] += g[f]
                acc[f, X - 1] -= g[f]
            else:
                acc[f, 1] -= g[f]
                acc[f, 0] += g[f]

    def x_last(buf, side):
        s = [outer[side, f] for f in range(NF)]
        if side:
            return x_face(buf, X, s, half_slope(buf, X))
        return [-v for v in x_face(buf, 0, half_slope(buf, -1), s)]

    def spread(cells, finish):
        @pl.when(bottom)
        def _():
            with_cut(cells, finish)

        @pl.when(jnp.logical_not(bottom))
        def _():
            for k, (total, scales, _, _) in enumerate(cells):
                finish(k, [scales * t for t in total])

    def with_cut(cells, finish):
        for k, (total, scales, keeps, gains) in enumerate(cells):
            moved = [jnp.sum(keeps * t, axis=1, keepdims=True) for t in total]
            finish(k, [scales * total[f] + gains * moved[f] for f in range(NF)])

    def cell_total(acc, c, g):
        total = [acc[f, c] for f in range(NF)]
        if g is not None:
            total = [t + v for t, v in zip(total, g)]
            if c == X - 1:
                total[1] = total[1] - press[c] * ox[X]
        return total

    def loop(step, buf, acc):
        def body(x, carry):
            step(x, buf, acc)
            return carry

        lax.fori_loop(0, X, body, 0, unroll=True)

    @pl.when(early_up[1] | early_down[1])
    def _():
        pl.semaphore_wait(ready.at[2], jnp.where(early_up[1], 1, 0) + jnp.where(early_down[1], 1, 0))

    send_early_up(1, y_high, None)
    send_early_down(1, y_low, None)
    loop(local_part, buf1, acc1)
    send_early_up(0, near_high, 1)
    send_early_up(2, (zs1[1],), 4)
    settle(recv_sem.at[3], tally.at[pl.ds(0, X * (4 * NF + 1))])
    loop(y_part, buf1, acc1)
    send_early_down(0, near_low, 0)
    send_early_up(0, rest_high, None)
    send_early_down(0, rest_low, None)
    loop(z_part, buf1, acc1)
    pack_slopes()
    x_inner(buf1, acc1)
    send_early_down(2, (zs1[0],), 3)

    @pl.when(bottom)
    def _():
        settle(recv_sem.at[4], tally.at[pl.ds(0, Y)])

    @pl.when(jnp.logical_not(bottom))
    def _():
        settle(recv_sem.at[4], tally.at[pl.ds(0, 2 * Y)])

    boundary_z(0)
    loop(z_fix, buf1, acc1)

    ys2 = y_copies(buf2, 2, PAD, buf2, 7)
    zs2 = z_copies(1, 8)

    def advance(place, rates):
        for f in range(NF):
            now = buf1[f, place, PAD:PAD + Y, :]
            buf2[f, place, PAD:PAD + Y, :] = now + TIME_STEP * rates[f]

    def finish_first(c, g=None):
        def finish(_, rates):
            for f in range(NF):
                first[f, c] = rates[f]
            advance(c + 2, rates)

        spread([(cell_total(acc1, c, g), scale[c], keep[c], gain[c])], finish)

    second = (
        remote(acc1.at[:, pl.ds(0, 1)], part.at[1], 5, down[0]),
        remote(acc1.at[:, pl.ds(X - 1, 1)], part.at[0], 6, up[0]),
        layer(buf2, 1, buf2, X + 3, 5, down[0]),
        layer(buf2, X - 2, buf2, 0, 9, up[0]),
    )
    high_first = late_up[0] & early_down[0]
    later_low = high_first & bottom

    def upper_steps():
        near_low[0].wait_recv()
        x_near(buf1, acc1, 1)
        second[1].start()
        for c in range(2, X - 1):
            finish_first(c)
        second[3].start()

    def lower_steps():
        near_high[0].wait_recv()
        x_near(buf1, acc1, 0)

        @pl.when(jnp.logical_not(later_low))
        def _():
            second[0].start()

        finish_first(1)

        @pl.when(jnp.logical_not(later_low))
        def _():
            second[2].start()

    @pl.when(early_down[0])
    def _():
        upper_steps()

    lower_steps()

    @pl.when(late_down[0])
    def _():
        upper_steps()

    pack(buf2, 1, range(1, X - 1), jnp.zeros((Y, Z), jnp.float32))
    settle(recv_sem.at[2], tally.at[pl.ds(0, (2 * NF + 1) * Y)])

    @pl.when(later_low & (lax.rem(me[1], 2) == 0))
    def _():
        second[0].start()
        second[2].start()

    g = x_last(buf1, 1)
    for f in range(NF):
        face_x[1, f] = -g[f]
    finish_first(X - 1, g)
    g = x_last(buf1, 0)
    for f in range(NF):
        face_x[0, f] = -g[f]
    finish_first(0, g)
    for c in ys2:
        c.start()
    pack(buf2, 1, (0, X - 1), pk[1])

    @pl.when(jnp.logical_not(bottom))
    def _():
        zs2[0].start()

    @pl.when(jnp.logical_not(top))
    def _():
        zs2[1].start()

    still_below(1)

    @pl.when(top)
    def _():
        rec_high[1] = rec_high[0]

    loop(local_part, buf2, acc2)
    @pl.when(later_low & (lax.rem(me[1], 2) == 1))
    def _():
        second[0].start()
        second[2].start()

    settle(recv_sem.at[7], tally.at[pl.ds(0, 4 * NF * X)])
    loop(y_part, buf2, acc2)
    loop(z_part, buf2, acc2)
    pack_slopes()
    x_inner(buf2, acc2)
    w = [buf1[f, 1, PAD:PAD + Y, :] for f in range(NF)]
    face_x[0, 1] -= pressure_of(w, 1.0 / w[0]) * ox[0]
    for side in (0, 1):
        v = volume_beside(side)
        scale_side[side], keep_side[side], gain_side[side] = factors(v, v <= 0.0, (v > 0.0) & (v < 1.0))

    def z_ends():
        @pl.when(top | bottom)
        def _():
            settle(recv_sem.at[8], tally.at[pl.ds(0, Y)])

        @pl.when(jnp.logical_not(top | bottom))
        def _():
            settle(recv_sem.at[8], tally.at[pl.ds(0, 2 * Y)])

        boundary_z(1)
        loop(z_fix, buf2, acc2)

    def finish_second(cells):
        def finish(k, rates):
            for f in range(NF):
                out[f, cells[k]] = 0.5 * (first[f, cells[k]] + rates[f])

        spread(
            [([acc2[f, c] for f in range(NF)], scale[c], keep[c], gain[c]) for c in cells], finish
        )

    def x_near_side(side, sem, count):
        settle(recv_sem.at[sem], tally.at[pl.ds(0, count * NF * Y)])
        total = [part[side, f, 0] + face_x[side, f] for f in range(NF)]
        spread(
            [(total, scale_side[side], keep_side[side], gain_side[side])],
            lambda _, rates: advance(X + 2 if side else 1, rates),
        )
        x_near(buf2, acc2, side)

    def x_last_side(side):
        c = X - 1 if side else 0
        total = cell_total(acc2, c, x_last(buf2, side))
        for f in range(NF):
            acc2[f, c] = total[f]

    z_first = top | jnp.logical_not(high_first | (late_up[0] & late_down[0] & jnp.logical_not(bottom)))
    upper_cells, lower_cells = range(X - 1, X // 2 - 1, -1), range(1, X // 2)

    def lower_last():
        settle(recv_sem.at[9], tally.at[pl.ds(0, NF * Y)])
        x_last_side(0)

    lower_first = z_first & late_down[0]

    @pl.when(lower_first)
    def _():
        x_near_side(0, 6, 1)
        lower_last()

    @pl.when(z_first)
    def _():
        z_ends()

    x_near_side(1, 5, 2)
    x_last_side(1)
    lower_end = z_first & jnp.logical_not(lower_first)

    @pl.when(lower_end)
    def _():
        finish_second(upper_cells)

    @pl.when(jnp.logical_not(lower_first))
    def _():
        x_near_side(0, 6, 1)

    @pl.when(lower_end)
    def _():
        finish_second(lower_cells)

    @pl.when(jnp.logical_not(lower_first))
    def _():
        lower_last()

    @pl.when(jnp.logical_not(z_first))
    def _():
        z_ends()

    @pl.when(lower_end)
    def _():
        finish_second((0,))

    @pl.when(jnp.logical_not(lower_end))
    def _():
        finish_second(range(X))

    sent = 8 * NF * Y + 8 * NF * X + Y + X

    @pl.when(top)
    def _():
        settle(send_sem, tally.at[pl.ds(0, sent + 2 * Y)])

    @pl.when(bottom)
    def _():
        settle(send_sem, tally.at[pl.ds(0, sent + 3 * Y)])

    @pl.when(jnp.logical_not(top | bottom))
    def _():
        settle(send_sem, tally.at[pl.ds(0, sent + 4 * Y)])


def on_device(state, volume, apertures, flags):
    _, X, Y, Z = state.shape
    f32 = jnp.float32
    wide = pltpu.VMEM((NF, X + 4, Y + 2 * PAD, Z), f32)
    cells = pltpu.VMEM((X, Y, Z), f32)
    fields = pltpu.VMEM((NF, X, Y, Z), f32)
    layer = pltpu.VMEM((Y, Z), f32)
    pair = pltpu.VMEM((2, Y, Z), f32)
    sides = pltpu.VMEM((2, NF, Y, Z), f32)
    return pl.pallas_call(
        kernel,
        out_shape=pltpu.VMEM(state.shape, f32),
        in_specs=[pl.BlockSpec(memory_space=pl.ANY)] * 4,
        out_specs=pl.BlockSpec(memory_space=pltpu.VMEM),
        scratch_shapes=[
            wide, wide,
            pltpu.VMEM((X + 1, Y, Z), f32),
            pltpu.VMEM((X, Y + 8, Z), f32),
            cells, cells, pltpu.VMEM((X, Y, Z), jnp.int32),
            pair, pair, pair,
            pltpu.VMEM((NF, Y, Z), f32), layer, layer,
            fields, fields, fields, cells, cells, cells, cells, fields, sides, sides,
            pltpu.VMEM((2, NF, 1, Y, Z), f32), pltpu.VMEM((2, NF, 1, Y, Z), f32), sides, pair, pair, pair,
            pltpu.VMEM((8 * NF * (X + Y) + 16 * Y + 8 * X, Z), f32),
            pltpu.SemaphoreType.DMA,
            pltpu.SemaphoreType.DMA((10,)),
            pltpu.SemaphoreType.REGULAR((5,)),
        ],
        compiler_params=pltpu.CompilerParams(collective_id=0, has_side_effects=True),
    )(state, volume, apertures, flags)


def solution(mesh):
    in_specs = (
        P(None, "gx", "gy", "gz"),
        P("gx", "gy", "gz"),
        P(None, "gx", "gy", "gz"),
        P("gx", "gy", "gz"),
    )
    return jax.shard_map(
        on_device, mesh=mesh, in_specs=in_specs, out_specs=P(None, "gx", "gy", "gz"),
        check_vma=False,
    )
```

```python
import jax
import jax.numpy as jnp
from jax import lax
from jax.experimental import pallas as pl
from jax.experimental.pallas import tpu as pltpu
from jax.sharding import PartitionSpec as P

CUTZ = 32
SOLID = CUTZ // 4
NF = 5
GAMMA_LESS = 0.4
DISSIPATION = 4.0
TIME_STEP = 0.02
VOLUME_FLOOR = 0.5
PAD = 8

MESH = pl.DeviceIdType.MESH


def minmod(a, b):
    return jnp.maximum(jnp.minimum(a, b), 0.0) + jnp.minimum(jnp.maximum(a, b), 0.0)


def pressure_of(w, inverse):
    kinetic = w[1] * w[1] + w[2] * w[2] + w[3] * w[3]
    return GAMMA_LESS * (w[4] - 0.5 * kinetic * inverse)


def flux(w, d):
    inverse = 1.0 / w[0]
    u = w[d] * inverse
    p = pressure_of(w, inverse)
    out = [w[d], w[1] * u, w[2] * u, w[3] * u, (w[4] + p) * u]
    out[d] = out[d] + p
    return out


def face(left, right, d, half_open):
    fl, fr = flux(left, d), flux(right, d)
    return [
        ((fl[f] + fr[f]) + DISSIPATION * (left[f] - right[f])) * half_open for f in range(NF)
    ]


def kernel(
    state, volume, apertures, flags, out,
    buf1, buf2, ox, oy, oz, vol, flg, pk, rec_low, rec_high, fix, slope_pk, press_pk,
    acc1, acc2, first, scale, keep, gain, press, inner, edge, outer,
    near_send, part, face_x, scale_side, keep_side, gain_side, tally,
    send_sem, recv_sem, ready,
):
    _, X, Y, Z = state.shape
    F4 = 4 * X
    me = [lax.axis_index(a) for a in ("gx", "gy", "gz")]
    size = [lax.axis_size(a) for a in ("gx", "gy", "gz")]
    up = [{a: lax.rem(me[i] + 1, size[i])} for i, a in enumerate(("gx", "gy", "gz"))]
    down = [{a: lax.rem(me[i] + size[i] - 1, size[i])} for i, a in enumerate(("gx", "gy", "gz"))]

    rows = pl.ds(PAD, Y)
    def settle(sem, ref):
        pltpu.make_async_copy(ref, ref, sem).wait()

    loads = [
        (state, buf1.at[:, pl.ds(2, X), rows, :]),
        (apertures.at[0], ox.at[pl.ds(0, X)]),
        (apertures.at[1], oy.at[:, pl.ds(0, Y), :]),
        (apertures.at[2], oz),
        (volume, vol),
        (flags, flg),
    ]
    loads = [pltpu.make_async_copy(s, d, send_sem) for s, d in loads]

    barrier = pltpu.get_barrier_semaphore()
    n_z = size[2]
    bottom, top = me[2] == 0, me[2] == n_z - 1
    early_up = [me[i] < size[i] // 2 for i in range(2)] + [jnp.logical_not(top)]
    early_down = [(me[i] == 0) | (me[i] > size[i] // 2) for i in range(2)] + [bottom]
    late_up = [jnp.logical_not(e) for e in early_up]
    late_down = [jnp.logical_not(e) for e in early_down]
    late_edges = 0
    for i in range(3):
        @pl.when(early_up[i])
        def _():
            pl.semaphore_signal(barrier, inc=1, device_id=up[i], device_id_type=MESH)

        @pl.when(early_down[i])
        def _():
            pl.semaphore_signal(barrier, inc=1, device_id=down[i], device_id_type=MESH)

        late_edges = late_edges + jnp.where(late_up[i], 1, 0) + jnp.where(late_down[i], 1, 0)

    up_slot, down_slot = (1, 2, 4), (0, 2, 3)
    for load in loads:
        load.start()

    @pl.when(late_edges > 0)
    def _():
        pl.semaphore_wait(barrier, late_edges)

    for i in range(3):
        @pl.when(late_down[i])
        def _():
            pl.semaphore_signal(ready.at[up_slot[i]], inc=1, device_id=down[i], device_id_type=MESH)

        @pl.when(late_up[i])
        def _():
            pl.semaphore_signal(ready.at[down_slot[i]], inc=1, device_id=up[i], device_id_type=MESH)

    def send_late(i, low, high):
        @pl.when(late_down[i])
        def _():
            for c in low:
                c.start()

        @pl.when(late_up[i])
        def _():
            for c in high:
                c.start()

    def send_early_up(i, high, slot, when=True):
        @pl.when(early_up[i] & when)
        def _():
            if slot is not None:
                pl.semaphore_wait(ready.at[slot], 1)
            for c in high:
                c.start()

    def send_early_down(i, low, slot, when=True):
        @pl.when(early_down[i] & when)
        def _():
            if slot is not None:
                pl.semaphore_wait(ready.at[slot], 1)
            for c in low:
                c.start()

    def remote(src, dst, recv, target):
        return pltpu.make_async_remote_copy(
            src_ref=src, dst_ref=dst, send_sem=send_sem, recv_sem=recv_sem.at[recv],
            device_id=target, device_id_type=MESH,
        )

    def layer(src, cell, dst, place, recv, target):
        return remote(
            src.at[:, pl.ds(2 + cell, 1), rows, :], dst.at[:, pl.ds(place, 1), rows, :],
            recv, target,
        )

    def y_copies(src, x0, y0, buf, recv):
        mid = pl.ds(x0, X)
        return (
            remote(src.at[:, mid, pl.ds(y0, 2), :],
                   buf.at[:, pl.ds(2, X), pl.ds(PAD + Y, 2), :], recv, down[1]),
            remote(src.at[:, mid, pl.ds(y0 + Y - 2, 2), :],
                   buf.at[:, pl.ds(2, X), pl.ds(PAD - 2, 2), :], recv, up[1]),
        )

    def z_copies(stage, recv):
        return (
            remote(pk.at[stage], rec_high.at[stage], recv, down[2]),
            remote(pk.at[stage], rec_low.at[stage], recv, up[2]),
        )

    near_low = (remote(near_send.at[0], buf1.at[:, pl.ds(X + 2, 1), rows, :], 0, down[0]),)
    near_high = (remote(near_send.at[1], buf1.at[:, pl.ds(1, 1), rows, :], 1, up[0]),)
    rest_low = (
        layer(buf1, 1, buf1, X + 3, 2, down[0]),
        remote(ox.at[pl.ds(0, 1)], ox.at[pl.ds(X, 1)], 2, down[0]),
    )
    rest_high = (layer(buf1, X - 2, buf1, 0, 2, up[0]),)
    ys1 = y_copies(buf1, 2, PAD, buf1, 3)
    ay = remote(oy.at[:, pl.ds(0, 1), :], oy.at[:, pl.ds(Y, 1), :], 3, down[1])
    y_low, y_high = (ay, ys1[0]), (ys1[1],)
    settle(send_sem, tally.at[pl.ds(0, 10 * X * Y)])
    send_late(1, y_low, y_high)
    lane = lax.broadcasted_iota(jnp.int32, (Y, Z), 1)

    for side, c in ((0, 0), (1, X - 1)):
        for f in range(NF):
            value = buf1[f, c + 2, PAD:PAD + Y, :]
            if f in (1, 2):
                value = jnp.where(
                    (lane < SOLID) & bottom, pltpu.roll(vol[c], Z - f * SOLID, 1), value
                )
            near_send[side, f, 0] = value

    def volume_beside(side):
        place = X + 2 if side else 1
        first_part = pltpu.roll(buf1[1, place, PAD:PAD + Y, :], SOLID, 1)
        second_part = pltpu.roll(buf1[2, place, PAD:PAD + Y, :], 2 * SOLID, 1)
        v = jnp.where(lane < 2 * SOLID, first_part, second_part)
        v = jnp.where(lane < SOLID, 0.0, jnp.where(lane < 3 * SOLID, v, 1.0))
        return jnp.where(bottom, v, 1.0)

    send_late(0, near_low, near_high)

    quad = lax.rem(lane, 4)

    def pack(buf, stage, planes, packed):
        for f in range(NF + 1):
            for x in planes:
                base = f * F4 + 4 * x
                value = buf[f, x + 2, PAD:PAD + Y, :] if f < NF else oz[x]
                inside = (lane >= base) & (lane < base + 4)
                packed = jnp.where(inside, pltpu.roll(value, base + 2, 1), packed)
        pk[stage] = packed

    def still_below(stage):
        @pl.when(bottom)
        def _():
            own = pk[stage]
            rec_low[stage] = jnp.where(
                quad == 0, pltpu.roll(own, Z - 2, 1), pltpu.roll(own, Z - 1, 1)
            )

    pack(buf1, 0, range(X), jnp.zeros((Y, Z), jnp.float32))
    zs1 = z_copies(0, 4)

    send_late(2, (zs1[0],), ())
    still_below(0)
    send_late(0, rest_low, rest_high)
    limit = jnp.where(me[2] == 0, CUTZ, 0)

    def factors(v, solid, cut):
        weight = jnp.sum(jnp.where(lane < CUTZ, v, 0.0), axis=1, keepdims=True)
        inverse = jnp.where(solid, 0.0, -1.0 / jnp.maximum(v, VOLUME_FLOOR))
        excess = jnp.where(cut & (lane < limit), 1.0 - v, 0.0)
        return (
            (1.0 - excess) * inverse,
            excess * inverse,
            jnp.where(lane < limit, v / weight, 0.0),
        )

    for x in range(X):
        scale[x], keep[x], gain[x] = factors(vol[x], flg[x] == 2, flg[x] == 1)

    def pack_slopes():
        slopes, pressures = jnp.zeros((Y, Z), jnp.float32), jnp.zeros((Y, Z), jnp.float32)
        for x in range(X):
            for f in range(NF):
                base = f * F4 + 4 * x
                inside = (lane >= base) & (lane < base + 4)
                slopes = jnp.where(inside, pltpu.roll(inner[f, x], base + 2, 1), slopes)
            inside = (lane >= 4 * x) & (lane < 4 * x + 4)
            pressures = jnp.where(inside, pltpu.roll(press[x], 4 * x + 2, 1), pressures)
        slope_pk[...] = 0.5 * slopes
        press_pk[...] = pressures

    def boundary_z(stage):
        own, low, high = pk[stage], rec_low[stage], rec_high[stage]
        lower, upper = jnp.where(quad < 2, low, own), jnp.where(quad < 2, own, high)
        below2, below, above = (pltpu.roll(lower, k % Z, 1) for k in (2, 1, -1))
        s_low = 0.5 * minmod(below - below2, lower - below)
        s_own = jnp.where(quad == 3, slope_pk[...], 0.5 * minmod(lower - below, above - lower))
        under, over, over2 = (pltpu.roll(upper, k % Z, 1) for k in (1, -1, -2))
        s_up = 0.5 * minmod(over - upper, over2 - over)
        s_top = jnp.where(quad == 0, slope_pk[...], 0.5 * minmod(upper - under, over - upper))
        left = jnp.where(quad < 2, upper + s_top, below + s_low)
        right = jnp.where(quad < 2, over - s_up, lower - s_own)
        opening = jnp.where(
            quad < 2, pltpu.roll(jnp.where(quad == 2, high, own), Z - 1, 1), own
        )
        ls = [pltpu.roll(left, Z - f * F4, 1) if f else left for f in range(NF)]
        rs = [pltpu.roll(right, Z - f * F4, 1) if f else right for f in range(NF)]
        opening = pltpu.roll(opening, Z - NF * F4, 1)
        live = lane < F4
        ls = [jnp.where(live, w, 1.0) for w in ls]
        rs = [jnp.where(live, w, 1.0) for w in rs]
        g = face(ls, rs, 3, 0.5 * opening)
        for f in range(NF):
            before, after = pltpu.roll(g[f], 1, 1), pltpu.roll(g[f], Z - 1, 1)
            change = jnp.where(
                quad == 0, g[f],
                jnp.where(quad == 1, g[f] - before, jnp.where(quad == 2, after - g[f], -g[f])),
            )
            if f == 3:
                change = change - jnp.where(quad == 1, press_pk[...] * opening, 0.0)
            fix[f] = change

    def local_part(x, buf, acc):
        v = [buf[f, x + 2, PAD:PAD + Y, :] for f in range(NF)]
        press[x] = pressure_of(v, 1.0 / v[0])
        for f in range(NF):
            d = v[f] - pltpu.roll(v[f], 1, 1)
            inner[f, x] = minmod(d, pltpu.roll(d, Z - 1, 1))

    def z_part(x, buf, acc):
        v = [buf[f, x + 2, PAD:PAD + Y, :] for f in range(NF)]
        p = press[x]
        a = oz[x]
        sl = [0.5 * inner[f, x] for f in range(NF)]
        left = [pltpu.roll(v[f] + sl[f], 1, 1) for f in range(NF)]
        right = [v[f] - sl[f] for f in range(NF)]
        g = face(left, right, 3, jnp.where((lane >= 2) & (lane < Z - 1), 0.5 * a, 0.0))
        div = [acc[f, x] + (pltpu.roll(g[f], Z - 1, 1) - g[f]) for f in range(NF)]
        div[3] = div[3] - p * (jnp.where(lane == Z - 1, 0.0, pltpu.roll(a, Z - 1, 1)) - a)
        for f in range(NF):
            acc[f, x] = div[f]

    def z_fix(x, buf, acc):
        ends = (lane < 2) | (lane >= Z - 2)
        for f in range(NF):
            acc[f, x] += jnp.where(ends, pltpu.roll(fix[f], Z - (4 * x + 2), 1), 0.0)

    def y_part(x, buf, acc):
        p = press[x]
        E = Y + 8
        left, right, div = [], [], []
        for f in range(NF):
            c = buf[f, x + 2, PAD - 1:PAD - 1 + E, :]
            b = buf[f, x + 2, PAD - 2:PAD - 2 + E, :]
            n = buf[f, x + 2, PAD:PAD + E, :]
            s = 0.5 * minmod(c - b, n - c)
            left.append(c + s)
            right.append(pltpu.roll(c - s, E - 1, 0))
        a = oy[x]
        g = face(left, right, 2, 0.5 * a)
        for f in range(NF):
            div.append(pltpu.roll(g[f], E - 1, 0)[:Y] - g[f][:Y])
        div[2] = div[2] - p * (oy[x, 1:Y + 1, :] - oy[x, 0:Y, :])
        for f in range(NF):
            acc[f, x] = div[f]

    def load(buf, f, x):
        return buf[f, x + 2, PAD:PAD + Y, :]

    def half_slope(buf, x):
        out = []
        for f in range(NF):
            c = load(buf, f, x)
            out.append(0.5 * minmod(c - load(buf, f, x - 1), load(buf, f, x + 1) - c))
        return out

    def x_face(buf, x, s_low, s_high):
        left = [load(buf, f, x - 1) + s_low[f] for f in range(NF)]
        right = [load(buf, f, x) - s_high[f] for f in range(NF)]
        return face(left, right, 1, 0.5 * ox[x])

    def x_inner(buf, acc):
        below = half_slope(buf, 1)
        for f in range(NF):
            edge[0, f] = below[f]
        for x in range(2, X - 1):
            s = half_slope(buf, x)
            g = x_face(buf, x, below, s)
            for f in range(NF):
                acc[f, x - 1] += g[f]
                acc[f, x] -= g[f]
            below = s
        for f in range(NF):
            edge[1, f] = below[f]
        for x in range(X):
            push = press[x] * (ox[x + 1] - ox[x]) if x < X - 1 else -press[x] * ox[x]
            acc[1, x] -= push

    def x_near(buf, acc, side):
        x = X - 1 if side else 0
        s = half_slope(buf, x)
        for f in range(NF):
            outer[side, f] = s[f]
        inner_s = [edge[side, f] for f in range(NF)]
        g = x_face(buf, x, inner_s, s) if side else x_face(buf, 1, s, inner_s)
        for f in range(NF):
            if side:
                acc[f, X - 2] += g[f]
                acc[f, X - 1] -= g[f]
            else:
                acc[f, 1] -= g[f]
                acc[f, 0] += g[f]

    def x_last(buf, side):
        s = [outer[side, f] for f in range(NF)]
        if side:
            return x_face(buf, X, s, half_slope(buf, X))
        return [-v for v in x_face(buf, 0, half_slope(buf, -1), s)]

    def spread(cells, finish):
        @pl.when(bottom)
        def _():
            with_cut(cells, finish)

        @pl.when(jnp.logical_not(bottom))
        def _():
            for k, (total, scales, _, _) in enumerate(cells):
                finish(k, [scales * t for t in total])

    def with_cut(cells, finish):
        for k, (total, scales, keeps, gains) in enumerate(cells):
            moved = [jnp.sum(keeps * t, axis=1, keepdims=True) for t in total]
            finish(k, [scales * total[f] + gains * moved[f] for f in range(NF)])

    def cell_total(acc, c, g):
        total = [acc[f, c] for f in range(NF)]
        if g is not None:
            total = [t + v for t, v in zip(total, g)]
            if c == X - 1:
                total[1] = total[1] - press[c] * ox[X]
        return total

    def loop(step, buf, acc):
        def body(x, carry):
            step(x, buf, acc)
            return carry

        lax.fori_loop(0, X, body, 0, unroll=True)

    @pl.when(early_up[1] | early_down[1])
    def _():
        pl.semaphore_wait(ready.at[2], jnp.where(early_up[1], 1, 0) + jnp.where(early_down[1], 1, 0))

    send_early_up(1, y_high, None)
    send_early_down(1, y_low, None)
    loop(local_part, buf1, acc1)
    send_early_up(0, near_high, 1)
    send_early_up(2, (zs1[1],), 4)
    settle(recv_sem.at[3], tally.at[pl.ds(0, X * (4 * NF + 1))])
    loop(y_part, buf1, acc1)
    send_early_down(0, near_low, 0)
    held = bottom & (lax.rem(me[1], 2) == 1) & late_up[0] & early_down[0]
    send_early_up(0, rest_high, None, jnp.logical_not(held))
    send_early_down(0, rest_low, None, jnp.logical_not(held))
    loop(z_part, buf1, acc1)
    pack_slopes()
    x_inner(buf1, acc1)
    send_early_down(2, (zs1[0],), 3)
    send_early_up(0, rest_high, None, held)
    send_early_down(0, rest_low, None, held)

    @pl.when(bottom)
    def _():
        settle(recv_sem.at[4], tally.at[pl.ds(0, Y)])

    @pl.when(jnp.logical_not(bottom))
    def _():
        settle(recv_sem.at[4], tally.at[pl.ds(0, 2 * Y)])

    boundary_z(0)
    loop(z_fix, buf1, acc1)

    ys2 = y_copies(buf2, 2, PAD, buf2, 7)
    zs2 = z_copies(1, 8)

    def advance(place, rates):
        for f in range(NF):
            now = buf1[f, place, PAD:PAD + Y, :]
            buf2[f, place, PAD:PAD + Y, :] = now + TIME_STEP * rates[f]

    def finish_first(c, g=None):
        def finish(_, rates):
            for f in range(NF):
                first[f, c] = rates[f]
            advance(c + 2, rates)

        spread([(cell_total(acc1, c, g), scale[c], keep[c], gain[c])], finish)

    second = (
        remote(acc1.at[:, pl.ds(0, 1)], part.at[1], 5, down[0]),
        remote(acc1.at[:, pl.ds(X - 1, 1)], part.at[0], 6, up[0]),
        layer(buf2, 1, buf2, X + 3, 5, down[0]),
        layer(buf2, X - 2, buf2, 0, 9, up[0]),
    )
    high_first = late_up[0] & early_down[0]
    later_low = high_first & bottom

    def upper_steps():
        near_low[0].wait_recv()
        x_near(buf1, acc1, 1)
        second[1].start()
        for c in range(2, X - 1):
            finish_first(c)
        second[3].start()

    def lower_steps():
        near_high[0].wait_recv()
        x_near(buf1, acc1, 0)

        @pl.when(jnp.logical_not(later_low))
        def _():
            second[0].start()

        finish_first(1)

        @pl.when(jnp.logical_not(later_low))
        def _():
            second[2].start()

    @pl.when(early_down[0])
    def _():
        upper_steps()

    lower_steps()

    @pl.when(late_down[0])
    def _():
        upper_steps()

    pack(buf2, 1, range(1, X - 1), jnp.zeros((Y, Z), jnp.float32))
    settle(recv_sem.at[2], tally.at[pl.ds(0, (2 * NF + 1) * Y)])

    @pl.when(later_low & (lax.rem(me[1], 2) == 0))
    def _():
        second[0].start()
        second[2].start()

    g = x_last(buf1, 1)
    for f in range(NF):
        face_x[1, f] = -g[f]
    finish_first(X - 1, g)
    g = x_last(buf1, 0)
    for f in range(NF):
        face_x[0, f] = -g[f]
    finish_first(0, g)
    for c in ys2:
        c.start()
    pack(buf2, 1, (0, X - 1), pk[1])

    @pl.when(jnp.logical_not(bottom))
    def _():
        zs2[0].start()

    @pl.when(jnp.logical_not(top))
    def _():
        zs2[1].start()

    still_below(1)

    @pl.when(top)
    def _():
        rec_high[1] = rec_high[0]

    loop(local_part, buf2, acc2)
    @pl.when(later_low & (lax.rem(me[1], 2) == 1))
    def _():
        second[0].start()
        second[2].start()

    settle(recv_sem.at[7], tally.at[pl.ds(0, 4 * NF * X)])
    loop(y_part, buf2, acc2)
    loop(z_part, buf2, acc2)
    pack_slopes()
    x_inner(buf2, acc2)
    w = [buf1[f, 1, PAD:PAD + Y, :] for f in range(NF)]
    face_x[0, 1] -= pressure_of(w, 1.0 / w[0]) * ox[0]
    for side in (0, 1):
        v = volume_beside(side)
        scale_side[side], keep_side[side], gain_side[side] = factors(v, v <= 0.0, (v > 0.0) & (v < 1.0))

    def z_ends():
        @pl.when(top | bottom)
        def _():
            settle(recv_sem.at[8], tally.at[pl.ds(0, Y)])

        @pl.when(jnp.logical_not(top | bottom))
        def _():
            settle(recv_sem.at[8], tally.at[pl.ds(0, 2 * Y)])

        boundary_z(1)
        loop(z_fix, buf2, acc2)

    def finish_second(cells):
        def finish(k, rates):
            for f in range(NF):
                out[f, cells[k]] = 0.5 * (first[f, cells[k]] + rates[f])

        spread(
            [([acc2[f, c] for f in range(NF)], scale[c], keep[c], gain[c]) for c in cells], finish
        )

    def x_near_side(side, sem, count):
        settle(recv_sem.at[sem], tally.at[pl.ds(0, count * NF * Y)])
        total = [part[side, f, 0] + face_x[side, f] for f in range(NF)]
        spread(
            [(total, scale_side[side], keep_side[side], gain_side[side])],
            lambda _, rates: advance(X + 2 if side else 1, rates),
        )
        x_near(buf2, acc2, side)

    def x_last_side(side):
        c = X - 1 if side else 0
        total = cell_total(acc2, c, x_last(buf2, side))
        for f in range(NF):
            acc2[f, c] = total[f]

    z_first = top | jnp.logical_not(high_first | (late_up[0] & late_down[0] & jnp.logical_not(bottom)))
    upper_cells, lower_cells = range(X - 1, X // 2 - 1, -1), range(1, X // 2)

    def lower_last():
        settle(recv_sem.at[9], tally.at[pl.ds(0, NF * Y)])
        x_last_side(0)

    lower_first = z_first & late_down[0]

    @pl.when(lower_first)
    def _():
        x_near_side(0, 6, 1)
        lower_last()

    @pl.when(z_first)
    def _():
        z_ends()

    x_near_side(1, 5, 2)
    x_last_side(1)
    lower_end = z_first & jnp.logical_not(lower_first)

    @pl.when(lower_end)
    def _():
        finish_second(upper_cells)

    @pl.when(jnp.logical_not(lower_first))
    def _():
        x_near_side(0, 6, 1)

    @pl.when(lower_end)
    def _():
        finish_second(lower_cells)

    @pl.when(jnp.logical_not(lower_first))
    def _():
        lower_last()

    @pl.when(jnp.logical_not(z_first))
    def _():
        z_ends()

    @pl.when(lower_end)
    def _():
        finish_second((0,))

    @pl.when(jnp.logical_not(lower_end))
    def _():
        finish_second(range(X))

    sent = 8 * NF * Y + 8 * NF * X + Y + X

    @pl.when(top)
    def _():
        settle(send_sem, tally.at[pl.ds(0, sent + 2 * Y)])

    @pl.when(bottom)
    def _():
        settle(send_sem, tally.at[pl.ds(0, sent + 3 * Y)])

    @pl.when(jnp.logical_not(top | bottom))
    def _():
        settle(send_sem, tally.at[pl.ds(0, sent + 4 * Y)])


def on_device(state, volume, apertures, flags):
    _, X, Y, Z = state.shape
    f32 = jnp.float32
    wide = pltpu.VMEM((NF, X + 4, Y + 2 * PAD, Z), f32)
    cells = pltpu.VMEM((X, Y, Z), f32)
    fields = pltpu.VMEM((NF, X, Y, Z), f32)
    layer = pltpu.VMEM((Y, Z), f32)
    pair = pltpu.VMEM((2, Y, Z), f32)
    sides = pltpu.VMEM((2, NF, Y, Z), f32)
    return pl.pallas_call(
        kernel,
        out_shape=pltpu.VMEM(state.shape, f32),
        in_specs=[pl.BlockSpec(memory_space=pl.ANY)] * 4,
        out_specs=pl.BlockSpec(memory_space=pltpu.VMEM),
        scratch_shapes=[
            wide, wide,
            pltpu.VMEM((X + 1, Y, Z), f32),
            pltpu.VMEM((X, Y + 8, Z), f32),
            cells, cells, pltpu.VMEM((X, Y, Z), jnp.int32),
            pair, pair, pair,
            pltpu.VMEM((NF, Y, Z), f32), layer, layer,
            fields, fields, fields, cells, cells, cells, cells, fields, sides, sides,
            pltpu.VMEM((2, NF, 1, Y, Z), f32), pltpu.VMEM((2, NF, 1, Y, Z), f32), sides, pair, pair, pair,
            pltpu.VMEM((8 * NF * (X + Y) + 16 * Y + 8 * X, Z), f32),
            pltpu.SemaphoreType.DMA,
            pltpu.SemaphoreType.DMA((10,)),
            pltpu.SemaphoreType.REGULAR((5,)),
        ],
        compiler_params=pltpu.CompilerParams(collective_id=0, has_side_effects=True),
    )(state, volume, apertures, flags)


def solution(mesh):
    in_specs = (
        P(None, "gx", "gy", "gz"),
        P("gx", "gy", "gz"),
        P(None, "gx", "gy", "gz"),
        P("gx", "gy", "gz"),
    )
    return jax.shard_map(
        on_device, mesh=mesh, in_specs=in_specs, out_specs=P(None, "gx", "gy", "gz"),
        check_vma=False,
    )
```

```python
import jax
import jax.numpy as jnp
from jax import lax
from jax.experimental import pallas as pl
from jax.experimental.pallas import tpu as pltpu
from jax.sharding import PartitionSpec as P

CUTZ = 32
SOLID = CUTZ // 4
NF = 5
GAMMA_LESS = 0.4
DISSIPATION = 4.0
TIME_STEP = 0.02
VOLUME_FLOOR = 0.5
PAD = 8

MESH = pl.DeviceIdType.MESH


def minmod(a, b):
    return jnp.maximum(jnp.minimum(a, b), 0.0) + jnp.minimum(jnp.maximum(a, b), 0.0)


def pressure_of(w, inverse):
    kinetic = w[1] * w[1] + w[2] * w[2] + w[3] * w[3]
    return GAMMA_LESS * (w[4] - 0.5 * kinetic * inverse)


def flux(w, d):
    inverse = 1.0 / w[0]
    u = w[d] * inverse
    p = pressure_of(w, inverse)
    out = [w[d], w[1] * u, w[2] * u, w[3] * u, (w[4] + p) * u]
    out[d] = out[d] + p
    return out


def face(left, right, d, half_open):
    fl, fr = flux(left, d), flux(right, d)
    return [
        ((fl[f] + fr[f]) + DISSIPATION * (left[f] - right[f])) * half_open for f in range(NF)
    ]


def kernel(
    state, volume, apertures, flags, out,
    buf1, buf2, ox, oy, oz, vol, flg, pk, rec_low, rec_high, fix, slope_pk, press_pk,
    acc1, acc2, first, scale, keep, gain, press, inner, edge, outer,
    near_send, part, face_x, scale_side, keep_side, gain_side, tally,
    send_sem, recv_sem, ready,
):
    _, X, Y, Z = state.shape
    F4 = 4 * X
    me = [lax.axis_index(a) for a in ("gx", "gy", "gz")]
    size = [lax.axis_size(a) for a in ("gx", "gy", "gz")]
    up = [{a: lax.rem(me[i] + 1, size[i])} for i, a in enumerate(("gx", "gy", "gz"))]
    down = [{a: lax.rem(me[i] + size[i] - 1, size[i])} for i, a in enumerate(("gx", "gy", "gz"))]

    rows = pl.ds(PAD, Y)
    def settle(sem, ref):
        pltpu.make_async_copy(ref, ref, sem).wait()

    loads = [
        (state, buf1.at[:, pl.ds(2, X), rows, :]),
        (apertures.at[0], ox.at[pl.ds(0, X)]),
        (apertures.at[1], oy.at[:, pl.ds(0, Y), :]),
        (apertures.at[2], oz),
        (volume, vol),
        (flags, flg),
    ]
    loads = [pltpu.make_async_copy(s, d, send_sem) for s, d in loads]

    barrier = pltpu.get_barrier_semaphore()
    n_z = size[2]
    bottom, top = me[2] == 0, me[2] == n_z - 1
    early_up = [me[i] < size[i] // 2 for i in range(2)] + [jnp.logical_not(top)]
    early_down = [(me[i] == 0) | (me[i] > size[i] // 2) for i in range(2)] + [bottom]
    late_up = [jnp.logical_not(e) for e in early_up]
    late_down = [jnp.logical_not(e) for e in early_down]
    late_edges = 0
    for i in range(3):
        @pl.when(early_up[i])
        def _():
            pl.semaphore_signal(barrier, inc=1, device_id=up[i], device_id_type=MESH)

        @pl.when(early_down[i])
        def _():
            pl.semaphore_signal(barrier, inc=1, device_id=down[i], device_id_type=MESH)

        late_edges = late_edges + jnp.where(late_up[i], 1, 0) + jnp.where(late_down[i], 1, 0)

    up_slot, down_slot = (1, 2, 4), (0, 2, 3)
    for load in loads:
        load.start()

    @pl.when(late_edges > 0)
    def _():
        pl.semaphore_wait(barrier, late_edges)

    for i in range(3):
        @pl.when(late_down[i])
        def _():
            pl.semaphore_signal(ready.at[up_slot[i]], inc=1, device_id=down[i], device_id_type=MESH)

        @pl.when(late_up[i])
        def _():
            pl.semaphore_signal(ready.at[down_slot[i]], inc=1, device_id=up[i], device_id_type=MESH)

    def send_late(i, low, high):
        @pl.when(late_down[i])
        def _():
            for c in low:
                c.start()

        @pl.when(late_up[i])
        def _():
            for c in high:
                c.start()

    def send_early_up(i, high, slot, when=True):
        @pl.when(early_up[i] & when)
        def _():
            if slot is not None:
                pl.semaphore_wait(ready.at[slot], 1)
            for c in high:
                c.start()

    def send_early_down(i, low, slot, when=True):
        @pl.when(early_down[i] & when)
        def _():
            if slot is not None:
                pl.semaphore_wait(ready.at[slot], 1)
            for c in low:
                c.start()

    def remote(src, dst, recv, target):
        return pltpu.make_async_remote_copy(
            src_ref=src, dst_ref=dst, send_sem=send_sem, recv_sem=recv_sem.at[recv],
            device_id=target, device_id_type=MESH,
        )

    def layer(src, cell, dst, place, recv, target):
        return remote(
            src.at[:, pl.ds(2 + cell, 1), rows, :], dst.at[:, pl.ds(place, 1), rows, :],
            recv, target,
        )

    def y_copies(src, x0, y0, buf, recv):
        mid = pl.ds(x0, X)
        return (
            remote(src.at[:, mid, pl.ds(y0, 2), :],
                   buf.at[:, pl.ds(2, X), pl.ds(PAD + Y, 2), :], recv, down[1]),
            remote(src.at[:, mid, pl.ds(y0 + Y - 2, 2), :],
                   buf.at[:, pl.ds(2, X), pl.ds(PAD - 2, 2), :], recv, up[1]),
        )

    def z_copies(stage, recv):
        return (
            remote(pk.at[stage], rec_high.at[stage], recv, down[2]),
            remote(pk.at[stage], rec_low.at[stage], recv, up[2]),
        )

    near_low = (remote(near_send.at[0], buf1.at[:, pl.ds(X + 2, 1), rows, :], 0, down[0]),)
    near_high = (remote(near_send.at[1], buf1.at[:, pl.ds(1, 1), rows, :], 1, up[0]),)
    rest_low = (
        layer(buf1, 1, buf1, X + 3, 2, down[0]),
        remote(ox.at[pl.ds(0, 1)], ox.at[pl.ds(X, 1)], 2, down[0]),
    )
    rest_high = (layer(buf1, X - 2, buf1, 0, 2, up[0]),)
    ys1 = y_copies(buf1, 2, PAD, buf1, 3)
    ay = remote(oy.at[:, pl.ds(0, 1), :], oy.at[:, pl.ds(Y, 1), :], 3, down[1])
    y_low, y_high = (ay, ys1[0]), (ys1[1],)
    settle(send_sem, tally.at[pl.ds(0, 10 * X * Y)])
    send_late(1, y_low, y_high)
    lane = lax.broadcasted_iota(jnp.int32, (Y, Z), 1)

    for side, c in ((0, 0), (1, X - 1)):
        for f in range(NF):
            value = buf1[f, c + 2, PAD:PAD + Y, :]
            if f in (1, 2):
                value = jnp.where(
                    (lane < SOLID) & bottom, pltpu.roll(vol[c], Z - f * SOLID, 1), value
                )
            near_send[side, f, 0] = value

    def volume_beside(side):
        place = X + 2 if side else 1
        first_part = pltpu.roll(buf1[1, place, PAD:PAD + Y, :], SOLID, 1)
        second_part = pltpu.roll(buf1[2, place, PAD:PAD + Y, :], 2 * SOLID, 1)
        v = jnp.where(lane < 2 * SOLID, first_part, second_part)
        v = jnp.where(lane < SOLID, 0.0, jnp.where(lane < 3 * SOLID, v, 1.0))
        return jnp.where(bottom, v, 1.0)

    send_late(0, near_low, near_high)

    quad = lax.rem(lane, 4)

    def pack(buf, stage, planes, packed):
        for f in range(NF + 1):
            for x in planes:
                base = f * F4 + 4 * x
                value = buf[f, x + 2, PAD:PAD + Y, :] if f < NF else oz[x]
                inside = (lane >= base) & (lane < base + 4)
                packed = jnp.where(inside, pltpu.roll(value, base + 2, 1), packed)
        pk[stage] = packed

    def still_below(stage):
        @pl.when(bottom)
        def _():
            own = pk[stage]
            rec_low[stage] = jnp.where(
                quad == 0, pltpu.roll(own, Z - 2, 1), pltpu.roll(own, Z - 1, 1)
            )

    pack(buf1, 0, range(X), jnp.zeros((Y, Z), jnp.float32))
    zs1 = z_copies(0, 4)

    send_late(2, (zs1[0],), ())
    still_below(0)
    send_late(0, rest_low, rest_high)
    limit = jnp.where(me[2] == 0, CUTZ, 0)

    def factors(v, solid, cut):
        weight = jnp.sum(jnp.where(lane < CUTZ, v, 0.0), axis=1, keepdims=True)
        inverse = jnp.where(solid, 0.0, -1.0 / jnp.maximum(v, VOLUME_FLOOR))
        excess = jnp.where(cut & (lane < limit), 1.0 - v, 0.0)
        return (
            (1.0 - excess) * inverse,
            excess * inverse,
            jnp.where(lane < limit, v / weight, 0.0),
        )

    for x in range(X):
        scale[x], keep[x], gain[x] = factors(vol[x], flg[x] == 2, flg[x] == 1)

    def pack_slopes():
        slopes, pressures = jnp.zeros((Y, Z), jnp.float32), jnp.zeros((Y, Z), jnp.float32)
        for x in range(X):
            for f in range(NF):
                base = f * F4 + 4 * x
                inside = (lane >= base) & (lane < base + 4)
                slopes = jnp.where(inside, pltpu.roll(inner[f, x], base + 2, 1), slopes)
            inside = (lane >= 4 * x) & (lane < 4 * x + 4)
            pressures = jnp.where(inside, pltpu.roll(press[x], 4 * x + 2, 1), pressures)
        slope_pk[...] = 0.5 * slopes
        press_pk[...] = pressures

    def boundary_z(stage):
        own, low, high = pk[stage], rec_low[stage], rec_high[stage]
        lower, upper = jnp.where(quad < 2, low, own), jnp.where(quad < 2, own, high)
        below2, below, above = (pltpu.roll(lower, k % Z, 1) for k in (2, 1, -1))
        s_low = 0.5 * minmod(below - below2, lower - below)
        s_own = jnp.where(quad == 3, slope_pk[...], 0.5 * minmod(lower - below, above - lower))
        under, over, over2 = (pltpu.roll(upper, k % Z, 1) for k in (1, -1, -2))
        s_up = 0.5 * minmod(over - upper, over2 - over)
        s_top = jnp.where(quad == 0, slope_pk[...], 0.5 * minmod(upper - under, over - upper))
        left = jnp.where(quad < 2, upper + s_top, below + s_low)
        right = jnp.where(quad < 2, over - s_up, lower - s_own)
        opening = jnp.where(
            quad < 2, pltpu.roll(jnp.where(quad == 2, high, own), Z - 1, 1), own
        )
        ls = [pltpu.roll(left, Z - f * F4, 1) if f else left for f in range(NF)]
        rs = [pltpu.roll(right, Z - f * F4, 1) if f else right for f in range(NF)]
        opening = pltpu.roll(opening, Z - NF * F4, 1)
        live = lane < F4
        ls = [jnp.where(live, w, 1.0) for w in ls]
        rs = [jnp.where(live, w, 1.0) for w in rs]
        g = face(ls, rs, 3, 0.5 * opening)
        for f in range(NF):
            before, after = pltpu.roll(g[f], 1, 1), pltpu.roll(g[f], Z - 1, 1)
            change = jnp.where(
                quad == 0, g[f],
                jnp.where(quad == 1, g[f] - before, jnp.where(quad == 2, after - g[f], -g[f])),
            )
            if f == 3:
                change = change - jnp.where(quad == 1, press_pk[...] * opening, 0.0)
            fix[f] = change

    def local_part(x, buf, acc):
        v = [buf[f, x + 2, PAD:PAD + Y, :] for f in range(NF)]
        press[x] = pressure_of(v, 1.0 / v[0])
        for f in range(NF):
            d = v[f] - pltpu.roll(v[f], 1, 1)
            inner[f, x] = minmod(d, pltpu.roll(d, Z - 1, 1))

    def z_part(x, buf, acc):
        v = [buf[f, x + 2, PAD:PAD + Y, :] for f in range(NF)]
        p = press[x]
        a = oz[x]
        sl = [0.5 * inner[f, x] for f in range(NF)]
        left = [pltpu.roll(v[f] + sl[f], 1, 1) for f in range(NF)]
        right = [v[f] - sl[f] for f in range(NF)]
        g = face(left, right, 3, jnp.where((lane >= 2) & (lane < Z - 1), 0.5 * a, 0.0))
        div = [acc[f, x] + (pltpu.roll(g[f], Z - 1, 1) - g[f]) for f in range(NF)]
        div[3] = div[3] - p * (jnp.where(lane == Z - 1, 0.0, pltpu.roll(a, Z - 1, 1)) - a)
        for f in range(NF):
            acc[f, x] = div[f]

    def z_fix(x, buf, acc):
        ends = (lane < 2) | (lane >= Z - 2)
        for f in range(NF):
            acc[f, x] += jnp.where(ends, pltpu.roll(fix[f], Z - (4 * x + 2), 1), 0.0)

    def y_part(x, buf, acc):
        p = press[x]
        E = Y + 8
        left, right, div = [], [], []
        for f in range(NF):
            c = buf[f, x + 2, PAD - 1:PAD - 1 + E, :]
            b = buf[f, x + 2, PAD - 2:PAD - 2 + E, :]
            n = buf[f, x + 2, PAD:PAD + E, :]
            s = 0.5 * minmod(c - b, n - c)
            left.append(c + s)
            right.append(pltpu.roll(c - s, E - 1, 0))
        a = oy[x]
        g = face(left, right, 2, 0.5 * a)
        for f in range(NF):
            div.append(pltpu.roll(g[f], E - 1, 0)[:Y] - g[f][:Y])
        div[2] = div[2] - p * (oy[x, 1:Y + 1, :] - oy[x, 0:Y, :])
        for f in range(NF):
            acc[f, x] = div[f]

    def load(buf, f, x):
        return buf[f, x + 2, PAD:PAD + Y, :]

    def half_slope(buf, x):
        out = []
        for f in range(NF):
            c = load(buf, f, x)
            out.append(0.5 * minmod(c - load(buf, f, x - 1), load(buf, f, x + 1) - c))
        return out

    def x_face(buf, x, s_low, s_high):
        left = [load(buf, f, x - 1) + s_low[f] for f in range(NF)]
        right = [load(buf, f, x) - s_high[f] for f in range(NF)]
        return face(left, right, 1, 0.5 * ox[x])

    def x_inner(buf, acc):
        below = half_slope(buf, 1)
        for f in range(NF):
            edge[0, f] = below[f]
        for x in range(2, X - 1):
            s = half_slope(buf, x)
            g = x_face(buf, x, below, s)
            for f in range(NF):
                acc[f, x - 1] += g[f]
                acc[f, x] -= g[f]
            below = s
        for f in range(NF):
            edge[1, f] = below[f]
        for x in range(X):
            push = press[x] * (ox[x + 1] - ox[x]) if x < X - 1 else -press[x] * ox[x]
            acc[1, x] -= push

    def x_near(buf, acc, side):
        x = X - 1 if side else 0
        s = half_slope(buf, x)
        for f in range(NF):
            outer[side, f] = s[f]
        inner_s = [edge[side, f] for f in range(NF)]
        g = x_face(buf, x, inner_s, s) if side else x_face(buf, 1, s, inner_s)
        for f in range(NF):
            if side:
                acc[f, X - 2] += g[f]
                acc[f, X - 1] -= g[f]
            else:
                acc[f, 1] -= g[f]
                acc[f, 0] += g[f]

    def x_last(buf, side):
        s = [outer[side, f] for f in range(NF)]
        if side:
            return x_face(buf, X, s, half_slope(buf, X))
        return [-v for v in x_face(buf, 0, half_slope(buf, -1), s)]

    def spread(cells, finish):
        @pl.when(bottom)
        def _():
            with_cut(cells, finish)

        @pl.when(jnp.logical_not(bottom))
        def _():
            for k, (total, scales, _, _) in enumerate(cells):
                finish(k, [scales * t for t in total])

    def with_cut(cells, finish):
        for k, (total, scales, keeps, gains) in enumerate(cells):
            moved = [jnp.sum(keeps * t, axis=1, keepdims=True) for t in total]
            finish(k, [scales * total[f] + gains * moved[f] for f in range(NF)])

    def cell_total(acc, c, g):
        total = [acc[f, c] for f in range(NF)]
        if g is not None:
            total = [t + v for t, v in zip(total, g)]
            if c == X - 1:
                total[1] = total[1] - press[c] * ox[X]
        return total

    def loop(step, buf, acc):
        def body(x, carry):
            step(x, buf, acc)
            return carry

        lax.fori_loop(0, X, body, 0, unroll=True)

    @pl.when(early_up[1] | early_down[1])
    def _():
        pl.semaphore_wait(ready.at[2], jnp.where(early_up[1], 1, 0) + jnp.where(early_down[1], 1, 0))

    send_early_up(1, y_high, None)
    send_early_down(1, y_low, None)
    loop(local_part, buf1, acc1)
    send_early_up(0, near_high, 1)
    send_early_up(2, (zs1[1],), 4)
    settle(recv_sem.at[3], tally.at[pl.ds(0, X * (4 * NF + 1))])
    loop(y_part, buf1, acc1)
    send_early_down(0, near_low, 0)
    held = bottom & (lax.rem(me[1], 2) == 1) & late_up[0] & early_down[0]
    send_early_up(0, rest_high, None, jnp.logical_not(held))
    send_early_down(0, rest_low, None, jnp.logical_not(held))
    loop(z_part, buf1, acc1)
    pack_slopes()
    x_inner(buf1, acc1)
    send_early_down(2, (zs1[0],), 3)
    send_early_up(0, rest_high, None, held)
    send_early_down(0, rest_low, None, held)

    @pl.when(bottom)
    def _():
        settle(recv_sem.at[4], tally.at[pl.ds(0, Y)])

    @pl.when(jnp.logical_not(bottom))
    def _():
        settle(recv_sem.at[4], tally.at[pl.ds(0, 2 * Y)])

    boundary_z(0)
    loop(z_fix, buf1, acc1)

    ys2 = y_copies(buf2, 2, PAD, buf2, 7)
    zs2 = z_copies(1, 8)

    def advance(place, rates):
        for f in range(NF):
            now = buf1[f, place, PAD:PAD + Y, :]
            buf2[f, place, PAD:PAD + Y, :] = now + TIME_STEP * rates[f]

    def finish_first(cells, outer_faces=None):
        def finish(k, rates):
            c = cells[k]
            for f in range(NF):
                first[f, c] = rates[f]
            advance(c + 2, rates)

        spread(
            [
                (cell_total(acc1, c, outer_faces and outer_faces[k]), scale[c], keep[c], gain[c])
                for k, c in enumerate(cells)
            ],
            finish,
        )

    second = (
        remote(acc1.at[:, pl.ds(0, 1)], part.at[1], 5, down[0]),
        remote(acc1.at[:, pl.ds(X - 1, 1)], part.at[0], 6, up[0]),
        layer(buf2, 1, buf2, X + 3, 5, down[0]),
        layer(buf2, X - 2, buf2, 0, 9, up[0]),
    )
    high_first = late_up[0] & early_down[0]
    later_low = high_first & bottom

    def upper_steps():
        near_low[0].wait_recv()
        x_near(buf1, acc1, 1)
        second[1].start()
        for c in range(2, X - 1):
            finish_first((c,))
        second[3].start()

    def lower_steps():
        near_high[0].wait_recv()
        x_near(buf1, acc1, 0)

        @pl.when(jnp.logical_not(later_low))
        def _():
            second[0].start()

        finish_first((1,))

        @pl.when(jnp.logical_not(later_low))
        def _():
            second[2].start()

    @pl.when(early_down[0])
    def _():
        upper_steps()

    lower_steps()

    @pl.when(late_down[0])
    def _():
        upper_steps()

    pack(buf2, 1, range(1, X - 1), jnp.zeros((Y, Z), jnp.float32))
    settle(recv_sem.at[2], tally.at[pl.ds(0, (2 * NF + 1) * Y)])

    @pl.when(later_low & (lax.rem(me[1], 2) == 0))
    def _():
        second[0].start()
        second[2].start()

    g_high, g_low = x_last(buf1, 1), x_last(buf1, 0)
    for f in range(NF):
        face_x[1, f] = -g_high[f]
        face_x[0, f] = -g_low[f]
    finish_first((X - 1, 0), (g_high, g_low))
    for c in ys2:
        c.start()
    pack(buf2, 1, (0, X - 1), pk[1])

    @pl.when(jnp.logical_not(bottom))
    def _():
        zs2[0].start()

    @pl.when(jnp.logical_not(top))
    def _():
        zs2[1].start()

    still_below(1)

    @pl.when(top)
    def _():
        rec_high[1] = rec_high[0]

    loop(local_part, buf2, acc2)
    @pl.when(later_low & (lax.rem(me[1], 2) == 1))
    def _():
        second[0].start()
        second[2].start()

    settle(recv_sem.at[7], tally.at[pl.ds(0, 4 * NF * X)])
    loop(y_part, buf2, acc2)
    loop(z_part, buf2, acc2)
    pack_slopes()
    x_inner(buf2, acc2)
    w = [buf1[f, 1, PAD:PAD + Y, :] for f in range(NF)]
    face_x[0, 1] -= pressure_of(w, 1.0 / w[0]) * ox[0]
    for side in (0, 1):
        v = volume_beside(side)
        scale_side[side], keep_side[side], gain_side[side] = factors(v, v <= 0.0, (v > 0.0) & (v < 1.0))

    def z_ends():
        @pl.when(top | bottom)
        def _():
            settle(recv_sem.at[8], tally.at[pl.ds(0, Y)])

        @pl.when(jnp.logical_not(top | bottom))
        def _():
            settle(recv_sem.at[8], tally.at[pl.ds(0, 2 * Y)])

        boundary_z(1)
        loop(z_fix, buf2, acc2)

    def finish_second(cells):
        def finish(k, rates):
            for f in range(NF):
                out[f, cells[k]] = 0.5 * (first[f, cells[k]] + rates[f])

        spread(
            [([acc2[f, c] for f in range(NF)], scale[c], keep[c], gain[c]) for c in cells], finish
        )

    def x_near_side(side, sem, count):
        settle(recv_sem.at[sem], tally.at[pl.ds(0, count * NF * Y)])
        total = [part[side, f, 0] + face_x[side, f] for f in range(NF)]
        spread(
            [(total, scale_side[side], keep_side[side], gain_side[side])],
            lambda _, rates: advance(X + 2 if side else 1, rates),
        )
        x_near(buf2, acc2, side)

    def x_last_side(side):
        c = X - 1 if side else 0
        total = cell_total(acc2, c, x_last(buf2, side))
        for f in range(NF):
            acc2[f, c] = total[f]

    z_first = top | jnp.logical_not(high_first | (late_up[0] & late_down[0] & jnp.logical_not(bottom)))
    upper_cells, lower_cells = range(X - 1, X // 2 - 1, -1), range(1, X // 2)

    def lower_last():
        settle(recv_sem.at[9], tally.at[pl.ds(0, NF * Y)])
        x_last_side(0)

    lower_first = z_first & late_down[0]

    @pl.when(lower_first)
    def _():
        x_near_side(0, 6, 1)
        lower_last()

    @pl.when(z_first)
    def _():
        z_ends()

    x_near_side(1, 5, 2)
    x_last_side(1)
    lower_end = z_first & jnp.logical_not(lower_first)

    @pl.when(lower_end)
    def _():
        finish_second(upper_cells)

    @pl.when(jnp.logical_not(lower_first))
    def _():
        x_near_side(0, 6, 1)

    @pl.when(lower_end)
    def _():
        finish_second(lower_cells)

    @pl.when(jnp.logical_not(lower_first))
    def _():
        lower_last()

    @pl.when(jnp.logical_not(z_first))
    def _():
        z_ends()

    @pl.when(lower_end)
    def _():
        finish_second((0,))

    @pl.when(jnp.logical_not(lower_end))
    def _():
        finish_second(range(X))

    sent = 8 * NF * Y + 8 * NF * X + Y + X

    @pl.when(top)
    def _():
        settle(send_sem, tally.at[pl.ds(0, sent + 2 * Y)])

    @pl.when(bottom)
    def _():
        settle(send_sem, tally.at[pl.ds(0, sent + 3 * Y)])

    @pl.when(jnp.logical_not(top | bottom))
    def _():
        settle(send_sem, tally.at[pl.ds(0, sent + 4 * Y)])


def on_device(state, volume, apertures, flags):
    _, X, Y, Z = state.shape
    f32 = jnp.float32
    wide = pltpu.VMEM((NF, X + 4, Y + 2 * PAD, Z), f32)
    cells = pltpu.VMEM((X, Y, Z), f32)
    fields = pltpu.VMEM((NF, X, Y, Z), f32)
    layer = pltpu.VMEM((Y, Z), f32)
    pair = pltpu.VMEM((2, Y, Z), f32)
    sides = pltpu.VMEM((2, NF, Y, Z), f32)
    return pl.pallas_call(
        kernel,
        out_shape=pltpu.VMEM(state.shape, f32),
        in_specs=[pl.BlockSpec(memory_space=pl.ANY)] * 4,
        out_specs=pl.BlockSpec(memory_space=pltpu.VMEM),
        scratch_shapes=[
            wide, wide,
            pltpu.VMEM((X + 1, Y, Z), f32),
            pltpu.VMEM((X, Y + 8, Z), f32),
            cells, cells, pltpu.VMEM((X, Y, Z), jnp.int32),
            pair, pair, pair,
            pltpu.VMEM((NF, Y, Z), f32), layer, layer,
            fields, fields, fields, cells, cells, cells, cells, fields, sides, sides,
            pltpu.VMEM((2, NF, 1, Y, Z), f32), pltpu.VMEM((2, NF, 1, Y, Z), f32), sides, pair, pair, pair,
            pltpu.VMEM((8 * NF * (X + Y) + 16 * Y + 8 * X, Z), f32),
            pltpu.SemaphoreType.DMA,
            pltpu.SemaphoreType.DMA((10,)),
            pltpu.SemaphoreType.REGULAR((5,)),
        ],
        compiler_params=pltpu.CompilerParams(collective_id=0, has_side_effects=True),
    )(state, volume, apertures, flags)


def solution(mesh):
    in_specs = (
        P(None, "gx", "gy", "gz"),
        P("gx", "gy", "gz"),
        P(None, "gx", "gy", "gz"),
        P("gx", "gy", "gz"),
    )
    return jax.shard_map(
        on_device, mesh=mesh, in_specs=in_specs, out_specs=P(None, "gx", "gy", "gz"),
        check_vma=False,
    )
```

```python
import jax
import jax.numpy as jnp
from jax import lax
from jax.experimental import pallas as pl
from jax.experimental.pallas import tpu as pltpu
from jax.sharding import PartitionSpec as P

CUTZ = 32
SOLID = CUTZ // 4
NF = 5
GAMMA_LESS = 0.4
DISSIPATION = 4.0
TIME_STEP = 0.02
VOLUME_FLOOR = 0.5
PAD = 8

MESH = pl.DeviceIdType.MESH


def minmod(a, b):
    return jnp.maximum(jnp.minimum(a, b), 0.0) + jnp.minimum(jnp.maximum(a, b), 0.0)


def pressure_of(w, inverse):
    kinetic = w[1] * w[1] + w[2] * w[2] + w[3] * w[3]
    return GAMMA_LESS * (w[4] - 0.5 * kinetic * inverse)


def flux(w, d):
    inverse = 1.0 / w[0]
    u = w[d] * inverse
    p = pressure_of(w, inverse)
    out = [w[d], w[1] * u, w[2] * u, w[3] * u, (w[4] + p) * u]
    out[d] = out[d] + p
    return out


def face(left, right, d, half_open):
    fl, fr = flux(left, d), flux(right, d)
    return [
        ((fl[f] + fr[f]) + DISSIPATION * (left[f] - right[f])) * half_open for f in range(NF)
    ]


def kernel(
    state, volume, apertures, flags, out,
    buf1, buf2, ox, oy, oz, vol, flg, pk, rec_low, rec_high, fix, slope_pk, press_pk,
    acc1, acc2, first, scale, keep, gain, press, inner, edge, outer,
    near_send, part, face_x, scale_side, keep_side, gain_side, tally,
    send_sem, recv_sem, ready,
):
    _, X, Y, Z = state.shape
    F4 = 4 * X
    me = [lax.axis_index(a) for a in ("gx", "gy", "gz")]
    size = [lax.axis_size(a) for a in ("gx", "gy", "gz")]
    up = [{a: lax.rem(me[i] + 1, size[i])} for i, a in enumerate(("gx", "gy", "gz"))]
    down = [{a: lax.rem(me[i] + size[i] - 1, size[i])} for i, a in enumerate(("gx", "gy", "gz"))]

    rows = pl.ds(PAD, Y)
    def settle(sem, ref):
        pltpu.make_async_copy(ref, ref, sem).wait()

    loads = [
        (state, buf1.at[:, pl.ds(2, X), rows, :]),
        (apertures.at[0], ox.at[pl.ds(0, X)]),
        (apertures.at[1], oy.at[:, pl.ds(0, Y), :]),
        (apertures.at[2], oz),
        (volume, vol),
    ]
    loads = [pltpu.make_async_copy(s, d, send_sem) for s, d in loads]

    barrier = pltpu.get_barrier_semaphore()
    n_z = size[2]
    bottom, top = me[2] == 0, me[2] == n_z - 1
    early_up = [me[i] < size[i] // 2 for i in range(2)] + [jnp.logical_not(top)]
    early_down = [(me[i] == 0) | (me[i] > size[i] // 2) for i in range(2)] + [bottom]
    late_up = [jnp.logical_not(e) for e in early_up]
    late_down = [jnp.logical_not(e) for e in early_down]
    late_edges = 0
    for i in range(3):
        @pl.when(early_up[i])
        def _():
            pl.semaphore_signal(barrier, inc=1, device_id=up[i], device_id_type=MESH)

        @pl.when(early_down[i])
        def _():
            pl.semaphore_signal(barrier, inc=1, device_id=down[i], device_id_type=MESH)

        late_edges = late_edges + jnp.where(late_up[i], 1, 0) + jnp.where(late_down[i], 1, 0)

    up_slot, down_slot = (1, 2, 4), (0, 2, 3)
    for load in loads:
        load.start()

    @pl.when(late_edges > 0)
    def _():
        pl.semaphore_wait(barrier, late_edges)

    for i in range(3):
        @pl.when(late_down[i])
        def _():
            pl.semaphore_signal(ready.at[up_slot[i]], inc=1, device_id=down[i], device_id_type=MESH)

        @pl.when(late_up[i])
        def _():
            pl.semaphore_signal(ready.at[down_slot[i]], inc=1, device_id=up[i], device_id_type=MESH)

    def send_late(i, low, high):
        @pl.when(late_down[i])
        def _():
            for c in low:
                c.start()

        @pl.when(late_up[i])
        def _():
            for c in high:
                c.start()

    def send_early_up(i, high, slot, when=True):
        @pl.when(early_up[i] & when)
        def _():
            if slot is not None:
                pl.semaphore_wait(ready.at[slot], 1)
            for c in high:
                c.start()

    def send_early_down(i, low, slot, when=True):
        @pl.when(early_down[i] & when)
        def _():
            if slot is not None:
                pl.semaphore_wait(ready.at[slot], 1)
            for c in low:
                c.start()

    def remote(src, dst, recv, target):
        return pltpu.make_async_remote_copy(
            src_ref=src, dst_ref=dst, send_sem=send_sem, recv_sem=recv_sem.at[recv],
            device_id=target, device_id_type=MESH,
        )

    def layer(src, cell, dst, place, recv, target):
        return remote(
            src.at[:, pl.ds(2 + cell, 1), rows, :], dst.at[:, pl.ds(place, 1), rows, :],
            recv, target,
        )

    def y_copies(src, x0, y0, buf, recv):
        mid = pl.ds(x0, X)
        return (
            remote(src.at[:, mid, pl.ds(y0, 2), :],
                   buf.at[:, pl.ds(2, X), pl.ds(PAD + Y, 2), :], recv, down[1]),
            remote(src.at[:, mid, pl.ds(y0 + Y - 2, 2), :],
                   buf.at[:, pl.ds(2, X), pl.ds(PAD - 2, 2), :], recv, up[1]),
        )

    def z_copies(stage, recv):
        return (
            remote(pk.at[stage], rec_high.at[stage], recv, down[2]),
            remote(pk.at[stage], rec_low.at[stage], recv, up[2]),
        )

    near_low = (remote(near_send.at[0], buf1.at[:, pl.ds(X + 2, 1), rows, :], 0, down[0]),)
    near_high = (remote(near_send.at[1], buf1.at[:, pl.ds(1, 1), rows, :], 1, up[0]),)
    rest_low = (
        layer(buf1, 1, buf1, X + 3, 2, down[0]),
        remote(ox.at[pl.ds(0, 1)], ox.at[pl.ds(X, 1)], 2, down[0]),
    )
    rest_high = (layer(buf1, X - 2, buf1, 0, 2, up[0]),)
    ys1 = y_copies(buf1, 2, PAD, buf1, 3)
    ay = remote(oy.at[:, pl.ds(0, 1), :], oy.at[:, pl.ds(Y, 1), :], 3, down[1])
    y_low, y_high = (ay, ys1[0]), (ys1[1],)
    settle(send_sem, tally.at[pl.ds(0, 9 * X * Y)])
    send_late(1, y_low, y_high)
    lane = lax.broadcasted_iota(jnp.int32, (Y, Z), 1)

    for side, c in ((0, 0), (1, X - 1)):
        for f in range(NF):
            value = buf1[f, c + 2, PAD:PAD + Y, :]
            if f in (1, 2):
                value = jnp.where(
                    (lane < SOLID) & bottom, pltpu.roll(vol[c], Z - f * SOLID, 1), value
                )
            near_send[side, f, 0] = value

    def volume_beside(side):
        place = X + 2 if side else 1
        first_part = pltpu.roll(buf1[1, place, PAD:PAD + Y, :], SOLID, 1)
        second_part = pltpu.roll(buf1[2, place, PAD:PAD + Y, :], 2 * SOLID, 1)
        v = jnp.where(lane < 2 * SOLID, first_part, second_part)
        v = jnp.where(lane < SOLID, 0.0, jnp.where(lane < 3 * SOLID, v, 1.0))
        return jnp.where(bottom, v, 1.0)

    send_late(0, near_low, near_high)

    quad = lax.rem(lane, 4)

    def pack(buf, stage, planes, packed):
        for f in range(NF + 1):
            for x in planes:
                base = f * F4 + 4 * x
                value = buf[f, x + 2, PAD:PAD + Y, :] if f < NF else oz[x]
                inside = (lane >= base) & (lane < base + 4)
                packed = jnp.where(inside, pltpu.roll(value, base + 2, 1), packed)
        pk[stage] = packed

    def still_below(stage):
        @pl.when(bottom)
        def _():
            own = pk[stage]
            rec_low[stage] = jnp.where(
                quad == 0, pltpu.roll(own, Z - 2, 1), pltpu.roll(own, Z - 1, 1)
            )

    pack(buf1, 0, range(X), jnp.zeros((Y, Z), jnp.float32))
    zs1 = z_copies(0, 4)

    send_late(2, (zs1[0],), ())
    still_below(0)
    send_late(0, rest_low, rest_high)
    limit = jnp.where(me[2] == 0, CUTZ, 0)

    def factors(v, solid, cut):
        weight = jnp.sum(jnp.where(lane < CUTZ, v, 0.0), axis=1, keepdims=True)
        inverse = jnp.where(solid, 0.0, -1.0 / jnp.maximum(v, VOLUME_FLOOR))
        excess = jnp.where(cut & (lane < limit), 1.0 - v, 0.0)
        return (
            (1.0 - excess) * inverse,
            excess * inverse,
            jnp.where(lane < limit, v / weight, 0.0),
        )

    for x in range(X):
        scale[x], keep[x], gain[x] = factors(
            vol[x], vol[x] <= 0.0, (vol[x] > 0.0) & (vol[x] < 1.0)
        )

    def pack_slopes():
        slopes, pressures = jnp.zeros((Y, Z), jnp.float32), jnp.zeros((Y, Z), jnp.float32)
        for x in range(X):
            for f in range(NF):
                base = f * F4 + 4 * x
                inside = (lane >= base) & (lane < base + 4)
                slopes = jnp.where(inside, pltpu.roll(inner[f, x], base + 2, 1), slopes)
            inside = (lane >= 4 * x) & (lane < 4 * x + 4)
            pressures = jnp.where(inside, pltpu.roll(press[x], 4 * x + 2, 1), pressures)
        slope_pk[...] = 0.5 * slopes
        press_pk[...] = pressures

    def boundary_z(stage):
        own, low, high = pk[stage], rec_low[stage], rec_high[stage]
        lower, upper = jnp.where(quad < 2, low, own), jnp.where(quad < 2, own, high)
        below2, below, above = (pltpu.roll(lower, k % Z, 1) for k in (2, 1, -1))
        s_low = 0.5 * minmod(below - below2, lower - below)
        s_own = jnp.where(quad == 3, slope_pk[...], 0.5 * minmod(lower - below, above - lower))
        under, over, over2 = (pltpu.roll(upper, k % Z, 1) for k in (1, -1, -2))
        s_up = 0.5 * minmod(over - upper, over2 - over)
        s_top = jnp.where(quad == 0, slope_pk[...], 0.5 * minmod(upper - under, over - upper))
        left = jnp.where(quad < 2, upper + s_top, below + s_low)
        right = jnp.where(quad < 2, over - s_up, lower - s_own)
        opening = jnp.where(
            quad < 2, pltpu.roll(jnp.where(quad == 2, high, own), Z - 1, 1), own
        )
        ls = [pltpu.roll(left, Z - f * F4, 1) if f else left for f in range(NF)]
        rs = [pltpu.roll(right, Z - f * F4, 1) if f else right for f in range(NF)]
        opening = pltpu.roll(opening, Z - NF * F4, 1)
        live = lane < F4
        ls = [jnp.where(live, w, 1.0) for w in ls]
        rs = [jnp.where(live, w, 1.0) for w in rs]
        g = face(ls, rs, 3, 0.5 * opening)
        for f in range(NF):
            before, after = pltpu.roll(g[f], 1, 1), pltpu.roll(g[f], Z - 1, 1)
            change = jnp.where(
                quad == 0, g[f],
                jnp.where(quad == 1, g[f] - before, jnp.where(quad == 2, after - g[f], -g[f])),
            )
            if f == 3:
                change = change - jnp.where(quad == 1, press_pk[...] * opening, 0.0)
            fix[f] = change

    def local_part(x, buf, acc):
        v = [buf[f, x + 2, PAD:PAD + Y, :] for f in range(NF)]
        press[x] = pressure_of(v, 1.0 / v[0])
        for f in range(NF):
            d = v[f] - pltpu.roll(v[f], 1, 1)
            inner[f, x] = minmod(d, pltpu.roll(d, Z - 1, 1))

    def z_part(x, buf, acc):
        v = [buf[f, x + 2, PAD:PAD + Y, :] for f in range(NF)]
        p = press[x]
        a = oz[x]
        sl = [0.5 * inner[f, x] for f in range(NF)]
        left = [pltpu.roll(v[f] + sl[f], 1, 1) for f in range(NF)]
        right = [v[f] - sl[f] for f in range(NF)]
        g = face(left, right, 3, jnp.where((lane >= 2) & (lane < Z - 1), 0.5 * a, 0.0))
        div = [acc[f, x] + (pltpu.roll(g[f], Z - 1, 1) - g[f]) for f in range(NF)]
        div[3] = div[3] - p * (jnp.where(lane == Z - 1, 0.0, pltpu.roll(a, Z - 1, 1)) - a)
        for f in range(NF):
            acc[f, x] = div[f]

    def z_fix(x, buf, acc):
        ends = (lane < 2) | (lane >= Z - 2)
        for f in range(NF):
            acc[f, x] += jnp.where(ends, pltpu.roll(fix[f], Z - (4 * x + 2), 1), 0.0)

    def y_part(x, buf, acc):
        p = press[x]
        E = Y + 8
        left, right, div = [], [], []
        for f in range(NF):
            c = buf[f, x + 2, PAD - 1:PAD - 1 + E, :]
            b = buf[f, x + 2, PAD - 2:PAD - 2 + E, :]
            n = buf[f, x + 2, PAD:PAD + E, :]
            s = 0.5 * minmod(c - b, n - c)
            left.append(c + s)
            right.append(pltpu.roll(c - s, E - 1, 0))
        a = oy[x]
        g = face(left, right, 2, 0.5 * a)
        for f in range(NF):
            div.append(pltpu.roll(g[f], E - 1, 0)[:Y] - g[f][:Y])
        div[2] = div[2] - p * (oy[x, 1:Y + 1, :] - oy[x, 0:Y, :])
        for f in range(NF):
            acc[f, x] = div[f]

    def load(buf, f, x):
        return buf[f, x + 2, PAD:PAD + Y, :]

    def half_slope(buf, x):
        out = []
        for f in range(NF):
            c = load(buf, f, x)
            out.append(0.5 * minmod(c - load(buf, f, x - 1), load(buf, f, x + 1) - c))
        return out

    def x_face(buf, x, s_low, s_high):
        left = [load(buf, f, x - 1) + s_low[f] for f in range(NF)]
        right = [load(buf, f, x) - s_high[f] for f in range(NF)]
        return face(left, right, 1, 0.5 * ox[x])

    def x_inner(buf, acc):
        below = half_slope(buf, 1)
        for f in range(NF):
            edge[0, f] = below[f]
        for x in range(2, X - 1):
            s = half_slope(buf, x)
            g = x_face(buf, x, below, s)
            for f in range(NF):
                acc[f, x - 1] += g[f]
                acc[f, x] -= g[f]
            below = s
        for f in range(NF):
            edge[1, f] = below[f]
        for x in range(X):
            push = press[x] * (ox[x + 1] - ox[x]) if x < X - 1 else -press[x] * ox[x]
            acc[1, x] -= push

    def x_near(buf, acc, side):
        x = X - 1 if side else 0
        s = half_slope(buf, x)
        for f in range(NF):
            outer[side, f] = s[f]
        inner_s = [edge[side, f] for f in range(NF)]
        g = x_face(buf, x, inner_s, s) if side else x_face(buf, 1, s, inner_s)
        for f in range(NF):
            if side:
                acc[f, X - 2] += g[f]
                acc[f, X - 1] -= g[f]
            else:
                acc[f, 1] -= g[f]
                acc[f, 0] += g[f]

    def x_last(buf, side):
        s = [outer[side, f] for f in range(NF)]
        if side:
            return x_face(buf, X, s, half_slope(buf, X))
        return [-v for v in x_face(buf, 0, half_slope(buf, -1), s)]

    def spread(cells, finish):
        @pl.when(bottom)
        def _():
            with_cut(cells, finish)

        @pl.when(jnp.logical_not(bottom))
        def _():
            for k, (total, scales, _, _) in enumerate(cells):
                finish(k, [scales * t for t in total])

    def with_cut(cells, finish):
        for k, (total, scales, keeps, gains) in enumerate(cells):
            moved = [jnp.sum(keeps * t, axis=1, keepdims=True) for t in total]
            finish(k, [scales * total[f] + gains * moved[f] for f in range(NF)])

    def cell_total(acc, c, g):
        total = [acc[f, c] for f in range(NF)]
        if g is not None:
            total = [t + v for t, v in zip(total, g)]
            if c == X - 1:
                total[1] = total[1] - press[c] * ox[X]
        return total

    def loop(step, buf, acc):
        def body(x, carry):
            step(x, buf, acc)
            return carry

        lax.fori_loop(0, X, body, 0, unroll=True)

    @pl.when(early_up[1] | early_down[1])
    def _():
        pl.semaphore_wait(ready.at[2], jnp.where(early_up[1], 1, 0) + jnp.where(early_down[1], 1, 0))

    send_early_up(1, y_high, None)
    send_early_down(1, y_low, None)
    loop(local_part, buf1, acc1)
    send_early_up(0, near_high, 1)
    send_early_up(2, (zs1[1],), 4)
    settle(recv_sem.at[3], tally.at[pl.ds(0, X * (4 * NF + 1))])
    loop(y_part, buf1, acc1)
    send_early_down(0, near_low, 0)
    held = bottom & (lax.rem(me[1], 2) == 1) & late_up[0] & early_down[0]
    send_early_up(0, rest_high, None, jnp.logical_not(held))
    send_early_down(0, rest_low, None, jnp.logical_not(held))
    loop(z_part, buf1, acc1)
    pack_slopes()
    x_inner(buf1, acc1)
    send_early_down(2, (zs1[0],), 3)
    send_early_up(0, rest_high, None, held)
    send_early_down(0, rest_low, None, held)

    @pl.when(bottom)
    def _():
        settle(recv_sem.at[4], tally.at[pl.ds(0, Y)])

    @pl.when(jnp.logical_not(bottom))
    def _():
        settle(recv_sem.at[4], tally.at[pl.ds(0, 2 * Y)])

    boundary_z(0)
    loop(z_fix, buf1, acc1)

    ys2 = y_copies(buf2, 2, PAD, buf2, 7)
    zs2 = z_copies(1, 8)

    def advance(place, rates):
        for f in range(NF):
            now = buf1[f, place, PAD:PAD + Y, :]
            buf2[f, place, PAD:PAD + Y, :] = now + TIME_STEP * rates[f]

    def finish_first(cells, outer_faces=None):
        def finish(k, rates):
            c = cells[k]
            for f in range(NF):
                first[f, c] = rates[f]
            advance(c + 2, rates)

        spread(
            [
                (cell_total(acc1, c, outer_faces and outer_faces[k]), scale[c], keep[c], gain[c])
                for k, c in enumerate(cells)
            ],
            finish,
        )

    second = (
        remote(acc1.at[:, pl.ds(0, 1)], part.at[1], 5, down[0]),
        remote(acc1.at[:, pl.ds(X - 1, 1)], part.at[0], 6, up[0]),
        layer(buf2, 1, buf2, X + 3, 5, down[0]),
        layer(buf2, X - 2, buf2, 0, 9, up[0]),
    )
    high_first = late_up[0] & early_down[0]
    later_low = high_first & bottom

    def upper_steps():
        near_low[0].wait_recv()
        x_near(buf1, acc1, 1)
        second[1].start()
        for c in range(2, X - 1):
            finish_first((c,))
        second[3].start()

    def lower_steps():
        near_high[0].wait_recv()
        x_near(buf1, acc1, 0)

        @pl.when(jnp.logical_not(later_low))
        def _():
            second[0].start()

        finish_first((1,))

        @pl.when(jnp.logical_not(later_low))
        def _():
            second[2].start()

    @pl.when(early_down[0])
    def _():
        upper_steps()

    lower_steps()

    @pl.when(late_down[0])
    def _():
        upper_steps()

    pack(buf2, 1, range(1, X - 1), jnp.zeros((Y, Z), jnp.float32))
    settle(recv_sem.at[2], tally.at[pl.ds(0, (2 * NF + 1) * Y)])

    @pl.when(later_low & (lax.rem(me[1], 2) == 0))
    def _():
        second[0].start()
        second[2].start()

    g_high, g_low = x_last(buf1, 1), x_last(buf1, 0)
    for f in range(NF):
        face_x[1, f] = -g_high[f]
        face_x[0, f] = -g_low[f]
    finish_first((X - 1, 0), (g_high, g_low))
    for c in ys2:
        c.start()
    pack(buf2, 1, (0, X - 1), pk[1])

    @pl.when(jnp.logical_not(bottom))
    def _():
        zs2[0].start()

    @pl.when(jnp.logical_not(top))
    def _():
        zs2[1].start()

    still_below(1)

    @pl.when(top)
    def _():
        rec_high[1] = rec_high[0]

    loop(local_part, buf2, acc2)
    @pl.when(later_low & (lax.rem(me[1], 2) == 1))
    def _():
        second[0].start()
        second[2].start()

    settle(recv_sem.at[7], tally.at[pl.ds(0, 4 * NF * X)])
    loop(y_part, buf2, acc2)
    loop(z_part, buf2, acc2)
    pack_slopes()
    x_inner(buf2, acc2)
    w = [buf1[f, 1, PAD:PAD + Y, :] for f in range(NF)]
    face_x[0, 1] -= pressure_of(w, 1.0 / w[0]) * ox[0]
    for side in (0, 1):
        v = volume_beside(side)
        scale_side[side], keep_side[side], gain_side[side] = factors(v, v <= 0.0, (v > 0.0) & (v < 1.0))

    def z_ends():
        @pl.when(top | bottom)
        def _():
            settle(recv_sem.at[8], tally.at[pl.ds(0, Y)])

        @pl.when(jnp.logical_not(top | bottom))
        def _():
            settle(recv_sem.at[8], tally.at[pl.ds(0, 2 * Y)])

        boundary_z(1)
        loop(z_fix, buf2, acc2)

    def finish_second(cells):
        def finish(k, rates):
            for f in range(NF):
                out[f, cells[k]] = 0.5 * (first[f, cells[k]] + rates[f])

        spread(
            [([acc2[f, c] for f in range(NF)], scale[c], keep[c], gain[c]) for c in cells], finish
        )

    def x_near_side(side, sem, count):
        settle(recv_sem.at[sem], tally.at[pl.ds(0, count * NF * Y)])
        total = [part[side, f, 0] + face_x[side, f] for f in range(NF)]
        spread(
            [(total, scale_side[side], keep_side[side], gain_side[side])],
            lambda _, rates: advance(X + 2 if side else 1, rates),
        )
        x_near(buf2, acc2, side)

    def x_last_side(side):
        c = X - 1 if side else 0
        total = cell_total(acc2, c, x_last(buf2, side))
        for f in range(NF):
            acc2[f, c] = total[f]

    z_first = top | jnp.logical_not(high_first | (late_up[0] & late_down[0] & jnp.logical_not(bottom)))
    upper_cells, lower_cells = range(X - 1, X // 2 - 1, -1), range(1, X // 2)

    def lower_last():
        settle(recv_sem.at[9], tally.at[pl.ds(0, NF * Y)])
        x_last_side(0)

    lower_first = z_first & late_down[0]

    @pl.when(lower_first)
    def _():
        x_near_side(0, 6, 1)
        lower_last()

    @pl.when(z_first)
    def _():
        z_ends()

    x_near_side(1, 5, 2)
    x_last_side(1)
    lower_end = z_first & jnp.logical_not(lower_first)

    @pl.when(lower_end)
    def _():
        finish_second(upper_cells)

    @pl.when(jnp.logical_not(lower_first))
    def _():
        x_near_side(0, 6, 1)

    @pl.when(lower_end)
    def _():
        finish_second(lower_cells)

    @pl.when(jnp.logical_not(lower_first))
    def _():
        lower_last()

    @pl.when(jnp.logical_not(z_first))
    def _():
        z_ends()

    @pl.when(lower_end)
    def _():
        finish_second((0,))

    @pl.when(jnp.logical_not(lower_end))
    def _():
        finish_second(range(X))

    sent = 8 * NF * Y + 8 * NF * X + Y + X

    @pl.when(top)
    def _():
        settle(send_sem, tally.at[pl.ds(0, sent + 2 * Y)])

    @pl.when(bottom)
    def _():
        settle(send_sem, tally.at[pl.ds(0, sent + 3 * Y)])

    @pl.when(jnp.logical_not(top | bottom))
    def _():
        settle(send_sem, tally.at[pl.ds(0, sent + 4 * Y)])


def on_device(state, volume, apertures, flags):
    _, X, Y, Z = state.shape
    f32 = jnp.float32
    wide = pltpu.VMEM((NF, X + 4, Y + 2 * PAD, Z), f32)
    cells = pltpu.VMEM((X, Y, Z), f32)
    fields = pltpu.VMEM((NF, X, Y, Z), f32)
    layer = pltpu.VMEM((Y, Z), f32)
    pair = pltpu.VMEM((2, Y, Z), f32)
    sides = pltpu.VMEM((2, NF, Y, Z), f32)
    return pl.pallas_call(
        kernel,
        out_shape=pltpu.VMEM(state.shape, f32),
        in_specs=[pl.BlockSpec(memory_space=pl.ANY)] * 4,
        out_specs=pl.BlockSpec(memory_space=pltpu.VMEM),
        scratch_shapes=[
            wide, wide,
            pltpu.VMEM((X + 1, Y, Z), f32),
            pltpu.VMEM((X, Y + 8, Z), f32),
            cells, cells, pltpu.VMEM((X, Y, Z), jnp.int32),
            pair, pair, pair,
            pltpu.VMEM((NF, Y, Z), f32), layer, layer,
            fields, fields, fields, cells, cells, cells, cells, fields, sides, sides,
            pltpu.VMEM((2, NF, 1, Y, Z), f32), pltpu.VMEM((2, NF, 1, Y, Z), f32), sides, pair, pair, pair,
            pltpu.VMEM((8 * NF * (X + Y) + 16 * Y + 8 * X, Z), f32),
            pltpu.SemaphoreType.DMA,
            pltpu.SemaphoreType.DMA((10,)),
            pltpu.SemaphoreType.REGULAR((5,)),
        ],
        compiler_params=pltpu.CompilerParams(collective_id=0, has_side_effects=True),
    )(state, volume, apertures, flags)


def solution(mesh):
    in_specs = (
        P(None, "gx", "gy", "gz"),
        P("gx", "gy", "gz"),
        P(None, "gx", "gy", "gz"),
        P("gx", "gy", "gz"),
    )
    return jax.shard_map(
        on_device, mesh=mesh, in_specs=in_specs, out_specs=P(None, "gx", "gy", "gz"),
        check_vma=False,
    )
```
